32 devices in a mesh: dp: 4 (over y, x), expert: 4 (over z), mp: 2 (over core).
Axes of the slice: x: 2, y: 2, z: 4, core: 2. Of those that a mesh axis runs over, the one named last changes fastest.
Arguments:
- tokens: bfloat16 [8192, 768], P(('dp', 'expert', 'mp')), may hold values from -6 to 6
- cotangent: bfloat16 [8192, 768], P(('dp', 'expert', 'mp')), may hold values from -6 to 6
- routes: int32 [8192, 1], P(('dp', 'expert')), may hold values from 0 to 3; in each aligned block of 512 rows (0 to 511, 512 to 1023, ...) at most 256 rows name the same one
- buckets: int32 [512, 512], replicated, may hold values from 0 to 31
- norm_first: float32 [768], replicated, may hold values from 0.5 to 1.5
- query_first: bfloat16 [768, 768], P('expert', 'mp'), may hold values from -0.21875 to 0.21875
- key_first: bfloat16 [768, 768], P('expert', 'mp'), may hold values from -0.21875 to 0.21875
- value_first: bfloat16 [768, 768], P('expert', 'mp'), may hold values from -0.21875 to 0.21875
- output_first: bfloat16 [768, 768], P('mp', 'expert'), may hold values from -1.75 to 1.75
- table_first: float32 [32, 12], replicated, may hold values from -4 to 4
- dense_gain: float32 [768], replicated, may hold values from 0.5 to 1.5
- dense_in: bfloat16 [768, 3072], P('expert', 'mp'), may hold values from -0.21875 to 0.21875
- dense_out: bfloat16 [3072, 768], P('mp', 'expert'), may hold values from -0.109375 to 0.109375
- norm_second: float32 [768], replicated, may hold values from 0.5 to 1.5
- query_second: bfloat16 [768, 768], P('expert', 'mp'), may hold values from -0.21875 to 0.21875
- key_second: bfloat16 [768, 768], P('expert', 'mp'), may hold values from -0.21875 to 0.21875
- value_second: bfloat16 [768, 768], P('expert', 'mp'), may hold values from -0.21875 to 0.21875
- output_second: bfloat16 [768, 768], P('mp', 'expert'), may hold values from -1.75 to 1.75
- table_second: float32 [32, 12], replicated, may hold values from -4 to 4
- expert_gain: float32 [768], replicated, may hold values from 0.5 to 1.5
- router: bfloat16 [768, 4], replicated, may hold values from -0.109375 to 0.109375
- expert_in: bfloat16 [4, 768, 3072], P('expert', None, 'mp'), may hold values from -0.21875 to 0.21875
- expert_out: bfloat16 [4, 3072, 768], P('expert', 'mp'), may hold values from -0.625 to 0.625
Outputs:
- block_output: float32 [8192, 768], P(('dp', 'expert', 'mp'))
- grad_tokens: float32 [8192, 768], P(('dp', 'expert', 'mp'))
- grad_norm_first: float32 [768], replicated
- grad_query_first: float32 [768, 768], P('expert', 'mp')
- grad_key_first: float32 [768, 768], P('expert', 'mp')
- grad_value_first: float32 [768, 768], P('expert', 'mp')
- grad_output_first: float32 [768, 768], P('mp', 'expert')
- grad_table_first: float32 [32, 12], replicated
- grad_dense_gain: float32 [768], replicated
- grad_dense_in: float32 [768, 3072], P('expert', 'mp')
- grad_dense_out: float32 [3072, 768], P('mp', 'expert')
- grad_norm_second: float32 [768], replicated
- grad_query_second: float32 [768, 768], P('expert', 'mp')
- grad_key_second: float32 [768, 768], P('expert', 'mp')
- grad_value_second: float32 [768, 768], P('expert', 'mp')
- grad_output_second: float32 [768, 768], P('mp', 'expert')
- grad_table_second: float32 [32, 12], replicated
- grad_expert_gain: float32 [768], replicated
- grad_router: float32 [768, 4], replicated
- grad_expert_in: float32 [4, 768, 3072], P('expert', None, 'mp')
- grad_expert_out: float32 [4, 3072, 768], P('expert', 'mp')
The draws below stay inside these ranges and needn't reach their ends.
Inputs may be any that keep to these rules, and one draw needn't show every extreme that they name: `routes`: in each aligned block of 512 rows (one sequence) no expert is named by more than 256 rows, and in every draw some block has an expert named by exactly 256 rows.
All inputs are finite; a program needn't handle non-finite values.
Results may differ from the reference program's by a relative error of at most 0.03.
Values may be sent and summed in bfloat16 or wider, within the bound.
No kernel may reach another device: no remote copies, remote signals or barrier semaphores. Data moves between devices by JAX's collectives and lax.ppermute only.
A program may use at most 192 MiB of HBM per device.

```python
import math
from functools import partial
import jax
import jax.numpy as jnp
import numpy as np
from jax import lax

D = 768
HEADS = 12
HEAD_DIM = 64
FF = 3072
BUCKETS = 32
SEQ = 512
TOKENS = 8192
EXPERTS = 4
CAP = 256


def set_ends(values, stream_key, low, high):
    dims = values.shape
    spot = [jax.random.randint(jax.random.fold_in(stream_key, axis), (), 0, dims[axis]) for axis in range(len(dims))]
    values = values.at[tuple(spot)].set(low)
    longest = dims.index(max(dims))
    spot[longest] = (spot[longest] + 1) % dims[longest]
    return values.at[tuple(spot)].set(high)


def levels(own_key, shape, pieces, low, top_value):
    def one(dim, blocks):
        heights = jax.random.uniform(jax.random.fold_in(jax.random.fold_in(own_key, 6), dim), (blocks,), jnp.float32, low / len(pieces), top_value / len(pieces))
        return jnp.repeat(jnp.exp(heights), shape[dim] // blocks).reshape((-1,) + (1,) * (len(shape) - dim - 1))

    loudness = one(*pieces[0])
    for cut in pieces[1:]:
        loudness = loudness * one(*cut)
    return loudness


def assign_block(rng, own, number, rows, number_of, top, most, skew):
    order = jax.random.permutation(rng, number_of)
    heavy_load, common = load_shares(number_of, rows * top, most, skew, True), load_shares(number_of, rows * top, most, skew, False)
    places = jnp.arange(number_of)

    def named(tallies, rotation):
        used = int((tallies > 0).sum())
        fixed = max(1, used // 4)
        shifted = fixed + (places - fixed + rotation * (used - fixed)) % max(1, number_of - fixed)
        return jnp.zeros((number_of,), jnp.int32).at[order[jnp.where(places < fixed, places, shifted)]].set(jnp.asarray(tallies, jnp.int32))

    tallies = jnp.where(number % 4 == 0, named(heavy_load, number // 4), named(common, number - number // 4 - 1))
    mixed = jax.random.permutation(jax.random.fold_in(own, 3), number_of)
    giver, receiver = mixed[0:number_of // 2 * 2:2], mixed[1:number_of // 2 * 2:2]
    margin = jnp.minimum(tallies[giver] - 1, most - tallies[receiver]) // 2
    margin = jnp.where((giver == order[0]) | (receiver == order[0]) | (tallies[receiver] == 0), 0, jnp.maximum(margin, 0))
    shifted = jax.random.randint(jax.random.fold_in(own, 4), (number_of // 2,), 0, 1 << 20) % (margin + 1)
    tallies = tallies.at[giver].add(-shifted).at[receiver].add(shifted)
    items = jnp.searchsorted(jnp.cumsum(tallies), jnp.arange(rows * top), side="right").astype(jnp.int32)
    table = items.reshape(top, rows).T
    table = table[jax.random.permutation(jax.random.fold_in(own, 1), rows)]
    rotation = jax.random.randint(jax.random.fold_in(own, 2), (rows, 1), 0, top)
    return jnp.take_along_axis(table, (jnp.arange(top)[None, :] + rotation) % top, axis=1)


def load_shares(number_of, total, bound, slope, full):
    portions = [(1 << 20) // math.isqrt(rank ** slope) + 1 for rank in range(1, number_of + 1)]
    largest = bound if full else min(bound, max(-(-total // number_of), total * portions[0] // sum(portions)))
    least = 1 if total - largest >= number_of - 1 else 0
    holding, surplus = [largest] + [least] * (number_of - 1), total - largest - least * (number_of - 1)
    while surplus > 0:
        candidates = [i for i in range(1, number_of) if holding[i] < largest] or [i for i in range(1, number_of) if holding[i] < bound]
        mass, left = sum([portions[i] for i in candidates]), surplus
        for i in candidates:
            addition = min(bound - holding[i], max(1, left * portions[i] // mass), surplus)
            holding[i] = holding[i] + addition
            surplus = surplus - addition
    return np.array(holding)


def normal_values(own_key, shape, spread, most, split=(), kind=jnp.bfloat16):
    values = spread * jax.random.normal(own_key, shape, jnp.float32)
    if split:
        values = values * levels(own_key, shape, split, -0.22, 0.18)
    return jnp.clip(values, -most, most).astype(kind)


def setup_inputs(seed: int = 0) -> dict:
    arg_keys = jax.random.split(jax.random.key(seed), 24)
    tokens = normal_values(arg_keys[0], (TOKENS, D), 1.0, 6.0, ((0, 32),))
    cotangent = normal_values(arg_keys[1], (TOKENS, D), 1.0, 6.0, ((0, 32),))
    routes_keys = jax.random.split(jax.random.fold_in(arg_keys[2], 1), TOKENS // SEQ)
    routes_turns = jax.random.permutation(jax.random.fold_in(arg_keys[2], 3), TOKENS // SEQ)
    routes = jax.vmap(lambda own, number: assign_block(jax.random.fold_in(arg_keys[2], 2), own, number, SEQ, EXPERTS, 1, CAP, 2))(routes_keys, routes_turns).reshape((TOKENS, 1))
    buckets = set_ends(jax.random.randint(arg_keys[3], (SEQ, SEQ), 0, BUCKETS), jax.random.fold_in(arg_keys[3], 1), 0, BUCKETS - 1).astype(jnp.int32)
    norm_first = jnp.clip(1.0 + 0.1 * jax.random.normal(arg_keys[4], (D,), jnp.float32), 0.5, 1.5)
    query_first = normal_values(arg_keys[5], (D, D), D ** -0.5, 0.21875, ((0, 4), (1, 2)))
    key_first = normal_values(arg_keys[6], (D, D), D ** -0.5, 0.21875, ((0, 4), (1, 2)))
    value_first = normal_values(arg_keys[7], (D, D), D ** -0.5, 0.21875, ((0, 4), (1, 2)))
    output_first = normal_values(arg_keys[8], (D, D), (D * 8 // SEQ) ** -0.5, 1.75, ((0, 2), (1, 4)))
    table_first = normal_values(arg_keys[9], (BUCKETS, HEADS), 1.0, 4.0, (), jnp.float32)
    dense_gain = jnp.clip(1.0 + 0.1 * jax.random.normal(arg_keys[10], (D,), jnp.float32), 0.5, 1.5)
    dense_in = normal_values(arg_keys[11], (D, FF), D ** -0.5, 0.21875, ((0, 4), (1, 2)))
    dense_out = normal_values(arg_keys[12], (FF, D), FF ** -0.5, 0.109375, ((0, 2), (1, 4)))
    norm_second = jnp.clip(1.0 + 0.1 * jax.random.normal(arg_keys[13], (D,), jnp.float32), 0.5, 1.5)
    query_second = normal_values(arg_keys[14], (D, D), D ** -0.5, 0.21875, ((0, 4), (1, 2)))
    key_second = normal_values(arg_keys[15], (D, D), D ** -0.5, 0.21875, ((0, 4), (1, 2)))
    value_second = normal_values(arg_keys[16], (D, D), D ** -0.5, 0.21875, ((0, 4), (1, 2)))
    output_second = normal_values(arg_keys[17], (D, D), (D * 8 // SEQ) ** -0.5, 1.75, ((0, 2), (1, 4)))
    table_second = normal_values(arg_keys[18], (BUCKETS, HEADS), 1.0, 4.0, (), jnp.float32)
    expert_gain = jnp.clip(1.0 + 0.1 * jax.random.normal(arg_keys[19], (D,), jnp.float32), 0.5, 1.5)
    router = normal_values(arg_keys[20], (D, EXPERTS), (4 * D) ** -0.5, 0.109375)
    expert_in = normal_values(arg_keys[21], (EXPERTS, D, FF), D ** -0.5, 0.21875, ((0, 4), (2, 2)))
    expert_out = normal_values(arg_keys[22], (EXPERTS, FF, D), (FF // 32) ** -0.5, 0.625, ((0, 4), (1, 2)))
    return {"tokens": tokens, "cotangent": cotangent, "routes": routes, "buckets": buckets, "norm_first": norm_first, "query_first": query_first, "key_first": key_first, "value_first": value_first, "output_first": output_first, "table_first": table_first, "dense_gain": dense_gain, "dense_in": dense_in, "dense_out": dense_out, "norm_second": norm_second, "query_second": query_second, "key_second": key_second, "value_second": value_second, "output_second": output_second, "table_second": table_second, "expert_gain": expert_gain, "router": router, "expert_in": expert_in, "expert_out": expert_out}


HIGHEST = lax.Precision.HIGHEST
EPSILON = 1e-06

@jax.custom_vjp
def low(v):
    return lax.optimization_barrier(v.astype(jnp.bfloat16)).astype(jnp.float32)

@jax.custom_vjp
def low_back(v):
    return v

def low_keep(v):
    return (low(v), None)

def low_pass(kept, grad):
    return (grad,)

def back_keep(v):
    return (v, None)

def back_low(kept, grad):
    return (low(grad),)
low.defvjp(low_keep, low_pass)
low_back.defvjp(back_keep, back_low)

def smooth_act(values):
    inner = 0.7978845608 * (values + 0.044715 * values * values * values)
    return 0.5 * values * (1.0 + jnp.tanh(inner))

def normalize(row_data, gain_vec):
    scale_rows = lax.rsqrt(lax.optimization_barrier(jnp.mean(row_data * row_data, axis=-1, keepdims=True)) + EPSILON)
    return row_data * scale_rows * gain_vec

def times_plain(operand_a, operand_b):
    return jnp.dot(operand_a, operand_b, precision=HIGHEST, preferred_element_type=jnp.float32)

def softmax_rows(scores):
    row_max = lax.optimization_barrier(jnp.max(scores, axis=-1, keepdims=True))
    exp_part = jnp.exp(scores - row_max)
    return exp_part / lax.optimization_barrier(jnp.sum(exp_part, axis=-1, keepdims=True))

def attend_sequence(query_rows, key_rows, value_rows, bias_full):
    scores = jnp.einsum('qhd,khd->hqk', query_rows, key_rows, precision=HIGHEST) * HEAD_DIM ** (-0.5) + bias_full
    probability = low(softmax_rows(low_back(scores)))
    return jnp.einsum('hqk,khd->qhd', probability, value_rows, precision=HIGHEST)

def attention(stream, gain_vec, w_query, w_key, w_value, w_output, table, buckets):
    normed = low(normalize(stream, gain_vec))
    seq_shape = (-1, SEQ, HEADS, HEAD_DIM)
    query_rows = low(low_back(times_plain(normed, w_query))).reshape(seq_shape)
    key_rows = low(low_back(times_plain(normed, w_key))).reshape(seq_shape)
    value_rows = low(low_back(times_plain(normed, w_value))).reshape(seq_shape)
    bias_full = jnp.transpose(table[buckets.astype(jnp.int32)], (2, 0, 1))

    def one_sequence(inputs):
        return attend_sequence(inputs[0], inputs[1], inputs[2], bias_full)
    mixed_rows = lax.map(jax.checkpoint(one_sequence), (query_rows, key_rows, value_rows))
    mixed_rows = low(low_back(mixed_rows.reshape(-1, D)))
    return low_back(times_plain(mixed_rows, w_output))

def feed_forward(stream, gain_vec, w_in, w_out):
    normed = low(normalize(stream, gain_vec))
    pre_act = low_back(times_plain(normed, w_in))
    hidden = low(smooth_act(pre_act))
    return low_back(times_plain(hidden, w_out))

def experts(stream, gain_vec, router, expert_in, expert_out, routes):
    normed = low(normalize(stream, gain_vec))
    probability = softmax_rows(low_back(times_plain(normed, router)))
    chosen = routes[:, 0].astype(jnp.int32)
    picked = chosen[:, None] == jnp.arange(EXPERTS, dtype=jnp.int32)[None, :]
    gate_value = lax.optimization_barrier(jnp.sum(jnp.where(picked, probability, 0.0), axis=-1, keepdims=True))
    by_sequence = picked.reshape(-1, SEQ, EXPERTS).astype(jnp.int32)
    running = (jnp.cumsum(by_sequence, axis=1) - 1).astype(jnp.int32)
    slot_ids = lax.optimization_barrier(jnp.sum(running * by_sequence, axis=2)).reshape(-1).astype(jnp.int32)
    sequence_id = (jnp.arange(chosen.shape[0], dtype=jnp.int32) // SEQ).astype(jnp.int32)
    positions = ((sequence_id * EXPERTS + chosen) * CAP + slot_ids).astype(jnp.int32)
    seq_count = chosen.shape[0] // SEQ
    buffer = jnp.zeros((seq_count * EXPERTS * CAP, D), normed.dtype).at[positions].set(normed)
    buffer = buffer.reshape(seq_count, EXPERTS, CAP, D)
    pre_act = low_back(jnp.einsum('secd,edf->secf', buffer, expert_in, precision=HIGHEST))
    hidden = low(smooth_act(pre_act))
    result_rows = low_back(jnp.einsum('secf,efd->secd', hidden, expert_out, precision=HIGHEST))
    return gate_value * result_rows.reshape(-1, D)[positions]

def forward(tokens, norm_first, query_first, key_first, value_first, output_first, table_first, dense_gain, dense_in, dense_out, norm_second, query_second, key_second, value_second, output_second, table_second, expert_gain, router, expert_in, expert_out, routes=None, buckets=None):
    stream_one = tokens + attention(tokens, norm_first, query_first, key_first, value_first, output_first, table_first, buckets)
    stream_two = stream_one + feed_forward(stream_one, dense_gain, dense_in, dense_out)
    stream_three = stream_two + attention(stream_two, norm_second, query_second, key_second, value_second, output_second, table_second, buckets)
    return stream_three + experts(stream_three, expert_gain, router, expert_in, expert_out, routes)

def reference(tokens, cotangent, routes, buckets, norm_first, query_first, key_first, value_first, output_first, table_first, dense_gain, dense_in, dense_out, norm_second, query_second, key_second, value_second, output_second, table_second, expert_gain, router, expert_in, expert_out):
    inputs = (tokens, norm_first, query_first, key_first, value_first, output_first, table_first, dense_gain, dense_in, dense_out, norm_second, query_second, key_second, value_second, output_second, table_second, expert_gain, router, expert_in, expert_out)
    floats = tuple((array_item.astype(jnp.float32) for array_item in inputs))
    result, pullback = jax.vjp(partial(forward, routes=routes, buckets=buckets), *floats)
    grads = pullback(cotangent.astype(jnp.float32))
    return (result, grads[0], grads[1], grads[2], grads[3], grads[4], grads[5], grads[6], grads[7], grads[8], grads[9], grads[10], grads[11], grads[12], grads[13], grads[14], grads[15], grads[16], grads[17], grads[18], grads[19])
```

```python
import functools

import jax
import jax.numpy as jnp
from jax import lax
from jax.experimental import pallas as pl
from jax.experimental.pallas import tpu as pltpu
from jax.sharding import PartitionSpec as P

EPSILON = 1e-06
BF16 = jnp.bfloat16
F32 = jnp.float32


def smooth_act(values):
    inner = 0.7978845608 * (values + 0.044715 * values * values * values)
    return 0.5 * values * (1.0 + jnp.tanh(inner))


def smooth_slope(values):
    inner = 0.7978845608 * (values + 0.044715 * values * values * values)
    tangent = jnp.tanh(inner)
    return 0.5 * (1.0 + tangent) + 0.5 * values * (1.0 - tangent * tangent) * 0.7978845608 * (
        1.0 + 0.134145 * values * values
    )


def row_scale(rows):
    return lax.rsqrt(jnp.mean(rows * rows, axis=-1, keepdims=True) + EPSILON)


def normalize(rows, gain):
    return rows * row_scale(rows) * gain


def norm_backward(rows, gain, upstream):
    scale = row_scale(rows)
    scaled = upstream * gain
    inner = jnp.mean(scaled * rows, axis=-1, keepdims=True)
    grad_rows = scale * scaled - rows * (scale * scale * scale * inner)
    grad_gain = jnp.sum(upstream * rows * scale, axis=0)
    return grad_rows, grad_gain


def dot_nn(a, b):
    return jnp.dot(a, b, preferred_element_type=F32)


def dot_tn(a, b):
    return lax.dot_general(a, b, (((0,), (0,)), ((), ())), preferred_element_type=F32)


def dot_nt(a, b):
    return lax.dot_general(a, b, (((1,), (1,)), ((), ())), preferred_element_type=F32)


def flip(x, axis, bit):
    count = lax.axis_size(axis)
    return lax.ppermute(x, axis, [(i, i ^ (1 << bit)) for i in range(count)])


def shift(x, axis, step):
    count = lax.axis_size(axis)
    return lax.ppermute(x, axis, [(i, (i + step) % count) for i in range(count)])


def kernel_call(body, outs, scalars, arrays, limit=48):
    vmem = pl.BlockSpec(memory_space=pltpu.VMEM)
    return pl.pallas_call(
        body,
        out_shape=[jax.ShapeDtypeStruct(shape, dtype) for shape, dtype in outs],
        in_specs=[pl.BlockSpec(memory_space=pltpu.SMEM)] + [vmem] * len(arrays),
        out_specs=[vmem] * len(outs),
        compiler_params=pltpu.CompilerParams(vmem_limit_bytes=limit << 20),
    )(scalars, *arrays)


def place_scalars():
    return jnp.stack([lax.axis_index("expert"), lax.axis_index("dp") & 3]).astype(jnp.int32)


def plane_spread(held):
    from_x = flip(held, "dp", 0)
    from_y = flip(held, "dp", 1)
    return held, from_x, from_y, flip(from_x[:, 0], "dp", 1), flip(from_y[:, 1], "dp", 0)


def gather_pair(left, right):
    count = lax.axis_size("expert")
    rows = left.shape[0] // 4
    place = (lax.axis_index("dp") & 3) * rows
    piece = jnp.stack([lax.dynamic_slice_in_dim(t, place, rows, 0) for t in (left, right)])
    return plane_spread(jnp.stack([shift(piece, "expert", step) for step in range(1, count)]))


def assemble(left, right, pieces):
    count = lax.axis_size("expert")
    rows, cols = left.shape
    quarter = rows // 4

    def body(where, left_ref, right_ref, own, from_x, from_y, diag_left, diag_right, *outs):
        z, place = where[0], where[1]
        for side, (shard, diag) in enumerate(((left_ref, diag_left), (right_ref, diag_right))):
            outs[side][pl.ds(pl.multiple_of(z * rows, 16), rows), :] = shard[...]
            for step in range(1, count):
                base = lax.rem(z + count - step, count) * rows
                for key, ref in ((0, own), (1, from_x), (2, from_y), (3, diag)):
                    row = pl.multiple_of(base + (place ^ key) * quarter, 16)
                    outs[side][pl.ds(row, quarter), :] = (
                        ref[step - 1] if key == 3 else ref[step - 1, side]
                    )

    full = ((count * rows, cols), left.dtype)
    return kernel_call(body, [full, full], place_scalars(), (left, right) + tuple(pieces))


def add_low(a, b):
    return (a.astype(F32) + b.astype(F32)).astype(BF16)


def reduce_pair(left, right, blocks):
    cols = left.shape[1]
    rows = left.shape[0] // blocks // 4
    shape = (blocks, 2, 2, rows, cols)
    where = place_scalars()

    def first(where, a, b, send_a, send_b, keep_a, keep_b):
        x, y = where[1] & 1, where[1] >> 1
        for k in range(blocks):
            for j in range(2):
                send_a[k, j] = a[k, j, 1 - x]
                keep_a[k, j] = a[k, j, x]
                send_b[k, j] = b[k, 1 - y, j]
                keep_b[k, j] = b[k, y, j]

    half = ((blocks, 2, rows, cols), BF16)
    send_a, send_b, keep_a, keep_b = kernel_call(
        first, [half] * 4, where, (left.reshape(shape), right.reshape(shape))
    )
    got_a, got_b = flip(send_a, "dp", 0), flip(send_b, "dp", 1)

    def second(where, keep_a, keep_b, got_a, got_b, send_a, send_b, next_a, next_b):
        x, y = where[1] & 1, where[1] >> 1
        for k in range(blocks):
            send_a[k] = add_low(keep_a[k, 1 - y], got_a[k, 1 - y])
            next_a[k] = add_low(keep_a[k, y], got_a[k, y])
            send_b[k] = add_low(keep_b[k, 1 - x], got_b[k, 1 - x])
            next_b[k] = add_low(keep_b[k, x], got_b[k, x])

    part = ((blocks, rows, cols), BF16)
    send_a, send_b, keep_a, keep_b = kernel_call(
        second, [part] * 4, where, (keep_a, keep_b, got_a, got_b)
    )
    got_a, got_b = flip(send_a, "dp", 1), flip(send_b, "dp", 0)
    far_bits = range(2, lax.axis_size("dp").bit_length() - 1)
    if blocks == 1:
        held = jnp.stack([add_low(keep_a, got_a), add_low(keep_b, got_b)], axis=1)
        for bit in far_bits:
            held = add_low(held, flip(held, "dp", bit))
    else:
        for bit in far_bits:
            keep_a, keep_b = add_low(keep_a, got_a), add_low(keep_b, got_b)
            got_a, got_b = flip(keep_a, "dp", bit), flip(keep_b, "dp", bit)

        def third(where, keep_a, keep_b, got_a, got_b, own, *sends):
            for step in range(blocks):
                block = lax.rem(where[0] + step, blocks)
                out = own if step == 0 else sends[step - 1]
                out[0] = add_low(keep_a[block], got_a[block])
                out[1] = add_low(keep_b[block], got_b[block])

        own, *sends = kernel_call(
            third, [((2, rows, cols), BF16)] * blocks, where, (keep_a, keep_b, got_a, got_b)
        )
        total = own.astype(F32)
        for step, send in enumerate(sends):
            total = total + shift(send, "expert", step + 1).astype(F32)
        held = total.astype(BF16)[None]
    spread = plane_spread(held)

    def last(where, own, from_x, from_y, diag_a, diag_b, out_a, out_b):
        place = where[1]
        for side, (out, diag) in enumerate(((out_a, diag_a), (out_b, diag_b))):
            for key, ref in ((0, own), (1, from_x), (2, from_y), (3, diag)):
                row = pl.multiple_of((place ^ key) * rows, 8)
                value = ref[0] if key == 3 else ref[0, side]
                out[pl.ds(row, rows), :] = value.astype(F32)

    return kernel_call(last, [((4 * rows, cols), F32)] * 2, where, spread)


def all_sum(x):
    for axis in ("mp", "dp", "expert"):
        for bit in range(lax.axis_size(axis).bit_length() - 1):
            x = x + flip(x, axis, bit)
    return x


def build_bias(buckets, tables):
    heads = tables.shape[0]
    seq_len = buckets.shape[0]
    padded = jnp.pad(tables, ((0, 0), (0, 128 - tables.shape[1])))

    def body(bucket_ref, table_ref, out_ref):
        head = pl.program_id(0)
        row = jnp.broadcast_to(table_ref[pl.ds(head, 1), :], (seq_len, 128))
        for part in range(seq_len // 128):
            index = bucket_ref[:, part * 128 : (part + 1) * 128]
            out_ref[0, :, part * 128 : (part + 1) * 128] = jnp.take_along_axis(row, index, axis=1)

    return pl.pallas_call(
        body,
        out_shape=jax.ShapeDtypeStruct((heads, seq_len, seq_len), F32),
        grid=(heads,),
        in_specs=[
            pl.BlockSpec((seq_len, seq_len), lambda h: (0, 0)),
            pl.BlockSpec((heads, 128), lambda h: (0, 0)),
        ],
        out_specs=pl.BlockSpec((1, seq_len, seq_len), lambda h: (h, 0, 0)),
    )(buckets, padded)


def attention_forward(normed, weights, bias):
    seq_len = normed.shape[0]
    heads = bias.shape[0]
    width = weights[0].shape[1] // 2
    head_width = width // heads
    joint = jnp.concatenate(
        [dot_nn(normed, weights[0]), dot_nn(normed, weights[1][:, :width])], axis=1
    ).astype(BF16)
    query, key, value = (
        joint[:, i * width : (i + 1) * width].reshape(seq_len, heads, head_width) for i in range(3)
    )
    scores = (
        jnp.einsum("qhd,khd->hqk", query, key, preferred_element_type=F32) * head_width**-0.5 + bias
    )
    row_max = jnp.max(scores, axis=-1, keepdims=True)
    exp_part = jnp.exp(scores - row_max)
    prob = (exp_part / jnp.sum(exp_part, axis=-1, keepdims=True)).astype(BF16)
    mixed = jnp.einsum("hqk,khd->qhd", prob, value, preferred_element_type=F32).astype(BF16)
    mixed = mixed.reshape(seq_len, width)
    partial = dot_nt(mixed, weights[1][:, width:]).astype(BF16)
    return partial, (normed, query, key, value, prob, mixed)


def attention_backward(saved, weights, buckets, bucket_count, grad):
    normed, query, key, value, prob, mixed = saved
    seq_len, heads, head_width = query.shape
    width = heads * head_width
    scale = head_width**-0.5
    grad_mixed = dot_nn(grad, weights[1][:, width:]).astype(BF16).reshape(seq_len, heads, head_width)
    grad_value = jnp.einsum("hqk,qhd->khd", prob, grad_mixed, preferred_element_type=F32)
    grad_prob = jnp.einsum("qhd,khd->hqk", grad_mixed, value, preferred_element_type=F32)
    wide = prob.astype(F32)
    grad_scores = (wide * (grad_prob - jnp.sum(wide * grad_prob, axis=-1, keepdims=True))).astype(BF16)
    grad_query = jnp.einsum("hqk,khd->qhd", grad_scores, key, preferred_element_type=F32) * scale
    grad_key = jnp.einsum("hqk,qhd->khd", grad_scores, query, preferred_element_type=F32) * scale
    grad_query, grad_key, grad_value = (
        g.reshape(seq_len, width).astype(BF16) for g in (grad_query, grad_key, grad_value)
    )
    left = jnp.concatenate([grad_query, grad_key], axis=1)
    partial = (dot_nt(left, weights[0]) + dot_nt(grad_value, weights[1][:, :width])).astype(BF16)
    grads = (
        dot_tn(normed, left).astype(BF16),
        jnp.concatenate(
            [dot_tn(normed, grad_value).astype(BF16), dot_tn(grad, mixed).astype(BF16)], axis=1
        ),
    )
    levels = jnp.arange(bucket_count, dtype=jnp.int32)
    onehot = (buckets[:, :, None] == levels[None, None, :]).astype(BF16)
    table = jnp.einsum("hqk,qkb->bh", grad_scores, onehot, preferred_element_type=F32)
    return partial, grads, table


def joined(stream, partial):
    other = flip(partial, "mp", 0)
    return stream + (partial.astype(F32) + other.astype(F32))


def on_device(
    tokens,
    cotangent,
    routes,
    buckets,
    norm_first,
    query_first,
    key_first,
    value_first,
    output_first,
    table_first,
    dense_gain,
    dense_in,
    dense_out,
    norm_second,
    query_second,
    key_second,
    value_second,
    output_second,
    table_second,
    expert_gain,
    router,
    expert_in,
    expert_out,
):
    mp_index = lax.axis_index("mp")
    z_index = lax.axis_index("expert")
    z_count = lax.axis_size("expert")
    tok_local, model_width = tokens.shape
    seq_len = buckets.shape[0]
    expert_count = router.shape[1]
    capacity = seq_len // 2
    slots = capacity // lax.axis_size("mp")
    bucket_count = table_first.shape[0]
    head_local = table_first.shape[1] // lax.axis_size("mp")

    width = query_first.shape[1]
    shards = (
        (
            jnp.concatenate([query_first, key_first], axis=1),
            jnp.concatenate([value_first, output_first.T], axis=1),
        ),
        (dense_in, dense_out.T),
        (
            jnp.concatenate([query_second, key_second], axis=1),
            jnp.concatenate([value_second, output_second.T], axis=1),
        ),
    )
    gathered = [gather_pair(*pair) for pair in shards]

    stream_zero = lax.all_gather(tokens, "mp", axis=0, tiled=True).astype(F32)
    grad_four_low = lax.all_gather(cotangent, "mp", axis=0, tiled=True)

    tables = jnp.concatenate(
        [
            lax.dynamic_slice_in_dim(t, mp_index * head_local, head_local, 1).T
            for t in (table_first, table_second)
        ],
        axis=0,
    )
    bias = build_bias(buckets, tables)

    chosen = routes[:, 0]
    experts = jnp.arange(expert_count, dtype=jnp.int32)
    picked = chosen[:, None] == experts[None, :]
    order = jnp.arange(seq_len, dtype=jnp.int32)
    earlier = (order[None, :] < order[:, None]).astype(BF16)
    rank = jnp.sum(
        jnp.where(picked, dot_nn(earlier, picked.astype(BF16)), 0.0), axis=1
    ).astype(jnp.int32)
    distance = (chosen - z_index + z_count) % z_count
    mine = jnp.where(rank // slots == mp_index, distance * slots + rank % slots, -1)
    send_spots = jnp.arange(z_count * slots, dtype=jnp.int32)
    to_slots = (send_spots[:, None] == mine[None, :]).astype(BF16)
    half = z_count * slots
    where_back = jnp.where(rank // slots == mp_index, 0, half) + distance * slots + rank % slots
    back_spots = jnp.arange(2 * half, dtype=jnp.int32)
    from_slots = (where_back[:, None] == back_spots[None, :]).astype(BF16)

    def dispatch(rows):
        sent = dot_nn(to_slots, rows).astype(BF16)
        blocks = [sent[:slots]] + [
            shift(sent[step * slots : (step + 1) * slots], "expert", step)
            for step in range(1, z_count)
        ]
        own = jnp.concatenate(blocks, axis=0)
        return own, jnp.concatenate([own, flip(own, "mp", 0)], axis=0)

    def give_back(rows):
        return jnp.concatenate(
            [rows[:slots]]
            + [
                shift(rows[step * slots : (step + 1) * slots], "expert", z_count - step)
                for step in range(1, z_count)
            ],
            axis=0,
        )

    weights_one = assemble(*shards[0], gathered[0])
    normed = normalize(stream_zero, norm_first).astype(BF16)
    partial, saved_one = attention_forward(normed, weights_one, bias[:head_local])
    stream_one = joined(stream_zero, partial)

    dense_in_full, dense_out_full = assemble(*shards[1], gathered[1])
    dense_normed = normalize(stream_one, dense_gain).astype(BF16)
    dense_pre = dot_nn(dense_normed, dense_in_full)
    dense_hidden = smooth_act(dense_pre).astype(BF16)
    stream_two = joined(stream_one, dot_nt(dense_hidden, dense_out_full).astype(BF16))

    grad_four_tied, stream_two = lax.optimization_barrier((grad_four_low, stream_two))
    grad_own, grad_at_expert = dispatch(grad_four_tied)

    weights_two = assemble(*shards[2], gathered[2])
    normed_two = normalize(stream_two, norm_second).astype(BF16)
    partial, saved_two = attention_forward(normed_two, weights_two, bias[head_local:])
    stream_three = joined(stream_two, partial)

    moe_rows = normalize(stream_three, expert_gain).astype(BF16)
    moe_own, moe_at = dispatch(moe_rows)
    logits = dot_nn(moe_at, router)
    exp_part = jnp.exp(logits - jnp.max(logits, axis=-1, keepdims=True))
    prob = exp_part / jnp.sum(exp_part, axis=-1, keepdims=True)
    here = (experts == z_index)[None, :]
    gate = jnp.sum(jnp.where(here, prob, 0.0), axis=-1, keepdims=True)
    w_in, w_out = expert_in[0], expert_out[0]
    expert_pre = dot_nn(moe_at, w_in)
    expert_hidden = smooth_act(expert_pre).astype(BF16)
    expert_part = dot_nn(expert_hidden, w_out).astype(BF16)
    grad_rows = (gate * grad_at_expert.astype(F32)).astype(BF16)
    grad_pre = (dot_nt(grad_rows, w_out) * smooth_slope(expert_pre)).astype(BF16)
    back_part = dot_nt(grad_pre, w_in).astype(BF16)
    expert_own = expert_part[:half].astype(F32) + flip(expert_part[half:], "mp", 0).astype(F32)
    back_own = back_part[:half].astype(F32) + flip(back_part[half:], "mp", 0).astype(F32)
    gate_own, prob_own = gate[:half], prob[:half]
    grad_gate = jnp.sum(grad_own.astype(F32) * expert_own, axis=-1, keepdims=True)
    grad_logits = (prob_own * (jnp.where(here, grad_gate, 0.0) - grad_gate * gate_own)).astype(BF16)
    back_own = (back_own + dot_nt(grad_logits, router)).astype(BF16)
    grad_router = dot_tn(moe_own, grad_logits)

    back_half = give_back(back_own)
    back_all = jnp.concatenate([back_half, flip(back_half, "mp", 0)], axis=0)
    grad_moe = dot_nn(from_slots, back_all)

    grad_expert_in = dot_tn(moe_at, grad_pre).astype(BF16)
    grad_expert_out = dot_tn(expert_hidden, grad_rows).astype(BF16)
    flat = (model_width, grad_expert_in.shape[1])
    expert_in_sum, expert_out_sum = reduce_pair(grad_expert_in, grad_expert_out.reshape(flat), 1)
    expert_out_sum = expert_out_sum.reshape(grad_expert_out.shape)

    result_half = give_back(expert_own.astype(BF16))
    result_all = jnp.concatenate([result_half, flip(result_half, "mp", 0)], axis=0)
    first_row = mp_index * tok_local
    own_spots = lax.dynamic_slice_in_dim(from_slots, first_row, tok_local, 0)
    own_rows = lax.dynamic_slice_in_dim(moe_rows, first_row, tok_local, 0)
    own_picked = lax.dynamic_slice_in_dim(picked, first_row, tok_local, 0)
    own_logits = dot_nn(own_rows, router)
    own_exp = jnp.exp(own_logits - jnp.max(own_logits, axis=-1, keepdims=True))
    own_prob = own_exp / jnp.sum(own_exp, axis=-1, keepdims=True)
    own_gate = jnp.sum(jnp.where(own_picked, own_prob, 0.0), axis=-1, keepdims=True)
    final_rows = lax.dynamic_slice_in_dim(
        stream_three, first_row, tok_local, 0
    ) + own_gate * dot_nn(own_spots, result_all)

    grad_input, grad_expert_gain = norm_backward(stream_three, expert_gain, grad_moe)
    grad_three = grad_four_low.astype(F32) + grad_input
    partial, unit_grads_two, table_grad_two = attention_backward(
        saved_two, weights_two, buckets, bucket_count, grad_three.astype(BF16)
    )
    zero = jnp.zeros((), F32)
    grad_input, grad_norm_second = norm_backward(stream_two, norm_second, joined(zero, partial))
    grad_two = grad_three + grad_input

    grad_low = grad_two.astype(BF16)
    grad_dense_pre = (dot_nn(grad_low, dense_out_full) * smooth_slope(dense_pre)).astype(BF16)
    partial = dot_nt(grad_dense_pre, dense_in_full).astype(BF16)
    unit_in = dot_tn(dense_normed, grad_dense_pre).astype(BF16)
    unit_out = dot_tn(grad_low, dense_hidden).astype(BF16)
    grad_input, grad_dense_gain = norm_backward(stream_one, dense_gain, joined(zero, partial))
    grad_one = grad_two + grad_input

    partial, unit_grads_one, table_grad_one = attention_backward(
        saved_one, weights_one, buckets, bucket_count, grad_one.astype(BF16)
    )
    grad_input, grad_norm_first = norm_backward(stream_zero, norm_first, joined(zero, partial))
    grad_zero = lax.dynamic_slice_in_dim(grad_one + grad_input, first_row, tok_local, 0)

    two = reduce_pair(*unit_grads_two, z_count)
    ff_in, ff_out = reduce_pair(unit_in, unit_out, z_count)
    one = reduce_pair(*unit_grads_one, z_count)

    table_zero = jnp.zeros(table_first.shape, F32)
    full_one = lax.dynamic_update_slice_in_dim(table_zero, table_grad_one, mp_index * head_local, 1)
    full_two = lax.dynamic_update_slice_in_dim(table_zero, table_grad_two, mp_index * head_local, 1)
    share = 1.0 / lax.axis_size("mp")
    parts = [
        grad_norm_first * share,
        grad_dense_gain * share,
        grad_norm_second * share,
        grad_expert_gain * share,
        grad_router.T.reshape(-1),
        full_one.T.reshape(-1),
        full_two.T.reshape(-1),
    ]
    sizes = [p.shape[0] for p in parts]
    packed = all_sum(jnp.concatenate(parts).reshape(-1, 128)).reshape(-1)
    small, start = [], 0
    for size in sizes:
        small.append(packed[start : start + size])
        start += size
    router_sum = small[4].reshape(expert_count, model_width).T
    table_one_sum = small[5].reshape(table_first.shape[1], bucket_count).T
    table_two_sum = small[6].reshape(table_first.shape[1], bucket_count).T

    return (
        final_rows,
        grad_zero,
        small[0],
        one[0][:, :width],
        one[0][:, width:],
        one[1][:, :width],
        one[1][:, width:].T,
        table_one_sum,
        small[1],
        ff_in,
        ff_out.T,
        small[2],
        two[0][:, :width],
        two[0][:, width:],
        two[1][:, :width],
        two[1][:, width:].T,
        table_two_sum,
        small[3],
        router_sum,
        expert_in_sum[None],
        expert_out_sum[None],
    )


def solution(mesh):
    rows = P(("dp", "expert", "mp"), None)
    cols_in, cols_out = P("expert", "mp"), P("mp", "expert")
    attention_in = (P(), cols_in, cols_in, cols_in, cols_out, P())
    dense = (P(), cols_in, cols_out)
    return jax.shard_map(
        on_device,
        mesh=mesh,
        in_specs=(rows, rows, P(("dp", "expert"), None), P())
        + attention_in
        + dense
        + attention_in
        + (P(), P(), P("expert", None, "mp"), P("expert", "mp", None)),
        out_specs=(rows, rows)
        + attention_in
        + dense
        + attention_in
        + (P(), P(), P("expert", None, "mp"), P("expert", "mp", None)),
        check_vma=False,
    )
```

```python
import functools

import jax
import jax.numpy as jnp
from jax import lax
from jax.experimental import pallas as pl
from jax.experimental.pallas import tpu as pltpu
from jax.sharding import PartitionSpec as P

EPSILON = 1e-06
BF16 = jnp.bfloat16
F32 = jnp.float32


def smooth_act(values):
    inner = 0.7978845608 * (values + 0.044715 * values * values * values)
    return 0.5 * values * (1.0 + jnp.tanh(inner))


def smooth_slope(values):
    inner = 0.7978845608 * (values + 0.044715 * values * values * values)
    tangent = jnp.tanh(inner)
    return 0.5 * (1.0 + tangent) + 0.5 * values * (1.0 - tangent * tangent) * 0.7978845608 * (
        1.0 + 0.134145 * values * values
    )


def row_scale(rows):
    return lax.rsqrt(jnp.mean(rows * rows, axis=-1, keepdims=True) + EPSILON)


def normalize(rows, gain):
    return rows * row_scale(rows) * gain


def dot_nn(a, b):
    return jnp.dot(a, b, preferred_element_type=F32)


def dot_tn(a, b):
    return lax.dot_general(a, b, (((0,), (0,)), ((), ())), preferred_element_type=F32)


def dot_nt(a, b):
    return lax.dot_general(a, b, (((1,), (1,)), ((), ())), preferred_element_type=F32)


def flip(x, axis, bit):
    count = lax.axis_size(axis)
    return lax.ppermute(x, axis, [(i, i ^ (1 << bit)) for i in range(count)])


def shift(x, axis, step):
    count = lax.axis_size(axis)
    return lax.ppermute(x, axis, [(i, (i + step) % count) for i in range(count)])


def kernel_call(body, outs, scalars, arrays, limit=48):
    vmem = pl.BlockSpec(memory_space=pltpu.VMEM)
    return pl.pallas_call(
        body,
        out_shape=[jax.ShapeDtypeStruct(shape, dtype) for shape, dtype in outs],
        in_specs=[pl.BlockSpec(memory_space=pltpu.SMEM)] + [vmem] * len(arrays),
        out_specs=[vmem] * len(outs),
        compiler_params=pltpu.CompilerParams(vmem_limit_bytes=limit << 20),
    )(scalars, *arrays)


def place_scalars():
    return jnp.stack([lax.axis_index("expert"), lax.axis_index("dp") & 3]).astype(jnp.int32)


def plane_spread(held):
    from_x = flip(held, "dp", 0)
    from_y = flip(held, "dp", 1)
    return held, from_x, from_y, flip(from_x[:, 0], "dp", 1), flip(from_y[:, 1], "dp", 0)


def gather_pair(left, right):
    count = lax.axis_size("expert")
    rows = left.shape[0] // 4
    place = (lax.axis_index("dp") & 3) * rows
    piece = jnp.stack([lax.dynamic_slice_in_dim(t, place, rows, 0) for t in (left, right)])
    return plane_spread(jnp.stack([shift(piece, "expert", step) for step in range(1, count)]))


def assemble(left, right, pieces):
    count = lax.axis_size("expert")
    rows, cols = left.shape
    quarter = rows // 4

    def body(where, left_ref, right_ref, own, from_x, from_y, diag_left, diag_right, *outs):
        z, place = where[0], where[1]
        for side, (shard, diag) in enumerate(((left_ref, diag_left), (right_ref, diag_right))):
            outs[side][pl.ds(pl.multiple_of(z * rows, 16), rows), :] = shard[...]
            for step in range(1, count):
                base = lax.rem(z + count - step, count) * rows
                for key, ref in ((0, own), (1, from_x), (2, from_y), (3, diag)):
                    row = pl.multiple_of(base + (place ^ key) * quarter, 16)
                    outs[side][pl.ds(row, quarter), :] = (
                        ref[step - 1] if key == 3 else ref[step - 1, side]
                    )

    full = ((count * rows, cols), left.dtype)
    return kernel_call(body, [full, full], place_scalars(), (left, right) + tuple(pieces))


def add_low(a, b):
    return (a.astype(F32) + b.astype(F32)).astype(BF16)


def reduce_pair(send_a, send_b, keep_a, keep_b):
    blocks, _, rows, cols = send_a.shape
    where = place_scalars()
    got_a, got_b = flip(send_a, "dp", 0), flip(send_b, "dp", 1)

    def second(where, keep_a, keep_b, got_a, got_b, send_a, send_b, next_a, next_b):
        x, y = where[1] & 1, where[1] >> 1
        for k in range(blocks):
            send_a[k] = add_low(keep_a[k, 1 - y], got_a[k, 1 - y])
            next_a[k] = add_low(keep_a[k, y], got_a[k, y])
            send_b[k] = add_low(keep_b[k, 1 - x], got_b[k, 1 - x])
            next_b[k] = add_low(keep_b[k, x], got_b[k, x])

    part = ((blocks, rows, cols), BF16)
    send_a, send_b, keep_a, keep_b = kernel_call(
        second, [part] * 4, where, (keep_a, keep_b, got_a, got_b)
    )
    got_a, got_b = flip(send_a, "dp", 1), flip(send_b, "dp", 0)
    far_bits = range(2, lax.axis_size("dp").bit_length() - 1)
    for bit in far_bits:
        keep_a, keep_b = add_low(keep_a, got_a), add_low(keep_b, got_b)
        got_a, got_b = flip(keep_a, "dp", bit), flip(keep_b, "dp", bit)

    def third(where, keep_a, keep_b, got_a, got_b, own, *sends):
        for step in range(blocks):
            block = lax.rem(where[0] + step, blocks)
            out = own if step == 0 else sends[step - 1]
            out[0] = add_low(keep_a[block], got_a[block])
            out[1] = add_low(keep_b[block], got_b[block])

    own, *sends = kernel_call(
        third, [((2, rows, cols), BF16)] * blocks, where, (keep_a, keep_b, got_a, got_b)
    )
    total = own.astype(F32)
    for step, send in enumerate(sends):
        total = total + shift(send, "expert", step + 1).astype(F32)
    held = total.astype(BF16)[None]
    spread = plane_spread(held)

    def last(where, own, from_x, from_y, diag_a, diag_b, out_a, out_b):
        place = where[1]
        for side, (out, diag) in enumerate(((out_a, diag_a), (out_b, diag_b))):
            for key, ref in ((0, own), (1, from_x), (2, from_y), (3, diag)):
                row = pl.multiple_of((place ^ key) * rows, 8)
                value = ref[0] if key == 3 else ref[0, side]
                out[pl.ds(row, rows), :] = value.astype(F32)

    return kernel_call(last, [((4 * rows, cols), F32)] * 2, where, spread)


def all_sum(x):
    for axis in ("mp", "dp", "expert"):
        for bit in range(lax.axis_size(axis).bit_length() - 1):
            x = x + flip(x, axis, bit)
    return x


def whole(shape):
    return pl.BlockSpec(shape, lambda *_: (0,) * len(shape))


PARAMS = pltpu.CompilerParams(vmem_limit_bytes=56 << 20)


def build_bias(buckets, tables):
    heads = tables.shape[0]
    seq_len = buckets.shape[0]
    padded = jnp.pad(tables, ((0, 0), (0, 128 - tables.shape[1])))

    def body(bucket_ref, table_ref, out_ref):
        head = pl.program_id(0)
        row = jnp.broadcast_to(table_ref[pl.ds(head, 1), :], (seq_len, 128))
        for part in range(seq_len // 128):
            index = bucket_ref[:, part * 128 : (part + 1) * 128]
            out_ref[0, :, part * 128 : (part + 1) * 128] = jnp.take_along_axis(row, index, axis=1)

    return pl.pallas_call(
        body,
        out_shape=jax.ShapeDtypeStruct((heads, seq_len, seq_len), F32),
        grid=(heads,),
        in_specs=[whole((seq_len, seq_len)), whole((heads, 128))],
        out_specs=pl.BlockSpec((1, seq_len, seq_len), lambda h: (h, 0, 0)),
        compiler_params=PARAMS,
    )(buckets, padded)


def lane_masks(head_width):
    lane = lax.broadcasted_iota(jnp.int32, (1, 2 * head_width), 1)
    return [lane < head_width, lane >= head_width]


def masked(value, mask):
    return jnp.where(mask, value, jnp.zeros_like(value))


def stream_sum(base, partials):
    total = base[...].astype(F32)
    if partials:
        total = total + (partials[0][...].astype(F32) + partials[1][...].astype(F32))
    return total


def attention_forward(base, partials, gain, weights, bias):
    seq_len, model = base.shape
    heads = bias.shape[0]
    width = weights[0].shape[1] // 2
    head_width = width // heads
    chunk = 128
    scale = head_width**-0.5
    count = len(partials)

    def body(*refs):
        base_ref, part_refs = refs[0], refs[1 : 1 + count]
        gain_ref, wa_ref, wb_ref, bias_ref = refs[1 + count : 5 + count]
        stream_ref, normed_ref, joint_ref, prob_ref, mixed_ref, partial_ref = refs[5 + count :]
        step = pl.program_id(0)

        @pl.when(step == 0)
        def _():
            rows = stream_sum(base_ref, part_refs)
            stream_ref[...] = rows
            normed = normalize(rows, gain_ref[...]).astype(BF16)
            normed_ref[...] = normed
            left = dot_nn(normed, wa_ref[...]).astype(BF16)
            joint_ref[:, :width] = left[:, :width] * jnp.asarray(scale, BF16)
            joint_ref[:, width : 2 * width] = left[:, width:]
            joint_ref[:, 2 * width :] = dot_nn(normed, wb_ref[:, :width]).astype(BF16)

        masks = lane_masks(head_width)
        rows = pl.ds(pl.multiple_of(step * chunk, chunk), chunk)
        for pair in range(heads // 2):
            cols = slice(pair * 2 * head_width, (pair + 1) * 2 * head_width)
            query = joint_ref[rows, cols]
            key = joint_ref[:, slice(width + cols.start, width + cols.stop)]
            value = joint_ref[:, slice(2 * width + cols.start, 2 * width + cols.stop)]
            mixed = None
            for side in range(2):
                head = 2 * pair + side
                scores = dot_nt(query, masked(key, masks[side])) + bias_ref[head]
                exp_part = jnp.exp(scores - jnp.max(scores, axis=-1, keepdims=True))
                prob = (exp_part / jnp.sum(exp_part, axis=-1, keepdims=True)).astype(BF16)
                prob_ref[head] = prob
                out = dot_nn(prob, masked(value, masks[side]))
                mixed = out if mixed is None else mixed + out
            mixed_ref[:, cols] = mixed.astype(BF16)
        partial_ref[...] = dot_nt(mixed_ref[...], wb_ref[:, width:]).astype(BF16)

    full = (seq_len, model)
    shapes = [
        (full, F32, whole(full)),
        (full, BF16, whole(full)),
        ((seq_len, 3 * width), BF16, whole((seq_len, 3 * width))),
        ((heads, seq_len, seq_len), BF16, pl.BlockSpec((heads, chunk, seq_len), lambda i: (0, i, 0))),
        ((seq_len, width), BF16, pl.BlockSpec((chunk, width), lambda i: (i, 0))),
        (full, BF16, pl.BlockSpec((chunk, model), lambda i: (i, 0))),
    ]
    return pl.pallas_call(
        body,
        out_shape=[jax.ShapeDtypeStruct(shape, dtype) for shape, dtype, _ in shapes],
        grid=(seq_len // chunk,),
        in_specs=[whole(full)] * (1 + count)
        + [whole((1, model)), whole(weights[0].shape), whole(weights[1].shape)]
        + [pl.BlockSpec((heads, chunk, seq_len), lambda i: (0, i, 0))],
        out_specs=[spec for _, _, spec in shapes],
        compiler_params=PARAMS,
    )(base, *partials, gain[None], *weights, bias)


def attention_backward(grad, weights, joint, prob):
    seq_len, model = grad.shape
    heads = prob.shape[0]
    width = weights[0].shape[1] // 2
    head_width = width // heads
    chunk = 128
    steps = seq_len // chunk
    scale = head_width**-0.5

    def body(grad_ref, wa_ref, wb_ref, joint_ref, prob_ref, dj_ref, ds_ref, partial_ref, dk_acc, dv_acc):
        step = pl.program_id(0)

        @pl.when(step == 0)
        def _():
            dk_acc[...] = jnp.zeros_like(dk_acc)
            dv_acc[...] = jnp.zeros_like(dv_acc)

        masks = lane_masks(head_width)
        rows = pl.ds(pl.multiple_of(step * chunk, chunk), chunk)
        grad_mixed = dot_nn(grad_ref[...], wb_ref[:, width:]).astype(BF16)
        for pair in range(heads // 2):
            cols = slice(pair * 2 * head_width, (pair + 1) * 2 * head_width)
            query = joint_ref[rows, cols]
            key = joint_ref[:, slice(width + cols.start, width + cols.stop)]
            value = joint_ref[:, slice(2 * width + cols.start, 2 * width + cols.stop)]
            go = grad_mixed[:, cols]
            dq = None
            dk = None
            dv = None
            for side in range(2):
                head = 2 * pair + side
                low = prob_ref[head]
                wide = low.astype(F32)
                grad_prob = dot_nt(go, masked(value, masks[side]))
                inner = jnp.sum(wide * grad_prob, axis=-1, keepdims=True)
                ds = (wide * (grad_prob - inner)).astype(BF16)
                ds_ref[head] = ds
                one_q = dot_nn(ds, masked(key, masks[side]))
                one_k = dot_tn(ds, masked(query, masks[side]))
                one_v = dot_tn(low, masked(go, masks[side]))
                dq = one_q if dq is None else dq + one_q
                dk = one_k if dk is None else dk + one_k
                dv = one_v if dv is None else dv + one_v
            dj_ref[rows, cols] = (dq * scale).astype(BF16)
            dk_acc[:, cols] += dk
            dv_acc[:, cols] += dv

        @pl.when(step == steps - 1)
        def _():
            dj_ref[:, width : 2 * width] = dk_acc[...].astype(BF16)
            dj_ref[:, 2 * width :] = dv_acc[...].astype(BF16)
            partial_ref[...] = (
                dot_nt(dj_ref[:, : 2 * width], wa_ref[...])
                + dot_nt(dj_ref[:, 2 * width :], wb_ref[:, :width])
            ).astype(BF16)

    full = (seq_len, model)
    rows_of = pl.BlockSpec((heads, chunk, seq_len), lambda i: (0, i, 0))
    return pl.pallas_call(
        body,
        out_shape=[
            jax.ShapeDtypeStruct((seq_len, 3 * width), BF16),
            jax.ShapeDtypeStruct(prob.shape, BF16),
            jax.ShapeDtypeStruct(full, BF16),
        ],
        grid=(steps,),
        in_specs=[
            pl.BlockSpec((chunk, model), lambda i: (i, 0)),
            whole(weights[0].shape),
            whole(weights[1].shape),
            whole(joint.shape),
            rows_of,
        ],
        out_specs=[whole((seq_len, 3 * width)), rows_of, whole(full)],
        scratch_shapes=[pltpu.VMEM((seq_len, width), F32)] * 2,
        compiler_params=PARAMS,
    )(grad, *weights, joint, prob)


def split_first(where, a, b, send_a, send_b, keep_a, keep_b, blocks):
    rows = send_a.shape[2]
    x, y = where[1] & 1, where[1] >> 1
    for k in range(blocks):
        for j in range(2):
            for i in range(2):
                at = (k * 4 + j * 2 + i) * rows
                piece_a, piece_b = a[at : at + rows], b[at : at + rows]

                @pl.when(x == i)
                def _():
                    keep_a[k, j] = piece_a

                @pl.when(x != i)
                def _():
                    send_a[k, j] = piece_a

                @pl.when(y == j)
                def _():
                    keep_b[k, i] = piece_b

                @pl.when(y != j)
                def _():
                    send_b[k, i] = piece_b


def weight_grads(blocks, lefts, rights):
    model = lefts[0][0].shape[1]
    cols = sum(y.shape[1] for _, y in lefts)
    rows = model // blocks // 4
    half = ((blocks, 2, rows, cols), BF16)
    flat = [t for pair in lefts + rights for t in pair]

    def body(where, *refs):
        inputs, outs = refs[: len(flat)], refs[len(flat) :]

        def side(number, pairs):
            return jnp.concatenate(
                [
                    dot_tn(inputs[number + 2 * i][...], inputs[number + 2 * i + 1][...]).astype(BF16)
                    for i in range(len(pairs))
                ],
                axis=1,
            )

        split_first(where, side(0, lefts), side(2 * len(lefts), rights), *outs, blocks)

    return kernel_call(body, [half] * 4, place_scalars(), flat)


def table_grad(ds, buckets, bucket_count):
    heads, seq_len, _ = ds.shape
    group = 8

    def body(ds_ref, bucket_ref, out_ref, acc):
        acc[...] = jnp.zeros_like(acc)

        def one(number, carry):
            rows = pl.ds(pl.multiple_of(number * group, group), group)
            index = bucket_ref[rows, :]
            hot = jnp.concatenate(
                [jnp.where(index == level, 1.0, 0.0) for level in range(bucket_count)], axis=0
            ).astype(BF16)
            left = jnp.concatenate(
                [ds_ref[head, rows, :].astype(F32) for head in range(heads)], axis=0
            ).astype(BF16)
            acc[...] += dot_nt(left, hot)
            return carry

        lax.fori_loop(0, seq_len // group, one, 0, unroll=2)
        shape = acc.shape
        same = (
            lax.broadcasted_iota(jnp.int32, shape, 0) % group
            == lax.broadcasted_iota(jnp.int32, shape, 1) % group
        )
        kept = jnp.where(same, acc[...], 0.0)
        spread = (
            lax.broadcasted_iota(jnp.int32, (shape[1], bucket_count), 0) // group
            == lax.broadcasted_iota(jnp.int32, (shape[1], bucket_count), 1)
        ).astype(F32)
        gather = (
            lax.broadcasted_iota(jnp.int32, (heads, shape[0]), 1) // group
            == lax.broadcasted_iota(jnp.int32, (heads, shape[0]), 0)
        ).astype(F32)
        exact = dict(preferred_element_type=F32, precision=lax.Precision.HIGHEST)
        out_ref[...] = jnp.dot(gather, jnp.dot(kept, spread, **exact), **exact)

    vmem = pl.BlockSpec(memory_space=pltpu.VMEM)
    return pl.pallas_call(
        body,
        out_shape=jax.ShapeDtypeStruct((heads, bucket_count), F32),
        in_specs=[vmem, vmem],
        out_specs=vmem,
        scratch_shapes=[pltpu.VMEM((heads * group, bucket_count * group), F32)],
        compiler_params=PARAMS,
    )(ds, buckets)


def dense_forward(base, partials, gain, w_in, w_out):
    seq_len, model = base.shape
    hidden_width = w_in.shape[1]
    chunk = 512
    steps = hidden_width // chunk

    def body(base_ref, own_ref, got_ref, gain_ref, in_ref, out_ref, stream_ref, normed_ref, hidden_ref, slope_ref, partial_ref, acc):
        step = pl.program_id(0)

        @pl.when(step == 0)
        def _():
            rows = stream_sum(base_ref, (own_ref, got_ref))
            stream_ref[...] = rows
            normed_ref[...] = normalize(rows, gain_ref[...]).astype(BF16)
            acc[...] = jnp.zeros_like(acc)

        pre = dot_nn(normed_ref[...], in_ref[...])
        hidden = smooth_act(pre).astype(BF16)
        hidden_ref[...] = hidden
        slope_ref[...] = smooth_slope(pre).astype(BF16)
        acc[...] += dot_nt(hidden, out_ref[...])

        @pl.when(step == steps - 1)
        def _():
            partial_ref[...] = acc[...].astype(BF16)

    full = (seq_len, model)
    col = pl.BlockSpec((model, chunk), lambda i: (0, i))
    act = pl.BlockSpec((seq_len, chunk), lambda i: (0, i))
    return pl.pallas_call(
        body,
        out_shape=[
            jax.ShapeDtypeStruct(full, F32),
            jax.ShapeDtypeStruct(full, BF16),
            jax.ShapeDtypeStruct((seq_len, hidden_width), BF16),
            jax.ShapeDtypeStruct((seq_len, hidden_width), BF16),
            jax.ShapeDtypeStruct(full, BF16),
        ],
        grid=(steps,),
        in_specs=[whole(full)] * 3 + [whole((1, model)), col, col],
        out_specs=[whole(full), whole(full), act, act, whole(full)],
        scratch_shapes=[pltpu.VMEM(full, F32)],
        compiler_params=PARAMS,
    )(base, *partials, gain[None], w_in, w_out)


def norm_step(grad_ref, rows_ref, gain_ref, own_ref, got_ref):
    upstream = own_ref[...].astype(F32) + got_ref[...].astype(F32)
    rows = rows_ref[...].astype(F32)
    scale = row_scale(rows)
    scaled = upstream * gain_ref[...]
    inner = jnp.mean(scaled * rows, axis=-1, keepdims=True)
    grad_rows = scale * scaled - rows * (scale * scale * scale * inner)
    grad_gain = jnp.sum(upstream * rows * scale, axis=0, keepdims=True)
    return grad_ref[...].astype(F32) + grad_rows, grad_gain


def norm_kernel(grad, rows, gain, partials):
    full = rows.shape

    def body(_, grad_ref, rows_ref, gain_ref, own_ref, got_ref, out_ref, low_ref, gain_out):
        total, gain_out[...] = norm_step(grad_ref, rows_ref, gain_ref, own_ref, got_ref)
        out_ref[...] = total
        low_ref[...] = total.astype(BF16)

    return kernel_call(
        body,
        [(full, F32), (full, BF16), ((1, full[1]), F32)],
        place_scalars(),
        (grad, rows, gain[None]) + tuple(partials),
    )


def dense_backward(grad, rows, gain, partials, w_in, w_out, slope):
    seq_len, model = rows.shape
    hidden_width = w_in.shape[1]
    chunk = 512
    steps = hidden_width // chunk

    def body(grad_ref, rows_ref, gain_ref, own_ref, got_ref, in_ref, out_ref, slope_ref, total_ref, low_ref, dpre_ref, partial_ref, gain_out, acc):
        step = pl.program_id(0)

        @pl.when(step == 0)
        def _():
            total, gain_out[...] = norm_step(grad_ref, rows_ref, gain_ref, own_ref, got_ref)
            total_ref[...] = total
            low_ref[...] = total.astype(BF16)
            acc[...] = jnp.zeros_like(acc)

        dpre = (dot_nn(low_ref[...], out_ref[...]) * slope_ref[...].astype(F32)).astype(BF16)
        dpre_ref[...] = dpre
        acc[...] += dot_nt(dpre, in_ref[...])

        @pl.when(step == steps - 1)
        def _():
            partial_ref[...] = acc[...].astype(BF16)

    full = (seq_len, model)
    col = pl.BlockSpec((model, chunk), lambda i: (0, i))
    act = pl.BlockSpec((seq_len, chunk), lambda i: (0, i))
    return pl.pallas_call(
        body,
        out_shape=[
            jax.ShapeDtypeStruct(full, F32),
            jax.ShapeDtypeStruct(full, BF16),
            jax.ShapeDtypeStruct((seq_len, hidden_width), BF16),
            jax.ShapeDtypeStruct(full, BF16),
            jax.ShapeDtypeStruct((1, model), F32),
        ],
        grid=(steps,),
        in_specs=[whole(full)] * 2 + [whole((1, model))] + [whole(full)] * 2 + [col, col, act],
        out_specs=[whole(full), whole(full), act, whole(full), whole((1, model))],
        scratch_shapes=[pltpu.VMEM(full, F32)],
        compiler_params=PARAMS,
    )(grad, rows, gain[None], *partials, w_in, w_out, slope)


def send_slots(base, partials, gain, spots, blocks):
    seq_len, model = base.shape
    slots = spots[1] // blocks
    full = (seq_len, model)

    def body(_, base_ref, own_ref, got_ref, gain_ref, spot_ref, stream_ref, normed_ref, *outs):
        rows = stream_sum(base_ref, (own_ref, got_ref))
        stream_ref[...] = rows
        normed = normalize(rows, gain_ref[...]).astype(BF16)
        normed_ref[...] = normed
        for block in range(blocks):
            slot = lax.broadcasted_iota(jnp.int32, (slots, seq_len), 0) + block * slots
            hot = jnp.where(slot == spot_ref[...], 1.0, 0.0).astype(BF16)
            outs[block][...] = dot_nn(hot, normed).astype(BF16)

    return kernel_call(
        body,
        [(full, F32), (full, BF16)] + [((slots, model), BF16)] * blocks,
        place_scalars(),
        (base, *partials, gain[None], spots[0]),
    )


def stacked(blocks):
    rows, cols = blocks[0].shape

    def body(_, *refs):
        for number, ref in enumerate(refs[:-1]):
            refs[-1][number * rows : (number + 1) * rows, :] = ref[...]

    return kernel_call(body, [((len(blocks) * rows, cols), blocks[0].dtype)], place_scalars(), blocks)[0]


def route_softmax(rows, router):
    logits = dot_nt(rows, router)
    exp_part = jnp.exp(logits - jnp.max(logits, axis=-1, keepdims=True))
    return exp_part / jnp.sum(exp_part, axis=-1, keepdims=True)


def expert_step(rows, grads, router, w_in, w_out):
    half, model = rows[0].shape
    hidden_width = w_in.shape[1]
    chunk = 256
    steps = hidden_width // chunk
    total = 2 * half

    def body(where, own_ref, other_ref, own_grad, other_grad, router_ref, in_ref, out_ref, hidden_ref, dpre_ref, grad_ref, res_own, res_other, back_own, back_other, res_acc, back_acc, rows_ref):
        step = pl.program_id(0)

        @pl.when(step == 0)
        def _():
            rows_ref[:half, :] = own_ref[...]
            rows_ref[half:, :] = other_ref[...]
            here = lax.broadcasted_iota(jnp.int32, (1, router_ref.shape[0]), 1) == where[0]
            for side, grad in enumerate((own_grad, other_grad)):
                part = slice(side * half, (side + 1) * half)
                prob = route_softmax(rows_ref[part, :], router_ref[...])
                gate = jnp.sum(jnp.where(here, prob, 0.0), axis=-1, keepdims=True)
                grad_ref[part, :] = (gate * grad[...].astype(F32)).astype(BF16)
            res_acc[...] = jnp.zeros_like(res_acc)
            back_acc[...] = jnp.zeros_like(back_acc)

        pre = dot_nn(rows_ref[...], in_ref[...])
        hidden = smooth_act(pre).astype(BF16)
        hidden_ref[...] = hidden
        dpre = (dot_nt(grad_ref[...], out_ref[...]) * smooth_slope(pre)).astype(BF16)
        dpre_ref[...] = dpre
        res_acc[...] += dot_nn(hidden, out_ref[...])
        back_acc[...] += dot_nt(dpre, in_ref[...])

        @pl.when(step == steps - 1)
        def _():
            res_own[...] = res_acc[:half, :]
            res_other[...] = res_acc[half:, :].astype(BF16)
            back_own[...] = back_acc[:half, :]
            back_other[...] = back_acc[half:, :].astype(BF16)

    part = (half, model)
    act = pl.BlockSpec((total, chunk), lambda i: (0, i))
    return pl.pallas_call(
        body,
        out_shape=[
            jax.ShapeDtypeStruct((total, hidden_width), BF16),
            jax.ShapeDtypeStruct((total, hidden_width), BF16),
            jax.ShapeDtypeStruct((total, model), BF16),
            jax.ShapeDtypeStruct(part, F32),
            jax.ShapeDtypeStruct(part, BF16),
            jax.ShapeDtypeStruct(part, F32),
            jax.ShapeDtypeStruct(part, BF16),
        ],
        grid=(steps,),
        in_specs=[pl.BlockSpec(memory_space=pltpu.SMEM)]
        + [whole(part)] * 4
        + [
            whole(router.shape),
            pl.BlockSpec((model, chunk), lambda i: (0, i)),
            pl.BlockSpec((chunk, model), lambda i: (i, 0)),
        ],
        out_specs=[act, act, whole((total, model))] + [whole(part)] * 4,
        scratch_shapes=[pltpu.VMEM((total, model), F32)] * 2 + [pltpu.VMEM((total, model), BF16)],
        compiler_params=PARAMS,
    )(place_scalars(), *rows, *grads, router, w_in, w_out)


def expert_finish(result, back, rows, grads, router, blocks):
    half, model = rows.shape
    slots = half // blocks

    def body(where, res_own, res_got, back_own, back_got, rows_ref, grad_ref, router_ref, *outs):
        here = lax.broadcasted_iota(jnp.int32, (1, router_ref.shape[0]), 1) == where[0]
        prob = route_softmax(rows_ref[...], router_ref[...])
        gate = jnp.sum(jnp.where(here, prob, 0.0), axis=-1, keepdims=True)
        result = res_own[...] + res_got[...].astype(F32)
        grad_gate = jnp.sum(grad_ref[...].astype(F32) * result, axis=-1, keepdims=True)
        dz = (prob * (jnp.where(here, grad_gate, 0.0) - grad_gate * gate)).astype(BF16)
        total = back_own[...] + back_got[...].astype(F32) + dot_nn(dz, router_ref[...])
        for block in range(blocks):
            part = slice(block * slots, (block + 1) * slots)
            outs[block][...] = total[part, :].astype(BF16)
            outs[blocks + block][...] = result[part, :].astype(BF16)
        outs[-1][...] = dot_tn(dz, rows_ref[...])

    return kernel_call(
        body,
        [((slots, model), BF16)] * (2 * blocks) + [(router.shape, F32)],
        place_scalars(),
        (*result, *back, rows, grads, router),
    )


def expert_grads(rows, hidden, dpre, grads):
    half, model = rows[0].shape
    hidden_width = hidden.shape[1]
    chunk = 256

    def body(own_ref, other_ref, hidden_ref, dpre_ref, grad_ref, in_ref, out_ref, rows_ref):
        @pl.when(pl.program_id(0) == 0)
        def _():
            rows_ref[:half, :] = own_ref[...]
            rows_ref[half:, :] = other_ref[...]

        in_ref[...] = dot_tn(rows_ref[...], dpre_ref[...]).astype(BF16)
        out_ref[...] = dot_tn(hidden_ref[...], grad_ref[...]).astype(BF16)

    act = pl.BlockSpec((2 * half, chunk), lambda i: (0, i))
    return pl.pallas_call(
        body,
        out_shape=[
            jax.ShapeDtypeStruct((model, hidden_width), BF16),
            jax.ShapeDtypeStruct((hidden_width, model), BF16),
        ],
        grid=(hidden_width // chunk,),
        in_specs=[whole((half, model))] * 2 + [act, act, whole((2 * half, model))],
        out_specs=[
            pl.BlockSpec((model, chunk), lambda i: (0, i)),
            pl.BlockSpec((chunk, model), lambda i: (i, 0)),
        ],
        scratch_shapes=[pltpu.VMEM((2 * half, model), BF16)],
        compiler_params=PARAMS,
    )(*rows, hidden, dpre, grads)


def receive_slots(grad, rows, gain, spots, halves):
    full = rows.shape
    half = halves[0].shape[0]

    def body(_, grad_ref, rows_ref, gain_ref, spot_ref, own_ref, got_ref, out_ref, low_ref, gain_out):
        slot = lax.broadcasted_iota(jnp.int32, (full[0], half), 1)
        first = jnp.where(slot == spot_ref[...], 1.0, 0.0).astype(BF16)
        second = jnp.where(slot + half == spot_ref[...], 1.0, 0.0).astype(BF16)
        upstream = dot_nn(first, own_ref[...]) + dot_nn(second, got_ref[...])
        value = rows_ref[...]
        scale = row_scale(value)
        scaled = upstream * gain_ref[...]
        inner = jnp.mean(scaled * value, axis=-1, keepdims=True)
        total = grad_ref[...].astype(F32) + (
            scale * scaled - value * (scale * scale * scale * inner)
        )
        gain_out[...] = jnp.sum(upstream * value * scale, axis=0, keepdims=True)
        out_ref[...] = total
        low_ref[...] = total.astype(BF16)

    return kernel_call(
        body,
        [(full, F32), (full, BF16), ((1, full[1]), F32)],
        place_scalars(),
        (grad, rows, gain[None], spots) + tuple(halves),
    )


def on_device(
    tokens,
    cotangent,
    routes,
    buckets,
    norm_first,
    query_first,
    key_first,
    value_first,
    output_first,
    table_first,
    dense_gain,
    dense_in,
    dense_out,
    norm_second,
    query_second,
    key_second,
    value_second,
    output_second,
    table_second,
    expert_gain,
    router,
    expert_in,
    expert_out,
):
    mp_index = lax.axis_index("mp")
    z_index = lax.axis_index("expert")
    z_count = lax.axis_size("expert")
    tok_local, model_width = tokens.shape
    seq_len = buckets.shape[0]
    expert_count = router.shape[1]
    capacity = seq_len // 2
    slots = capacity // lax.axis_size("mp")
    bucket_count = table_first.shape[0]
    head_local = table_first.shape[1] // lax.axis_size("mp")

    width = query_first.shape[1]
    shards = (
        (
            jnp.concatenate([query_first, key_first], axis=1),
            jnp.concatenate([value_first, output_first.T], axis=1),
        ),
        (dense_in, dense_out.T),
        (
            jnp.concatenate([query_second, key_second], axis=1),
            jnp.concatenate([value_second, output_second.T], axis=1),
        ),
    )
    gathered = [gather_pair(*pair) for pair in shards]

    stream_zero = lax.all_gather(tokens, "mp", axis=0, tiled=True)
    grad_four = lax.all_gather(cotangent, "mp", axis=0, tiled=True)

    def local_bias(table):
        return build_bias(
            buckets, lax.dynamic_slice_in_dim(table, mp_index * head_local, head_local, 1).T
        )

    chosen = routes[:, 0]
    experts = jnp.arange(expert_count, dtype=jnp.int32)
    picked = chosen[:, None] == experts[None, :]
    order = jnp.arange(seq_len, dtype=jnp.int32)
    earlier = (order[None, :] < order[:, None]).astype(BF16)
    rank = jnp.sum(
        jnp.where(picked, dot_nn(earlier, picked.astype(BF16)), 0.0), axis=1
    ).astype(jnp.int32)
    distance = (chosen - z_index + z_count) % z_count
    spot = distance * slots + rank % slots
    half = z_count * slots
    in_own_half = rank // slots == mp_index
    send_spots = jnp.where(in_own_half, spot, -1)[None, :]
    back_spots = jnp.where(in_own_half, spot, spot + half)[:, None]

    def dispatch(blocks):
        own = stacked(
            [blocks[0]] + [shift(blocks[step], "expert", step) for step in range(1, z_count)]
        )
        return own, flip(own, "mp", 0)

    def give_back(blocks):
        own = stacked(
            [blocks[0]]
            + [shift(blocks[step], "expert", z_count - step) for step in range(1, z_count)]
        )
        return own, flip(own, "mp", 0)

    def swapped(partial):
        return partial, flip(partial, "mp", 0)

    weights_one = assemble(*shards[0], gathered[0])
    _, normed_one, joint_one, prob_one, mixed_one, partial = attention_forward(
        stream_zero, (), norm_first, weights_one, local_bias(table_first)
    )
    w_in_full, w_out_full = assemble(*shards[1], gathered[1])
    stream_one, normed_ff, hidden, slope, partial = dense_forward(
        stream_zero, swapped(partial), dense_gain, w_in_full, w_out_full
    )

    grad_four, partial = lax.optimization_barrier((grad_four, partial))
    to_slots = (jnp.arange(half, dtype=jnp.int32)[:, None] == send_spots).astype(BF16)
    grad_sent = dot_nn(to_slots, grad_four).astype(BF16)
    grad_slots = dispatch([grad_sent[i * slots : (i + 1) * slots] for i in range(z_count)])

    weights_two = assemble(*shards[2], gathered[2])
    stream_two, normed_two, joint_two, prob_two, mixed_two, partial = attention_forward(
        stream_one, swapped(partial), norm_second, weights_two, local_bias(table_second)
    )

    stream_three, moe_rows, *sent = send_slots(
        stream_two, swapped(partial), expert_gain, (send_spots, half), z_count
    )
    moe_slots = dispatch(sent)
    router_rows = router.T
    expert_hidden, expert_dpre, expert_rows, res_own, res_other, back_own, back_other = expert_step(
        moe_slots, grad_slots, router_rows, expert_in[0], expert_out[0]
    )
    *returns, grad_router = expert_finish(
        (res_own, flip(res_other, "mp", 0)),
        (back_own, flip(back_other, "mp", 0)),
        moe_slots[0],
        grad_slots[0],
        router_rows,
        z_count,
    )
    back_slots = give_back(returns[:z_count])
    grad_expert_in, grad_expert_out = expert_grads(
        moe_slots, expert_hidden, expert_dpre, expert_rows
    )
    expert_in_sum, expert_out_sum = lax.psum((grad_expert_in, grad_expert_out), "dp")

    grad_three, grad_low, grad_expert_gain = receive_slots(
        grad_four, stream_three, expert_gain, back_spots, back_slots
    )

    dj_two, ds_two, partial = attention_backward(grad_low, weights_two, joint_two, prob_two)

    def attention_grads(normed, dj, low, mixed):
        return reduce_pair(
            *weight_grads(
                z_count,
                [(normed, dj[:, : 2 * width])],
                [(normed, dj[:, 2 * width :]), (low, mixed)],
            )
        )

    two = attention_grads(normed_two, dj_two, grad_low, mixed_two)
    grad_two, grad_low, dpre, partial, grad_norm_second = dense_backward(
        grad_three, stream_two, norm_second, swapped(partial), w_in_full, w_out_full, slope
    )
    ff_in, ff_out = reduce_pair(
        *weight_grads(z_count, [(normed_ff, dpre)], [(grad_low, hidden)])
    )
    grad_one, grad_low, grad_dense_gain = norm_kernel(
        grad_two, stream_one, dense_gain, swapped(partial)
    )
    dj_one, ds_one, partial = attention_backward(grad_low, weights_one, joint_one, prob_one)
    one = attention_grads(normed_one, dj_one, grad_low, mixed_one)
    grad_zero, _, grad_norm_first = norm_kernel(
        grad_one, stream_zero, norm_first, swapped(partial)
    )
    first_row = mp_index * tok_local
    grad_zero = lax.dynamic_slice_in_dim(grad_zero, first_row, tok_local, 0)

    result_own, result_got = give_back(returns[z_count:])
    spots_here = lax.dynamic_slice_in_dim(back_spots, first_row, tok_local, 0)
    lanes = jnp.arange(half, dtype=jnp.int32)[None, :]
    result_rows = dot_nn((lanes == spots_here).astype(BF16), result_own) + dot_nn(
        (lanes + half == spots_here).astype(BF16), result_got
    )
    own_rows = lax.dynamic_slice_in_dim(moe_rows, first_row, tok_local, 0)
    own_picked = lax.dynamic_slice_in_dim(picked, first_row, tok_local, 0)
    own_gate = jnp.sum(
        jnp.where(own_picked, route_softmax(own_rows, router_rows), 0.0), axis=-1, keepdims=True
    )
    final_rows = (
        lax.dynamic_slice_in_dim(stream_three, first_row, tok_local, 0) + own_gate * result_rows
    )

    table_one_grad = table_grad(ds_one, buckets, bucket_count)
    table_two_grad = table_grad(ds_two, buckets, bucket_count)

    def full_table(local):
        zero = jnp.zeros((table_first.shape[1], bucket_count), F32)
        return lax.dynamic_update_slice_in_dim(zero, local, mp_index * head_local, 0)

    share = 1.0 / lax.axis_size("mp")
    parts = [
        grad_norm_first[0] * share,
        grad_dense_gain[0] * share,
        grad_norm_second[0] * share,
        grad_expert_gain[0] * share,
        grad_router.reshape(-1),
        full_table(table_one_grad).reshape(-1),
        full_table(table_two_grad).reshape(-1),
    ]
    sizes = [p.shape[0] for p in parts]
    packed = all_sum(jnp.concatenate(parts).reshape(-1, 128)).reshape(-1)
    small, start = [], 0
    for size in sizes:
        small.append(packed[start : start + size])
        start += size
    router_sum = small[4].reshape(expert_count, model_width).T
    table_one_sum = small[5].reshape(table_first.shape[1], bucket_count).T
    table_two_sum = small[6].reshape(table_first.shape[1], bucket_count).T

    return (
        final_rows,
        grad_zero,
        small[0],
        one[0][:, :width],
        one[0][:, width:],
        one[1][:, :width],
        one[1][:, width:].T,
        table_one_sum,
        small[1],
        ff_in,
        ff_out.T,
        small[2],
        two[0][:, :width],
        two[0][:, width:],
        two[1][:, :width],
        two[1][:, width:].T,
        table_two_sum,
        small[3],
        router_sum,
        expert_in_sum.astype(F32)[None],
        expert_out_sum.astype(F32)[None],
    )


def solution(mesh):
    rows = P(("dp", "expert", "mp"), None)
    cols_in, cols_out = P("expert", "mp"), P("mp", "expert")
    attention_in = (P(), cols_in, cols_in, cols_in, cols_out, P())
    dense = (P(), cols_in, cols_out)
    return jax.shard_map(
        on_device,
        mesh=mesh,
        in_specs=(rows, rows, P(("dp", "expert"), None), P())
        + attention_in
        + dense
        + attention_in
        + (P(), P(), P("expert", None, "mp"), P("expert", "mp", None)),
        out_specs=(rows, rows)
        + attention_in
        + dense
        + attention_in
        + (P(), P(), P("expert", None, "mp"), P("expert", "mp", None)),
        check_vma=False,
    )
```

```python
import functools

import jax
import jax.numpy as jnp
from jax import lax
from jax.experimental import pallas as pl
from jax.experimental.pallas import tpu as pltpu
from jax.sharding import PartitionSpec as P

EPSILON = 1e-06
BF16 = jnp.bfloat16
F32 = jnp.float32


def smooth_both(values):
    square = values * values
    tangent = jnp.tanh(0.7978845608 * values * (1.0 + 0.044715 * square))
    rest = 0.5 * (1.0 + tangent)
    slope = rest + (0.5 * 0.7978845608) * values * (1.0 - tangent * tangent) * (
        1.0 + 0.134145 * square
    )
    return values * rest, slope


def row_scale(rows):
    return lax.rsqrt(jnp.mean(rows * rows, axis=-1, keepdims=True) + EPSILON)


def normalize(rows, gain):
    return rows * row_scale(rows) * gain


def dot_nn(a, b):
    return jnp.dot(a, b, preferred_element_type=F32)


def dot_tn(a, b):
    return lax.dot_general(a, b, (((0,), (0,)), ((), ())), preferred_element_type=F32)


def dot_nt(a, b):
    return lax.dot_general(a, b, (((1,), (1,)), ((), ())), preferred_element_type=F32)


def flip(x, axis, bit):
    count = lax.axis_size(axis)
    return lax.ppermute(x, axis, [(i, i ^ (1 << bit)) for i in range(count)])


def meet(*values):
    leaves, tree = jax.tree.flatten(values)
    return jax.tree.unflatten(tree, lax.optimization_barrier(leaves))


def tie(value, *others):
    return meet(value, *others)[0]


def shift(x, axis, step):
    count = lax.axis_size(axis)
    return lax.ppermute(x, axis, [(i, (i + step) % count) for i in range(count)])


COST = pl.CostEstimate(flops=1, transcendentals=0, bytes_accessed=1)


def kernel_call(body, outs, scalars, arrays, limit=16):
    vmem = pl.BlockSpec(memory_space=pltpu.VMEM)
    return pl.pallas_call(
        body,
        out_shape=[jax.ShapeDtypeStruct(shape, dtype) for shape, dtype in outs],
        in_specs=[pl.BlockSpec(memory_space=pltpu.SMEM)] + [vmem] * len(arrays),
        out_specs=[vmem] * len(outs),
        compiler_params=pltpu.CompilerParams(vmem_limit_bytes=limit << 20),
        cost_estimate=COST,
    )(scalars, *arrays)


def place_scalars():
    return jnp.stack([lax.axis_index("expert"), lax.axis_index("dp") & 3]).astype(jnp.int32)


def plane_first(held):
    return flip(held, "dp", 0), flip(held, "dp", 1)


def plane_second(from_x, from_y):
    return flip(from_x[:, 0], "dp", 1), flip(from_y[:, 1], "dp", 0)


def quarter_of(left, right):
    rows = left.shape[0] // 4
    place = (lax.axis_index("dp") & 3) * rows
    return jnp.stack([lax.dynamic_slice_in_dim(t, place, rows, 0) for t in (left, right)])


def z_parts(piece):
    return [shift(piece, "expert", step) for step in range(1, lax.axis_size("expert"))]


def z_spread(piece):
    return jnp.stack(z_parts(piece))


def assemble(left, right, pieces):
    count = lax.axis_size("expert")
    rows, cols = left.shape
    quarter = rows // 4

    def body(where, left_ref, right_ref, own, from_x, from_y, diag_left, diag_right, *outs):
        z, place = where[0], where[1]
        for side, (shard, diag) in enumerate(((left_ref, diag_left), (right_ref, diag_right))):
            outs[side][pl.ds(pl.multiple_of(z * rows, 16), rows), :] = shard[...]
            for step in range(1, count):
                base = lax.rem(z + count - step, count) * rows
                for key, ref in ((0, own), (1, from_x), (2, from_y), (3, diag)):
                    row = pl.multiple_of(base + (place ^ key) * quarter, 16)
                    outs[side][pl.ds(row, quarter), :] = (
                        ref[step - 1] if key == 3 else ref[step - 1, side]
                    )

    full = ((count * rows, cols), left.dtype)
    return kernel_call(body, [full, full], place_scalars(), (left, right) + tuple(pieces))


def add_low(a, b):
    return (a.astype(F32) + b.astype(F32)).astype(BF16)


def first_trip(send_a, send_b):
    return flip(send_a, "dp", 0), flip(send_b, "dp", 1)


def second_trip(send_a, send_b):
    return flip(send_a, "dp", 1), flip(send_b, "dp", 0)


def reduce_second(keep_a, keep_b, got_a, got_b):
    blocks = keep_a.shape[0]

    def body(where, keep_a, keep_b, got_a, got_b, send_a, send_b, next_a, next_b):
        x, y = where[1] & 1, where[1] >> 1
        for k in range(blocks):
            send_a[k] = add_low(keep_a[k, 1 - y], got_a[k, 1 - y])
            next_a[k] = add_low(keep_a[k, y], got_a[k, y])
            send_b[k] = add_low(keep_b[k, 1 - x], got_b[k, 1 - x])
            next_b[k] = add_low(keep_b[k, x], got_b[k, x])

    parts = [((blocks,) + keep.shape[2:], BF16) for keep in (keep_a, keep_b)]
    return kernel_call(body, parts * 2, place_scalars(), (keep_a, keep_b, got_a, got_b))


def far_sum(keep_a, keep_b, got_a, got_b):
    for bit in range(2, lax.axis_size("dp").bit_length() - 1):
        keep_a, keep_b = add_low(keep_a, got_a), add_low(keep_b, got_b)
        got_a, got_b = flip(keep_a, "dp", bit), flip(keep_b, "dp", bit)
    return keep_a, keep_b, got_a, got_b


def expert_held(*parts):
    def body(where, keep_a, keep_b, got_a, got_b, held_a, held_b):
        held_a[...] = add_low(keep_a[...], got_a[...])
        held_b[...] = add_low(keep_b[...], got_b[...])

    shapes = [(part.shape, BF16) for part in parts[:2]]
    return kernel_call(body, shapes, place_scalars(), far_sum(*parts))


def plane_first_e(held, got):
    return (
        (flip(held[0], "dp", 0), flip(held[1], "dp", 1)),
        (flip(got[0], "dp", 0), flip(got[1], "dp", 1)),
    )


def expert_last(held, got, diagonal):
    def body(where, *refs):
        place = where[1]
        for side in range(2):
            own, near, far_near, far_diag = (refs[side + 2 * number] for number in range(4))
            rows, cols = own.shape[1:]
            first = 2 if side == 0 else 1
            for key, ref in ((0, own), (first, near), (3 - first, far_near), (3, far_diag)):
                if side == 0:
                    at = pl.multiple_of((place ^ key) * cols, 128)
                    refs[8][:, pl.ds(at, cols)] = ref[0].astype(F32)
                else:
                    at = pl.multiple_of((place ^ key) * rows, 16)
                    refs[9][pl.ds(at, rows), :] = ref[0].astype(F32)

    (_, model, quarter), _ = (part.shape for part in held)
    shapes = [((model, 4 * quarter), F32), ((4 * quarter, model), F32)]
    return kernel_call(body, shapes, place_scalars(), (*held, *got, *diagonal[0], *diagonal[1]))


def reduce_third(*parts):
    blocks, rows, cols = parts[0].shape

    def body(where, keep_a, keep_b, got_a, got_b, *outs):
        for step, out in enumerate(outs):
            block = lax.rem(where[0] + step, blocks)
            out[0, 0] = add_low(keep_a[block], got_a[block])
            out[0, 1] = add_low(keep_b[block], got_b[block])

    own, *sends = kernel_call(
        body, [((1, 2, rows, cols), BF16)] * blocks, place_scalars(), far_sum(*parts)
    )
    return own, sends


def z_trip(sends):
    return [shift(send, "expert", step + 1) for step, send in enumerate(sends)]


def reduce_fourth(own, got):
    total = own.astype(F32)
    for part in got:
        total = total + part.astype(F32)
    return total.astype(BF16)


def reduce_last(held, near, diagonal):
    _, _, rows, cols = held.shape

    def body(where, own, from_x, from_y, diag_a, diag_b, out_a, out_b):
        place = where[1]
        for side, (out, diag) in enumerate(((out_a, diag_a), (out_b, diag_b))):
            for key, ref in ((0, own), (1, from_x), (2, from_y), (3, diag)):
                row = pl.multiple_of((place ^ key) * rows, 8)
                value = ref[0] if key == 3 else ref[0, side]
                out[pl.ds(row, rows), :] = value.astype(F32)

    return kernel_call(
        body, [((4 * rows, cols), F32)] * 2, place_scalars(), (held, *near, *diagonal)
    )


def pack_small(gains, router, tables):
    model = gains[0].shape[1]
    heads, levels = tables[0].shape
    top = len(gains) + router.shape[0]
    share = 1.0 / lax.axis_size("mp")

    def body(core, *refs):
        out = refs[-1]
        out[...] = jnp.zeros_like(out)
        for number in range(len(gains)):
            out[number : number + 1, :] = refs[number][...] * share
        out[len(gains) : top, :] = refs[len(gains)][...]
        for layer in range(2):
            for side in range(2):

                @pl.when(core[0] == side)
                def _():
                    at = (layer * 2 + side) * 128
                    out[top : top + heads, at : at + levels] = refs[len(gains) + 1 + layer][...]

    return kernel_call(
        body,
        [((16, model), F32)],
        jnp.stack([lax.axis_index("mp")]).astype(jnp.int32),
        (*gains, router, *tables),
    )[0]


def whole(shape):
    return pl.BlockSpec(memory_space=pltpu.VMEM)


PARAMS = pltpu.CompilerParams(vmem_limit_bytes=28 << 20)


def build_bias(buckets, tables, token):
    heads = tables.shape[0]
    seq_len = buckets.shape[0]
    padded = jnp.pad(tables, ((0, 0), (0, 128 - tables.shape[1])))

    def body(bucket_ref, table_ref, _, out_ref):
        head = pl.program_id(0)
        row = jnp.broadcast_to(table_ref[pl.ds(head, 1), :], (seq_len, 128))
        for part in range(seq_len // 128):
            index = bucket_ref[:, part * 128 : (part + 1) * 128]
            out_ref[0, :, part * 128 : (part + 1) * 128] = jnp.take_along_axis(row, index, axis=1)

    return pl.pallas_call(
        body,
        out_shape=jax.ShapeDtypeStruct((heads, seq_len, seq_len), F32),
        grid=(heads,),
        in_specs=[whole((seq_len, seq_len)), whole((heads, 128)), whole(token.shape)],
        out_specs=pl.BlockSpec((1, seq_len, seq_len), lambda h: (h, 0, 0)),
        compiler_params=PARAMS,
        cost_estimate=COST,
    )(buckets, padded, token)


def lane_masks(head_width):
    lane = lax.broadcasted_iota(jnp.int32, (1, 2 * head_width), 1)
    return [lane < head_width, lane >= head_width]


def masked(value, mask):
    return jnp.where(mask, value, jnp.zeros_like(value))


def both(own, got):
    return own[...].astype(F32) + got[...].astype(F32)


def stream_sum(base, partials):
    total = base[...].astype(F32)
    if partials:
        total = total + both(*partials)
    return total


def attention_forward(base, partials, gain, weights, bias):
    seq_len, model = base.shape
    heads = bias.shape[0]
    width = weights[0].shape[1] // 2
    head_width = width // heads
    chunk = 128
    scale = head_width**-0.5
    count = len(partials)

    def body(*refs):
        base_ref, part_refs = refs[0], refs[1 : 1 + count]
        gain_ref, wa_ref, wb_ref, bias_ref = refs[1 + count : 5 + count]
        stream_ref, normed_ref, joint_ref, prob_ref, mixed_ref, partial_ref = refs[5 + count :]
        step = pl.program_id(0)

        @pl.when(step == 0)
        def _():
            rows = stream_sum(base_ref, part_refs)
            stream_ref[...] = rows
            normed = normalize(rows, gain_ref[...]).astype(BF16)
            normed_ref[...] = normed
            left = dot_nn(normed, wa_ref[...]).astype(BF16)
            joint_ref[:, :width] = left[:, :width] * jnp.asarray(scale, BF16)
            joint_ref[:, width : 2 * width] = left[:, width:]
            joint_ref[:, 2 * width :] = dot_nn(normed, wb_ref[:, :width]).astype(BF16)

        masks = lane_masks(head_width)
        rows = pl.ds(pl.multiple_of(step * chunk, chunk), chunk)
        for pair in range(heads // 2):
            cols = slice(pair * 2 * head_width, (pair + 1) * 2 * head_width)
            query = joint_ref[rows, cols]
            key = joint_ref[:, slice(width + cols.start, width + cols.stop)]
            value = joint_ref[:, slice(2 * width + cols.start, 2 * width + cols.stop)]
            mixed = None
            for side in range(2):
                head = 2 * pair + side
                scores = dot_nt(query, masked(key, masks[side])) + bias_ref[head]
                exp_part = jnp.exp(scores - jnp.max(scores, axis=-1, keepdims=True))
                share = 1.0 / jnp.sum(exp_part, axis=-1, keepdims=True)
                prob = (exp_part * share).astype(BF16)
                prob_ref[head] = prob
                out = dot_nn(prob, masked(value, masks[side]))
                mixed = out if mixed is None else mixed + out
            mixed_ref[:, cols] = mixed.astype(BF16)
        partial_ref[...] = dot_nt(mixed_ref[...], wb_ref[:, width:]).astype(BF16)

    full = (seq_len, model)
    shapes = [
        (full, F32, whole(full)),
        (full, BF16, whole(full)),
        ((seq_len, 3 * width), BF16, whole((seq_len, 3 * width))),
        ((heads, seq_len, seq_len), BF16, pl.BlockSpec((heads, chunk, seq_len), lambda i: (0, i, 0))),
        ((seq_len, width), BF16, pl.BlockSpec((chunk, width), lambda i: (i, 0))),
        (full, BF16, pl.BlockSpec((chunk, model), lambda i: (i, 0))),
    ]
    return pl.pallas_call(
        body,
        out_shape=[jax.ShapeDtypeStruct(shape, dtype) for shape, dtype, _ in shapes],
        grid=(seq_len // chunk,),
        in_specs=[whole(full)]
        + [whole(full)] * count
        + [whole((1, model)), whole(weights[0].shape), whole(weights[1].shape)]
        + [pl.BlockSpec((heads, chunk, seq_len), lambda i: (0, i, 0))],
        out_specs=[spec for _, _, spec in shapes],
        compiler_params=PARAMS,
        cost_estimate=COST,
    )(base, *partials, gain[None], *weights, bias)


def attention_backward(grad, weights, joint, prob):
    seq_len, model = grad.shape
    heads = prob.shape[0]
    width = weights[0].shape[1] // 2
    head_width = width // heads
    chunk = 128
    steps = seq_len // chunk
    scale = head_width**-0.5

    def body(grad_ref, wa_ref, wb_ref, joint_ref, prob_ref, dj_ref, ds_ref, partial_ref, dk_acc, dv_acc):
        step = pl.program_id(0)

        @pl.when(step == 0)
        def _():
            dk_acc[...] = jnp.zeros_like(dk_acc)
            dv_acc[...] = jnp.zeros_like(dv_acc)

        masks = lane_masks(head_width)
        rows = pl.ds(pl.multiple_of(step * chunk, chunk), chunk)
        grad_mixed = dot_nn(grad_ref[...], wb_ref[:, width:]).astype(BF16)
        for pair in range(heads // 2):
            cols = slice(pair * 2 * head_width, (pair + 1) * 2 * head_width)
            query = joint_ref[rows, cols]
            key = joint_ref[:, slice(width + cols.start, width + cols.stop)]
            value = joint_ref[:, slice(2 * width + cols.start, 2 * width + cols.stop)]
            go = grad_mixed[:, cols]
            dq = None
            dk = None
            dv = None
            for side in range(2):
                head = 2 * pair + side
                low = prob_ref[head]
                wide = low.astype(F32)
                grad_prob = dot_nt(go, masked(value, masks[side]))
                inner = jnp.sum(wide * grad_prob, axis=-1, keepdims=True)
                ds = (wide * (grad_prob - inner)).astype(BF16)
                ds_ref[head] = ds
                one_q = dot_nn(ds, masked(key, masks[side]))
                one_k = dot_tn(ds, masked(query, masks[side]))
                one_v = dot_tn(low, masked(go, masks[side]))
                dq = one_q if dq is None else dq + one_q
                dk = one_k if dk is None else dk + one_k
                dv = one_v if dv is None else dv + one_v
            dj_ref[rows, cols] = (dq * scale).astype(BF16)
            dk_acc[:, cols] += dk
            dv_acc[:, cols] += dv

        @pl.when(step == steps - 1)
        def _():
            dj_ref[:, width : 2 * width] = dk_acc[...].astype(BF16)
            dj_ref[:, 2 * width :] = dv_acc[...].astype(BF16)
            partial_ref[...] = (
                dot_nt(dj_ref[:, : 2 * width], wa_ref[...])
                + dot_nt(dj_ref[:, 2 * width :], wb_ref[:, :width])
            ).astype(BF16)

    full = (seq_len, model)
    rows_of = pl.BlockSpec((heads, chunk, seq_len), lambda i: (0, i, 0))
    return pl.pallas_call(
        body,
        out_shape=[
            jax.ShapeDtypeStruct((seq_len, 3 * width), BF16),
            jax.ShapeDtypeStruct(prob.shape, BF16),
            jax.ShapeDtypeStruct(full, BF16),
        ],
        grid=(steps,),
        in_specs=[
            pl.BlockSpec((chunk, model), lambda i: (i, 0)),
            whole(weights[0].shape),
            whole(weights[1].shape),
            whole(joint.shape),
            rows_of,
        ],
        out_specs=[whole((seq_len, 3 * width)), rows_of, whole(full)],
        scratch_shapes=[pltpu.VMEM((seq_len, width), F32)] * 2,
        compiler_params=PARAMS,
        cost_estimate=COST,
    )(grad, *weights, joint, prob)


def split_first(where, a, b, send_a, send_b, keep_a, keep_b, blocks):
    rows = send_a.shape[2]
    x, y = where[1] & 1, where[1] >> 1
    for k in range(blocks):
        for j in range(2):
            for i in range(2):
                at = (k * 4 + j * 2 + i) * rows
                piece_a, piece_b = a[at : at + rows], b[at : at + rows]

                @pl.when(x == i)
                def _():
                    keep_a[k, j] = piece_a

                @pl.when(x != i)
                def _():
                    send_a[k, j] = piece_a

                @pl.when(y == j)
                def _():
                    keep_b[k, i] = piece_b

                @pl.when(y != j)
                def _():
                    send_b[k, i] = piece_b


def weight_grads(blocks, lefts, rights):
    model = lefts[0][0].shape[1]
    cols = sum(stop - start for _, _, start, stop in lefts)
    rows = model // blocks // 4
    half = ((blocks, 2, rows, cols), BF16)
    flat = [t for pair in lefts + rights for t in pair[:2]]

    def body(where, *refs):
        inputs, outs = refs[: len(flat)], refs[len(flat) :]

        def side(number, pairs):
            return jnp.concatenate(
                [
                    dot_tn(
                        inputs[number + 2 * i][...], inputs[number + 2 * i + 1][:, start:stop]
                    ).astype(BF16)
                    for i, (_, _, start, stop) in enumerate(pairs)
                ],
                axis=1,
            )

        split_first(where, side(0, lefts), side(2 * len(lefts), rights), *outs, blocks)

    return kernel_call(body, [half] * 4, place_scalars(), flat)


def table_grad(ds, buckets, bucket_count):
    heads, seq_len, _ = ds.shape
    group = 8

    def body(ds_ref, bucket_ref, out_ref, acc):
        acc[...] = jnp.zeros_like(acc)

        def one(number, carry):
            rows = pl.ds(pl.multiple_of(number * group, group), group)
            index = bucket_ref[rows, :]
            hot = jnp.concatenate(
                [jnp.where(index == level, 1.0, 0.0) for level in range(bucket_count)], axis=0
            ).astype(BF16)
            right = jnp.concatenate(
                [ds_ref[head, rows, :].astype(F32) for head in range(heads)], axis=0
            ).astype(BF16)
            acc[...] += dot_nt(hot, right)
            return carry

        lax.fori_loop(0, seq_len // group, one, 0, unroll=4)
        shape = acc.shape
        same = (
            lax.broadcasted_iota(jnp.int32, shape, 0) % group
            == lax.broadcasted_iota(jnp.int32, shape, 1) % group
        )
        kept = jnp.where(same, acc[...], 0.0)
        spread = (
            lax.broadcasted_iota(jnp.int32, (bucket_count, shape[0]), 1) // group
            == lax.broadcasted_iota(jnp.int32, (bucket_count, shape[0]), 0)
        ).astype(F32)
        gather = (
            lax.broadcasted_iota(jnp.int32, (heads, shape[1]), 1) // group
            == lax.broadcasted_iota(jnp.int32, (heads, shape[1]), 0)
        ).astype(F32)
        exact = dict(preferred_element_type=F32, precision=lax.Precision.HIGHEST)
        by_level = jnp.dot(spread, kept, **exact)
        out_ref[...] = lax.dot_general(gather, by_level, (((1,), (1,)), ((), ())), **exact)

    vmem = pl.BlockSpec(memory_space=pltpu.VMEM)
    return pl.pallas_call(
        body,
        out_shape=jax.ShapeDtypeStruct((heads, bucket_count), F32),
        in_specs=[vmem, vmem],
        out_specs=vmem,
        scratch_shapes=[pltpu.VMEM((bucket_count * group, heads * group), F32)],
        compiler_params=PARAMS,
        cost_estimate=COST,
    )(ds, buckets)


def dense_forward(base, partials, gain, w_in, w_out):
    seq_len, model = base.shape
    hidden_width = w_in.shape[1]
    chunk = 512
    steps = hidden_width // chunk

    def body(base_ref, own_ref, got_ref, gain_ref, in_ref, out_ref, stream_ref, normed_ref, hidden_ref, slope_ref, partial_ref, acc):
        step = pl.program_id(0)

        @pl.when(step == 0)
        def _():
            rows = stream_sum(base_ref, (own_ref, got_ref))
            stream_ref[...] = rows
            normed_ref[...] = normalize(rows, gain_ref[...]).astype(BF16)
            acc[...] = jnp.zeros_like(acc)

        pre = dot_nn(normed_ref[...], in_ref[...])
        act, slope = smooth_both(pre)
        hidden = act.astype(BF16)
        hidden_ref[...] = hidden
        slope_ref[...] = slope.astype(BF16)
        acc[...] += dot_nt(hidden, out_ref[...])

        @pl.when(step == steps - 1)
        def _():
            partial_ref[...] = acc[...].astype(BF16)

    full = (seq_len, model)
    col = pl.BlockSpec((model, chunk), lambda i: (0, i))
    act = pl.BlockSpec((seq_len, chunk), lambda i: (0, i))
    return pl.pallas_call(
        body,
        out_shape=[
            jax.ShapeDtypeStruct(full, F32),
            jax.ShapeDtypeStruct(full, BF16),
            jax.ShapeDtypeStruct((seq_len, hidden_width), BF16),
            jax.ShapeDtypeStruct((seq_len, hidden_width), BF16),
            jax.ShapeDtypeStruct(full, BF16),
        ],
        grid=(steps,),
        in_specs=[whole(full)] * 3 + [whole((1, model)), col, col],
        out_specs=[whole(full), whole(full), act, act, whole(full)],
        scratch_shapes=[pltpu.VMEM(full, F32)],
        compiler_params=PARAMS,
        cost_estimate=COST,
    )(base, *partials, gain[None], w_in, w_out)


def norm_step(grad_ref, rows_ref, gain_ref, own_ref, got_ref):
    upstream = both(own_ref, got_ref)
    rows = rows_ref[...].astype(F32)
    scale = row_scale(rows)
    scaled = upstream * gain_ref[...]
    inner = jnp.mean(scaled * rows, axis=-1, keepdims=True)
    grad_rows = scale * scaled - rows * (scale * scale * scale * inner)
    grad_gain = jnp.sum(upstream * rows * scale, axis=0, keepdims=True)
    return grad_ref[...].astype(F32) + grad_rows, grad_gain


def norm_kernel(grad, rows, gain, partials):
    full = rows.shape

    def body(_, grad_ref, rows_ref, gain_ref, own_ref, got_ref, out_ref, low_ref, gain_out):
        total, gain_out[...] = norm_step(grad_ref, rows_ref, gain_ref, own_ref, got_ref)
        out_ref[...] = total
        low_ref[...] = total.astype(BF16)

    return kernel_call(
        body,
        [(full, F32), (full, BF16), ((1, full[1]), F32)],
        place_scalars(),
        (grad, rows, gain[None], *partials),
    )


def dense_backward(grad, rows, gain, partials, w_in, w_out, slope):
    seq_len, model = rows.shape
    hidden_width = w_in.shape[1]
    chunk = 512
    steps = hidden_width // chunk

    def body(grad_ref, rows_ref, gain_ref, own_ref, got_ref, in_ref, out_ref, slope_ref, total_ref, low_ref, dpre_ref, partial_ref, gain_out, acc):
        step = pl.program_id(0)

        @pl.when(step == 0)
        def _():
            total, gain_out[...] = norm_step(grad_ref, rows_ref, gain_ref, own_ref, got_ref)
            total_ref[...] = total
            low_ref[...] = total.astype(BF16)
            acc[...] = jnp.zeros_like(acc)

        dpre = (dot_nn(low_ref[...], out_ref[...]) * slope_ref[...].astype(F32)).astype(BF16)
        dpre_ref[...] = dpre
        acc[...] += dot_nt(dpre, in_ref[...])

        @pl.when(step == steps - 1)
        def _():
            partial_ref[...] = acc[...].astype(BF16)

    full = (seq_len, model)
    col = pl.BlockSpec((model, chunk), lambda i: (0, i))
    act = pl.BlockSpec((seq_len, chunk), lambda i: (0, i))
    return pl.pallas_call(
        body,
        out_shape=[
            jax.ShapeDtypeStruct(full, F32),
            jax.ShapeDtypeStruct(full, BF16),
            jax.ShapeDtypeStruct((seq_len, hidden_width), BF16),
            jax.ShapeDtypeStruct(full, BF16),
            jax.ShapeDtypeStruct((1, model), F32),
        ],
        grid=(steps,),
        in_specs=[whole(full)] * 2 + [whole((1, model))] + [whole(full)] * 2 + [col, col, act],
        out_specs=[whole(full), whole(full), act, whole(full), whole((1, model))],
        scratch_shapes=[pltpu.VMEM(full, F32)],
        compiler_params=PARAMS,
        cost_estimate=COST,
    )(grad, rows, gain[None], *partials, w_in, w_out, slope)


def send_slots(base, partials, gain, spots, blocks):
    seq_len, model = base.shape
    slots = spots[1] // blocks
    full = (seq_len, model)

    def body(_, base_ref, own_ref, got_ref, gain_ref, spot_ref, stream_ref, normed_ref, *outs):
        rows = stream_sum(base_ref, (own_ref, got_ref))
        stream_ref[...] = rows
        normed = normalize(rows, gain_ref[...]).astype(BF16)
        normed_ref[...] = normed
        for block in range(blocks):
            slot = lax.broadcasted_iota(jnp.int32, (slots, seq_len), 0) + block * slots
            hot = jnp.where(slot == spot_ref[...], 1.0, 0.0).astype(BF16)
            outs[block][...] = dot_nn(hot, normed).astype(BF16)

    return kernel_call(
        body,
        [(full, F32), (full, BF16)] + [((slots, model), BF16)] * blocks,
        place_scalars(),
        (base, *partials, gain[None], spots[0]),
    )


def stacked(blocks):
    rows, cols = blocks[0].shape

    def body(_, *refs):
        for number, ref in enumerate(refs[:-1]):
            refs[-1][number * rows : (number + 1) * rows, :] = ref[...]

    return kernel_call(body, [((len(blocks) * rows, cols), blocks[0].dtype)], place_scalars(), blocks)[0]


def route_softmax(rows, router):
    logits = dot_nt(rows, router)
    exp_part = jnp.exp(logits - jnp.max(logits, axis=-1, keepdims=True))
    return exp_part / jnp.sum(exp_part, axis=-1, keepdims=True)


def expert_step(rows, grads, router, w_in, w_out):
    half, model = rows[0].shape
    hidden_width = w_in.shape[1]
    chunk = 512
    steps = hidden_width // chunk
    total = 2 * half

    def body(where, own_ref, other_ref, own_grad, other_grad, router_ref, in_ref, out_ref, hidden_ref, dpre_ref, grad_ref, res_own, res_other, back_own, back_other, res_acc, back_acc, rows_ref):
        step = pl.program_id(0)

        @pl.when(step == 0)
        def _():
            rows_ref[:half, :] = own_ref[...]
            rows_ref[half:, :] = other_ref[...]
            here = lax.broadcasted_iota(jnp.int32, (1, router_ref.shape[0]), 1) == where[0]
            for side, grad in enumerate((own_grad, other_grad)):
                part = slice(side * half, (side + 1) * half)
                prob = route_softmax(rows_ref[part, :], router_ref[...])
                gate = jnp.sum(jnp.where(here, prob, 0.0), axis=-1, keepdims=True)
                grad_ref[part, :] = (gate * grad[...].astype(F32)).astype(BF16)
            res_acc[...] = jnp.zeros_like(res_acc)
            back_acc[...] = jnp.zeros_like(back_acc)

        pre = dot_nn(rows_ref[...], in_ref[...])
        act, slope = smooth_both(pre)
        hidden = act.astype(BF16)
        hidden_ref[...] = hidden
        dpre = (dot_nt(grad_ref[...], out_ref[...]) * slope).astype(BF16)
        dpre_ref[...] = dpre
        res_acc[...] += dot_nn(hidden, out_ref[...])
        back_acc[...] += dot_nt(dpre, in_ref[...])

        @pl.when(step == steps - 1)
        def _():
            res_own[...] = res_acc[:half, :]
            res_other[...] = res_acc[half:, :].astype(BF16)
            back_own[...] = back_acc[:half, :]
            back_other[...] = back_acc[half:, :].astype(BF16)

    part = (half, model)
    act = pl.BlockSpec((total, chunk), lambda i: (0, i))
    return pl.pallas_call(
        body,
        out_shape=[
            jax.ShapeDtypeStruct((total, hidden_width), BF16),
            jax.ShapeDtypeStruct((total, hidden_width), BF16),
            jax.ShapeDtypeStruct((total, model), BF16),
            jax.ShapeDtypeStruct(part, F32),
            jax.ShapeDtypeStruct(part, BF16),
            jax.ShapeDtypeStruct(part, F32),
            jax.ShapeDtypeStruct(part, BF16),
        ],
        grid=(steps,),
        in_specs=[pl.BlockSpec(memory_space=pltpu.SMEM)]
        + [whole(part)] * 4
        + [
            whole(router.shape),
            pl.BlockSpec((model, chunk), lambda i: (0, i)),
            pl.BlockSpec((chunk, model), lambda i: (i, 0)),
        ],
        out_specs=[act, act, whole((total, model))] + [whole(part)] * 4,
        scratch_shapes=[pltpu.VMEM((total, model), F32)] * 2 + [pltpu.VMEM((total, model), BF16)],
        compiler_params=PARAMS,
        cost_estimate=COST,
    )(place_scalars(), *rows, *grads, router, w_in, w_out)


def expert_finish(result, back, rows, grads, router, blocks):
    half, model = rows.shape
    slots = half // blocks

    def body(where, res_own, res_got, back_own, back_got, rows_ref, grad_ref, router_ref, *outs):
        here = lax.broadcasted_iota(jnp.int32, (1, router_ref.shape[0]), 1) == where[0]
        prob = route_softmax(rows_ref[...], router_ref[...])
        gate = jnp.sum(jnp.where(here, prob, 0.0), axis=-1, keepdims=True)
        result = res_own[...] + res_got[...].astype(F32)
        grad_gate = jnp.sum(grad_ref[...].astype(F32) * result, axis=-1, keepdims=True)
        dz = (prob * (jnp.where(here, grad_gate, 0.0) - grad_gate * gate)).astype(BF16)
        total = back_own[...] + back_got[...].astype(F32) + dot_nn(dz, router_ref[...])
        for block in range(blocks):
            part = slice(block * slots, (block + 1) * slots)
            outs[block][...] = total[part, :].astype(BF16)
            outs[blocks + block][...] = result[part, :].astype(BF16)
        outs[-1][...] = dot_tn(dz, rows_ref[...])

    return kernel_call(
        body,
        [((slots, model), BF16)] * (2 * blocks) + [(router.shape, F32)],
        place_scalars(),
        (*result, *back, rows, grads, router),
    )


def expert_grads(rows, hidden, dpre, grads):
    half, model = rows[0].shape
    hidden_width = hidden.shape[1]
    quarter = hidden_width // 4

    def body(where, own_ref, other_ref, hidden_ref, dpre_ref, grad_ref, send_a, send_b, keep_a, keep_b, rows_ref):
        @pl.when(pl.program_id(0) == 0)
        def _():
            rows_ref[:half, :] = own_ref[...]
            rows_ref[half:, :] = other_ref[...]

        step = pl.program_id(0)
        x, y = where[1] & 1, where[1] >> 1
        for first, value, keep, send in (
            ((step & 1) == x, dot_tn(rows_ref[...], dpre_ref[...]), keep_a, send_a),
            ((step >> 1) == y, dot_tn(hidden_ref[...], grad_ref[...]), keep_b, send_b),
        ):
            low = value.astype(BF16)

            @pl.when(first)
            def _():
                keep[0] = low

            @pl.when(jnp.logical_not(first))
            def _():
                send[0] = low

    def early(step):
        return jnp.minimum(step, 1)

    def late(step):
        return jnp.maximum(step - 2, 0)

    def spot_keep(step, where):
        y = where[1] >> 1
        return (1 - y) * early(step) + y * late(step), 0, 0

    def spot_send(step, where):
        y = where[1] >> 1
        return y * early(step) + (1 - y) * late(step), 0, 0

    act = pl.BlockSpec((2 * half, quarter), lambda i, w: (0, i))
    shape_a, shape_b = (model, quarter), (quarter, model)
    col = pl.BlockSpec((1,) + shape_a, lambda i, w: (i >> 1, 0, 0))
    return pl.pallas_call(
        body,
        out_shape=[jax.ShapeDtypeStruct((2,) + shape, BF16) for shape in (shape_a, shape_b)] * 2,
        grid_spec=pltpu.PrefetchScalarGridSpec(
            num_scalar_prefetch=1,
            grid=(4,),
            in_specs=[whole(None), whole(None), act, act, whole(None)],
            out_specs=[
                col,
                pl.BlockSpec((1,) + shape_b, spot_send),
                col,
                pl.BlockSpec((1,) + shape_b, spot_keep),
            ],
            scratch_shapes=[pltpu.VMEM((2 * half, model), BF16)],
        ),
        compiler_params=PARAMS,
        cost_estimate=COST,
    )(place_scalars(), *rows, hidden, dpre, grads)


def receive_slots(grad, rows, gain, spots, halves):
    full = rows.shape
    half = halves[0].shape[0]

    def body(_, grad_ref, rows_ref, gain_ref, spot_ref, own_ref, got_ref, out_ref, low_ref, gain_out):
        slot = lax.broadcasted_iota(jnp.int32, (full[0], half), 1)
        first = jnp.where(slot == spot_ref[...], 1.0, 0.0).astype(BF16)
        second = jnp.where(slot + half == spot_ref[...], 1.0, 0.0).astype(BF16)
        upstream = dot_nn(first, own_ref[...]) + dot_nn(second, got_ref[...])
        value = rows_ref[...]
        scale = row_scale(value)
        scaled = upstream * gain_ref[...]
        inner = jnp.mean(scaled * value, axis=-1, keepdims=True)
        total = grad_ref[...].astype(F32) + (
            scale * scaled - value * (scale * scale * scale * inner)
        )
        gain_out[...] = jnp.sum(upstream * value * scale, axis=0, keepdims=True)
        out_ref[...] = total
        low_ref[...] = total.astype(BF16)

    return kernel_call(
        body,
        [(full, F32), (full, BF16), ((1, full[1]), F32)],
        place_scalars(),
        (grad, rows, gain[None], spots) + tuple(halves),
    )


def on_device(
    tokens,
    cotangent,
    routes,
    buckets,
    norm_first,
    query_first,
    key_first,
    value_first,
    output_first,
    table_first,
    dense_gain,
    dense_in,
    dense_out,
    norm_second,
    query_second,
    key_second,
    value_second,
    output_second,
    table_second,
    expert_gain,
    router,
    expert_in,
    expert_out,
):
    mp_index = lax.axis_index("mp")
    z_index = lax.axis_index("expert")
    z_count = lax.axis_size("expert")
    tok_local, model_width = tokens.shape
    seq_len = buckets.shape[0]
    expert_count = router.shape[1]
    capacity = seq_len // 2
    slots = capacity // lax.axis_size("mp")
    bucket_count = table_first.shape[0]
    head_local = table_first.shape[1] // lax.axis_size("mp")

    width = query_first.shape[1]
    ff_width = dense_in.shape[1]
    shards = (
        (
            jnp.concatenate([query_first, key_first], axis=1),
            jnp.concatenate([value_first, output_first.T], axis=1),
        ),
        (dense_in, dense_out.T),
        (
            jnp.concatenate([query_second, key_second], axis=1),
            jnp.concatenate([value_second, output_second.T], axis=1),
        ),
    )
    far_one = z_spread(quarter_of(*shards[0]))

    stream_zero = lax.all_gather(tokens, "mp", axis=0, tiled=True)
    grad_four = lax.all_gather(cotangent, "mp", axis=0, tiled=True)

    def local_bias(table, token):
        return build_bias(
            buckets, lax.dynamic_slice_in_dim(table, mp_index * head_local, head_local, 1).T, token
        )

    chosen = routes[:, 0]
    experts = jnp.arange(expert_count, dtype=jnp.int32)
    picked = chosen[:, None] == experts[None, :]
    order = jnp.arange(seq_len, dtype=jnp.int32)
    earlier = (order[None, :] < order[:, None]).astype(BF16)
    rank = jnp.sum(
        jnp.where(picked, dot_nn(earlier, picked.astype(BF16)), 0.0), axis=1
    ).astype(jnp.int32)
    distance = (chosen - z_index + z_count) % z_count
    spot = distance * slots + rank % slots
    half = z_count * slots
    in_own_half = rank // slots == mp_index
    send_spots = jnp.where(in_own_half, spot, -1)[None, :]
    back_spots = jnp.where(in_own_half, spot, spot + half)[:, None]

    def sent_on(blocks):
        return [blocks[0]] + [shift(blocks[step], "expert", step) for step in range(1, z_count)]

    def with_other(own):
        return own, flip(own, "mp", 0)

    def sent_back(blocks):
        return [blocks[0]] + [
            shift(blocks[step], "expert", z_count - step) for step in range(1, z_count)
        ]

    def swapped(partial):
        return partial, flip(partial, "mp", 0)

    near_one = plane_first(far_one)
    token = flip(far_one[0, 0, :8, :128], "mp", 0)
    piece_ff, token = meet(quarter_of(*shards[1]), token)
    got_ff = z_parts(piece_ff)
    bias_one = local_bias(table_first, token)
    near_one, bias_one = meet(near_one, bias_one)
    diag_one = plane_second(*near_one)
    bias_two = local_bias(table_second, near_one[0][0, 0, :8, :128])
    diag_one, got_ff, bias_two = meet(diag_one, got_ff, bias_two)
    far_ff = jnp.stack(got_ff)
    near_ff = plane_first(far_ff)
    weights_one = assemble(*shards[0], (far_one, *near_one, *diag_one))
    _, normed_one, joint_one, prob_one, mixed_one, partial = attention_forward(
        tie(stream_zero, far_ff), (), norm_first, weights_one, bias_one
    )
    piece_two, partial = meet(quarter_of(*shards[2]), partial)
    got_two = z_parts(piece_two)
    pair, near_ff = meet(swapped(partial), near_ff)
    diag_ff = plane_second(*near_ff)
    diag_ff, pair, got_two = meet(diag_ff, pair, got_two)
    far_two = jnp.stack(got_two)
    near_two = plane_first(far_two)
    to_slots = (jnp.arange(half, dtype=jnp.int32)[:, None] == send_spots).astype(BF16)
    grad_sent = dot_nn(to_slots, tie(grad_four, pair)).astype(BF16)
    grad_got = sent_on([grad_sent[i * slots : (i + 1) * slots] for i in range(z_count)])
    w_in_full, w_out_full = assemble(*shards[1], (far_ff, *near_ff, *diag_ff))
    stream_one, normed_ff, hidden, slope, partial = dense_forward(
        stream_zero, pair, dense_gain, w_in_full, tie(w_out_full, grad_sent)
    )
    near_two, partial = meet(near_two, partial)
    diag_two = plane_second(*near_two)
    pair, diag_two = meet(swapped(partial), diag_two)
    weights_two = assemble(*shards[2], (far_two, *near_two, *diag_two))
    stream_two, normed_two, joint_two, prob_two, mixed_two, partial = attention_forward(
        stream_one, pair, norm_second, weights_two, bias_two
    )

    partial, grad_got = meet(partial, grad_got)

    stream_three, moe_rows, *sent = send_slots(
        stream_two, swapped(partial), expert_gain, (send_spots, half), z_count
    )
    moe_got = sent_on(sent)
    grad_slots = with_other(stacked(tie(grad_got, sent)))
    moe_slots = with_other(stacked(tie(moe_got, grad_slots)))
    router_rows = router.T
    expert_hidden, expert_dpre, expert_rows, res_own, res_other, back_own, back_other = expert_step(
        moe_slots, grad_slots, router_rows, expert_in[0], expert_out[0]
    )
    halves_e = expert_grads(moe_slots, expert_hidden, expert_dpre, expert_rows)
    res_got, back_got, halves_e = meet(
        flip(res_other, "mp", 0), flip(back_other, "mp", 0), halves_e
    )
    got_e = first_trip(*halves_e[:2])
    keep_e = [part[None] for part in halves_e[2:]]
    *returns, grad_router = expert_finish(
        (res_own, res_got),
        (back_own, back_got),
        moe_slots[0],
        grad_slots[0],
        router_rows,
        z_count,
    )
    back_slots = with_other(stacked(sent_back(returns[:z_count])))
    grad_three, grad_low, grad_expert_gain = receive_slots(
        grad_four, stream_three, expert_gain, back_spots, back_slots
    )
    grad_low, got_e = meet(grad_low, got_e)
    send_ea, send_eb, *keep_e = reduce_second(*keep_e, got_e[0][None], got_e[1][None])
    send_ea, send_eb, grad_low, *result_blocks = meet(send_ea, send_eb, grad_low, *returns[z_count:])
    got_e = second_trip(send_ea, send_eb)
    result_got = sent_back(result_blocks)

    def attention_grads(normed, dj, low, mixed):
        return weight_grads(
            z_count,
            [(normed, dj, 0, 2 * width)],
            [(normed, dj, 2 * width, 3 * width), (low, mixed, 0, width)],
        )

    dj_two, ds_two, partial = attention_backward(grad_low, weights_two, joint_two, prob_two)
    result_got, partial, dj_two, got_e = meet(result_got, partial, dj_two, got_e)
    pair = swapped(partial)
    held_e = expert_held(*keep_e, *got_e)
    held_e, dj_two = meet(held_e, dj_two)
    from_e = (flip(held_e[0], "dp", 1), flip(held_e[1], "dp", 0))
    halves_two = attention_grads(normed_two, dj_two, grad_low, mixed_two)
    pair, halves_two = meet(pair, halves_two)
    got_two = first_trip(*halves_two[:2])
    grad_two, grad_low, dpre, partial, grad_norm_second = dense_backward(
        grad_three, stream_two, norm_second, pair, w_in_full, w_out_full, slope
    )
    from_e, partial, dpre = meet(from_e, partial, dpre)
    pair = swapped(partial)
    halves_ff = weight_grads(
        z_count, [(normed_ff, dpre, 0, ff_width)], [(grad_low, hidden, 0, ff_width)]
    )
    pair, halves_ff, got_two = meet(pair, halves_ff, got_two)
    got_ff = first_trip(*halves_ff[:2])
    *send_two, keep_a, keep_b = reduce_second(*halves_two[2:], *got_two)
    keep_two = (keep_a, keep_b)
    send_two, pair = meet(send_two, pair)
    got_two = second_trip(*send_two)
    grad_one, grad_low, grad_dense_gain = norm_kernel(grad_two, stream_one, dense_gain, pair)
    dj_one, ds_one, partial = attention_backward(grad_low, weights_one, joint_one, prob_one)
    pair = swapped(partial)
    halves_one = attention_grads(normed_one, dj_one, grad_low, mixed_one)
    pair, halves_one, got_two = meet(pair, halves_one, got_two)
    own_two, send_two = reduce_third(*keep_two, *got_two)
    send_two, halves_one = meet(send_two, halves_one)
    got_one = first_trip(*halves_one[:2])
    grad_zero, _, grad_norm_first = norm_kernel(grad_one, stream_zero, norm_first, pair)
    grad_norm_first, got_ff, send_two = meet(grad_norm_first, got_ff, send_two)
    got_two = z_trip(send_two)
    *send_ff, keep_a, keep_b = reduce_second(*halves_ff[2:], *got_ff)
    keep_ff = (keep_a, keep_b)
    send_ff, ds_two, got_one = meet(send_ff, ds_two, got_one)
    got_ff = second_trip(*send_ff)
    *send_one, keep_a, keep_b = reduce_second(*halves_one[2:], *got_one)
    keep_one = (keep_a, keep_b)
    table_two_grad = table_grad(ds_two, buckets, bucket_count)
    table_two_grad, got_ff, got_two, send_one = meet(table_two_grad, got_ff, got_two, send_one)
    got_one = second_trip(*send_one)
    own_ff, send_ff = reduce_third(*keep_ff, *got_ff)
    send_ff, ds_one = meet(send_ff, ds_one)
    got_ff = z_trip(send_ff)
    held_two = reduce_fourth(own_two, got_two)
    table_one_grad = table_grad(ds_one, buckets, bucket_count)
    small = pack_small(
        (grad_norm_first, grad_dense_gain, grad_norm_second, grad_expert_gain),
        grad_router,
        (table_one_grad, table_two_grad),
    )
    small, got_one, held_two = meet(small, got_one, held_two)
    own_one, send_one = reduce_third(*keep_one, *got_one)
    near_e = plane_first_e(held_e, from_e)
    got_small = flip(small, "mp", 0)
    send_one, got_small, got_ff = meet(send_one, got_small, got_ff)
    small = small + got_small
    got_one = z_trip(send_one)
    held_ff = reduce_fourth(own_ff, got_ff)
    held_ff, near_e = meet(held_ff, near_e)
    near_ff = plane_first(held_ff)
    got_small = flip(small, "dp", 0)
    expert_in_sum, expert_out_sum = expert_last(held_e, from_e, near_e)
    near_ff, got_small, got_one, expert_in_sum = meet(near_ff, got_small, got_one, expert_in_sum)
    small = small + got_small
    held_one = reduce_fourth(own_one, got_one)
    diag_ff = plane_second(*near_ff)
    got_small = flip(small, "dp", 1)
    diag_ff, got_small, held_one = meet(diag_ff, got_small, held_one)
    small = small + got_small
    for bit in range(2, lax.axis_size("dp").bit_length() - 1):
        small = small + flip(small, "dp", bit)
    near_two, near_one = plane_first(held_two), plane_first(held_one)
    got_small = flip(small, "expert", 0)
    ff_in, ff_out = reduce_last(held_ff, near_ff, diag_ff)
    near_two, near_one, got_small, ff_in = meet(near_two, near_one, got_small, ff_in)
    small = small + got_small
    diag_two, diag_one = plane_second(*near_two), plane_second(*near_one)
    small = small + flip(small, "expert", 1)
    two = reduce_last(held_two, near_two, diag_two)
    one = reduce_last(held_one, near_one, diag_one)
    first_row = mp_index * tok_local
    grad_zero = lax.dynamic_slice_in_dim(grad_zero, first_row, tok_local, 0)
    result_own = stacked(result_got)

    result_got = flip(result_own, "mp", 0)
    spots_here = lax.dynamic_slice_in_dim(back_spots, first_row, tok_local, 0)
    lanes = jnp.arange(half, dtype=jnp.int32)[None, :]
    result_rows = dot_nn((lanes == spots_here).astype(BF16), result_own) + dot_nn(
        (lanes + half == spots_here).astype(BF16), result_got
    )
    own_rows = lax.dynamic_slice_in_dim(moe_rows, first_row, tok_local, 0)
    own_picked = lax.dynamic_slice_in_dim(picked, first_row, tok_local, 0)
    own_gate = jnp.sum(
        jnp.where(own_picked, route_softmax(own_rows, router_rows), 0.0), axis=-1, keepdims=True
    )
    final_rows = (
        lax.dynamic_slice_in_dim(stream_three, first_row, tok_local, 0) + own_gate * result_rows
    )

    router_sum = small[4 : 4 + expert_count].T
    base = 4 + expert_count
    table_one_sum, table_two_sum = (
        jnp.concatenate(
            [
                small[base : base + head_local, at * 128 : at * 128 + bucket_count]
                for at in (layer * 2, layer * 2 + 1)
            ],
            axis=0,
        ).T
        for layer in range(2)
    )

    return (
        final_rows,
        grad_zero,
        small[0],
        one[0][:, :width],
        one[0][:, width:],
        one[1][:, :width],
        one[1][:, width:].T,
        table_one_sum,
        small[1],
        ff_in,
        ff_out.T,
        small[2],
        two[0][:, :width],
        two[0][:, width:],
        two[1][:, :width],
        two[1][:, width:].T,
        table_two_sum,
        small[3],
        router_sum,
        expert_in_sum[None],
        expert_out_sum[None],
    )


def solution(mesh):
    rows = P(("dp", "expert", "mp"), None)
    cols_in, cols_out = P("expert", "mp"), P("mp", "expert")
    attention_in = (P(), cols_in, cols_in, cols_in, cols_out, P())
    dense = (P(), cols_in, cols_out)
    return jax.shard_map(
        on_device,
        mesh=mesh,
        in_specs=(rows, rows, P(("dp", "expert"), None), P())
        + attention_in
        + dense
        + attention_in
        + (P(), P(), P("expert", None, "mp"), P("expert", "mp", None)),
        out_specs=(rows, rows)
        + attention_in
        + dense
        + attention_in
        + (P(), P(), P("expert", None, "mp"), P("expert", "mp", None)),
        check_vma=False,
    )
```

```python
import functools

import jax
import jax.numpy as jnp
from jax import lax
from jax.experimental import pallas as pl
from jax.experimental.pallas import tpu as pltpu
from jax.sharding import PartitionSpec as P

EPSILON = 1e-06
BF16 = jnp.bfloat16
F32 = jnp.float32


def smooth_both(values):
    square = values * values
    tangent = jnp.tanh(0.7978845608 * values * (1.0 + 0.044715 * square))
    rest = 0.5 * (1.0 + tangent)
    slope = rest + (0.5 * 0.7978845608) * values * (1.0 - tangent * tangent) * (
        1.0 + 0.134145 * square
    )
    return values * rest, slope


def row_scale(rows):
    return lax.rsqrt(jnp.mean(rows * rows, axis=-1, keepdims=True) + EPSILON)


def normalize(rows, gain):
    return rows * row_scale(rows) * gain


def dot_nn(a, b):
    return jnp.dot(a, b, preferred_element_type=F32)


def dot_tn(a, b):
    return lax.dot_general(a, b, (((0,), (0,)), ((), ())), preferred_element_type=F32)


def dot_nt(a, b):
    return lax.dot_general(a, b, (((1,), (1,)), ((), ())), preferred_element_type=F32)


def flip(x, axis, bit):
    count = lax.axis_size(axis)
    return lax.ppermute(x, axis, [(i, i ^ (1 << bit)) for i in range(count)])


def meet(*values):
    leaves, tree = jax.tree.flatten(values)
    return jax.tree.unflatten(tree, lax.optimization_barrier(leaves))


def tie(value, *others):
    return meet(value, *others)[0]


def shift(x, axis, step):
    count = lax.axis_size(axis)
    return lax.ppermute(x, axis, [(i, (i + step) % count) for i in range(count)])


COST = pl.CostEstimate(flops=1, transcendentals=0, bytes_accessed=1)


def kernel_call(body, outs, scalars, arrays, limit=16):
    vmem = pl.BlockSpec(memory_space=pltpu.VMEM)
    return pl.pallas_call(
        body,
        out_shape=[jax.ShapeDtypeStruct(shape, dtype) for shape, dtype in outs],
        in_specs=[pl.BlockSpec(memory_space=pltpu.SMEM)] + [vmem] * len(arrays),
        out_specs=[vmem] * len(outs),
        compiler_params=pltpu.CompilerParams(vmem_limit_bytes=limit << 20),
        cost_estimate=COST,
    )(scalars, *arrays)


def place_scalars():
    return jnp.stack([lax.axis_index("expert"), lax.axis_index("dp") & 3]).astype(jnp.int32)


def plane_first(held):
    return flip(held, "dp", 0), flip(held, "dp", 1)


def plane_second(from_x, from_y):
    return flip(from_x[0], "dp", 1), flip(from_y[1], "dp", 0)


def quarter_of(left, right):
    rows = left.shape[0] // 4
    place = (lax.axis_index("dp") & 3) * rows
    return jnp.stack([lax.dynamic_slice_in_dim(t, place, rows, 0) for t in (left, right)])


def z_parts(piece):
    return [shift(piece, "expert", step) for step in range(1, lax.axis_size("expert"))]


def z_spread(piece):
    return jnp.stack(z_parts(piece), axis=1)


def assemble(left, right, pieces):
    count = lax.axis_size("expert")
    rows, cols = left.shape
    quarter = rows // 4

    def body(where, left_ref, right_ref, own, from_x, from_y, diag_left, diag_right, *outs):
        z, place = where[0], where[1]
        for side, (shard, diag) in enumerate(((left_ref, diag_left), (right_ref, diag_right))):
            outs[side][pl.ds(pl.multiple_of(z * rows, 16), rows), :] = shard[...]
            for step in range(1, count):
                base = lax.rem(z + count - step, count) * rows
                for key, ref in ((0, own), (1, from_x), (2, from_y), (3, diag)):
                    row = pl.multiple_of(base + (place ^ key) * quarter, 16)
                    outs[side][pl.ds(row, quarter), :] = (
                        ref[step - 1] if key == 3 else ref[side, step - 1]
                    )

    full = ((count * rows, cols), left.dtype)
    return kernel_call(body, [full, full], place_scalars(), (left, right) + tuple(pieces))


def add_low(a, b):
    return (a.astype(F32) + b.astype(F32)).astype(BF16)


def first_trip(send_a, send_b):
    return flip(send_a, "dp", 0), flip(send_b, "dp", 1)


def second_trip(send_a, send_b):
    return flip(send_a, "dp", 1), flip(send_b, "dp", 0)


def reduce_second(keep_a, keep_b, got_a, got_b):
    blocks = keep_a.shape[0]

    def body(where, keep_a, keep_b, got_a, got_b, send_a, send_b, next_a, next_b):
        x, y = where[1] & 1, where[1] >> 1
        for k in range(blocks):
            send_a[k] = add_low(keep_a[k, 1 - y], got_a[k, 1 - y])
            next_a[k] = add_low(keep_a[k, y], got_a[k, y])
            send_b[k] = add_low(keep_b[k, 1 - x], got_b[k, 1 - x])
            next_b[k] = add_low(keep_b[k, x], got_b[k, x])

    parts = [((blocks,) + keep.shape[2:], BF16) for keep in (keep_a, keep_b)]
    return kernel_call(body, parts * 2, place_scalars(), (keep_a, keep_b, got_a, got_b))


def far_sum(keep_a, keep_b, got_a, got_b):
    for bit in range(2, lax.axis_size("dp").bit_length() - 1):
        keep_a, keep_b = add_low(keep_a, got_a), add_low(keep_b, got_b)
        got_a, got_b = flip(keep_a, "dp", bit), flip(keep_b, "dp", bit)
    return keep_a, keep_b, got_a, got_b


def expert_held(*parts):
    def body(where, keep_a, keep_b, got_a, got_b, held_a, held_b):
        held_a[...] = add_low(keep_a[...], got_a[...])
        held_b[...] = add_low(keep_b[...], got_b[...])

    shapes = [(part.shape, BF16) for part in parts[:2]]
    return kernel_call(body, shapes, place_scalars(), far_sum(*parts))


def last_trip_e(held, got):
    both_a, both_b = (jnp.concatenate(pair, axis=0) for pair in zip(held, got))
    return flip(both_a, "dp", 0), flip(both_b, "dp", 1)


def expert_last(held, got, far):
    def body(where, *refs):
        place = where[1]
        for side in range(2):
            own, near, both = (refs[side + 2 * number] for number in range(3))
            rows, cols = own.shape[1:]
            first = 2 if side == 0 else 1
            for key, value in (
                (0, own[0]),
                (first, near[0]),
                (3 - first, both[0]),
                (3, both[1]),
            ):
                if side == 0:
                    at = pl.multiple_of((place ^ key) * cols, 128)
                    refs[6][:, pl.ds(at, cols)] = value.astype(F32)
                else:
                    at = pl.multiple_of((place ^ key) * rows, 16)
                    refs[7][pl.ds(at, rows), :] = value.astype(F32)

    (_, model, quarter), _ = (part.shape for part in held)
    shapes = [((model, 4 * quarter), F32), ((4 * quarter, model), F32)]
    return kernel_call(body, shapes, place_scalars(), (*held, *got, *far))


def reduce_third(*parts):
    blocks, rows, cols = parts[0].shape

    def body(where, keep_a, keep_b, got_a, got_b, *outs):
        for step, out in enumerate(outs):
            block = lax.rem(where[0] + step, blocks)
            out[0] = add_low(keep_a[block], got_a[block])
            out[1] = add_low(keep_b[block], got_b[block])

    own, *sends = kernel_call(
        body, [((2, rows, cols), BF16)] * blocks, place_scalars(), far_sum(*parts)
    )
    return own, sends


def reduce_halves(*parts):
    blocks, rows, cols = parts[0].shape
    half = blocks // 2

    def body(where, keep_a, keep_b, got_a, got_b, send, keep):
        upper = where[0] // half
        for k in range(half):
            for out, base in ((send, (1 - upper) * half), (keep, upper * half)):
                out[k, 0] = add_low(keep_a[base + k], got_a[base + k])
                out[k, 1] = add_low(keep_b[base + k], got_b[base + k])

    return kernel_call(
        body, [((half, 2, rows, cols), BF16)] * 2, place_scalars(), far_sum(*parts)
    )


def reduce_last_half(keep, got):
    half = keep.shape[0]

    def body(where, keep, got, send, own):
        odd = lax.rem(where[0], half)
        send[...] = add_low(keep[1 - odd], got[1 - odd])
        own[...] = add_low(keep[odd], got[odd])

    return kernel_call(
        body, [(keep.shape[1:], BF16)] * 2, place_scalars(), (keep, got)
    )


def z_trip(sends):
    return [shift(send, "expert", step + 1) for step, send in enumerate(sends)]


def reduce_fourth(own, got):
    total = own.astype(F32)
    for part in got:
        total = total + part.astype(F32)
    return total.astype(BF16)


def reduce_last(held, near, diagonal, widths):
    _, rows, _ = held.shape

    def body(where, own, from_x, from_y, diag_a, diag_b, *outs):
        place = where[1]
        start = 0
        for number, width in enumerate(widths):
            cols = slice(start, start + width)
            for side, diag in enumerate((diag_a, diag_b)):
                out = outs[2 * number + side]
                for key, ref in ((0, own), (1, from_x), (2, from_y), (3, diag)):
                    row = pl.multiple_of((place ^ key) * rows, 8)
                    value = ref[:, cols] if key == 3 else ref[side, :, cols]
                    out[pl.ds(row, rows), :] = value.astype(F32)
            start += width

    shapes = [((4 * rows, width), F32) for width in widths for _ in range(2)]
    outs = kernel_call(body, shapes, place_scalars(), (held, *near, *diagonal))
    return [outs[2 * i : 2 * i + 2] for i in range(len(widths))]


def pack_small(gains, router, tables):
    model = gains[0].shape[1]
    heads, levels = tables[0].shape
    top = len(gains) + router.shape[0]
    share = 1.0 / lax.axis_size("mp")

    def body(core, *refs):
        out = refs[-1]
        out[...] = jnp.zeros_like(out)
        for number in range(len(gains)):
            out[number : number + 1, :] = refs[number][...] * share
        out[len(gains) : top, :] = refs[len(gains)][...]
        for layer in range(2):
            for side in range(2):

                @pl.when(core[0] == side)
                def _():
                    at = (layer * 2 + side) * 128
                    out[top : top + heads, at : at + levels] = refs[len(gains) + 1 + layer][...]

    return kernel_call(
        body,
        [((16, model), F32)],
        jnp.stack([lax.axis_index("mp")]).astype(jnp.int32),
        (*gains, router, *tables),
    )[0]


def whole(shape):
    return pl.BlockSpec(memory_space=pltpu.VMEM)


PARAMS = pltpu.CompilerParams(vmem_limit_bytes=16 << 20)
MIDDLE = pltpu.CompilerParams(vmem_limit_bytes=20 << 20)
LARGE = pltpu.CompilerParams(vmem_limit_bytes=30 << 20)


def build_bias(buckets, tables, token):
    heads = tables.shape[0]
    seq_len = buckets.shape[0]
    padded = jnp.pad(tables, ((0, 0), (0, 128 - tables.shape[1])))

    def body(bucket_ref, table_ref, _, out_ref):
        head = pl.program_id(0)
        row = jnp.broadcast_to(table_ref[pl.ds(head, 1), :], (seq_len, 128))
        for part in range(seq_len // 128):
            index = bucket_ref[:, part * 128 : (part + 1) * 128]
            out_ref[0, :, part * 128 : (part + 1) * 128] = jnp.take_along_axis(row, index, axis=1)

    return pl.pallas_call(
        body,
        out_shape=jax.ShapeDtypeStruct((heads, seq_len, seq_len), F32),
        grid=(heads,),
        in_specs=[whole((seq_len, seq_len)), whole((heads, 128)), whole(token.shape)],
        out_specs=pl.BlockSpec((1, seq_len, seq_len), lambda h: (h, 0, 0)),
        compiler_params=PARAMS,
        cost_estimate=COST,
    )(buckets, padded, token)


def lane_masks(head_width):
    lane = lax.broadcasted_iota(jnp.int32, (1, 2 * head_width), 1)
    return [lane < head_width, lane >= head_width]


def masked(value, mask):
    return jnp.where(mask, value, jnp.zeros_like(value))


def both(first, second):
    if len(first.shape) == 2:
        return first[...].astype(F32) + second[...].astype(F32)
    return jnp.concatenate(
        [part[0].astype(F32) + part[1].astype(F32) for part in (first, second)], axis=0
    )


def stream_sum(base, partials):
    total = base[...].astype(F32)
    if partials:
        total = total + both(*partials)
    return total


def attention_forward(base, partials, gain, weights, bias):
    seq_len, model = base.shape
    heads = bias.shape[0]
    width = weights[0].shape[1] // 2
    head_width = width // heads
    chunk = 128
    scale = head_width**-0.5
    count = len(partials)

    def body(*refs):
        base_ref, part_refs = refs[0], refs[1 : 1 + count]
        gain_ref, wa_ref, wb_ref, bias_ref = refs[1 + count : 5 + count]
        stream_out, normed_out, joint_out, prob_ref, mixed_ref, partial_ref = refs[5 + count : -3]
        stream_ref, normed_ref, joint_ref = refs[-3:]
        step = pl.program_id(0)

        @pl.when(step == 0)
        def _():
            rows = stream_sum(base_ref, part_refs)
            stream_ref[...] = rows
            normed = normalize(rows, gain_ref[...]).astype(BF16)
            normed_ref[...] = normed
            left = dot_nn(normed, wa_ref[...]).astype(BF16)
            joint_ref[:, :width] = left[:, :width] * jnp.asarray(scale, BF16)
            joint_ref[:, width : 2 * width] = left[:, width:]
            joint_ref[:, 2 * width :] = dot_nn(normed, wb_ref[:, :width]).astype(BF16)

        masks = lane_masks(head_width)
        rows = pl.ds(pl.multiple_of(step * chunk, chunk), chunk)
        stream_out[...] = stream_ref[rows, :]
        normed_out[...] = normed_ref[rows, :]
        joint_out[...] = joint_ref[rows, :]
        for pair in range(heads // 2):
            cols = slice(pair * 2 * head_width, (pair + 1) * 2 * head_width)
            query = joint_ref[rows, cols]
            key = joint_ref[:, slice(width + cols.start, width + cols.stop)]
            value = joint_ref[:, slice(2 * width + cols.start, 2 * width + cols.stop)]
            mixed = None
            for side in range(2):
                head = 2 * pair + side
                scores = dot_nt(query, masked(key, masks[side])) + bias_ref[head]
                exp_part = jnp.exp(scores - jnp.max(scores, axis=-1, keepdims=True))
                share = 1.0 / jnp.sum(exp_part, axis=-1, keepdims=True)
                prob = (exp_part * share).astype(BF16)
                prob_ref[head] = prob
                out = dot_nn(prob, masked(value, masks[side]))
                mixed = out if mixed is None else mixed + out
            mixed_ref[:, cols] = mixed.astype(BF16)
        partial_ref[...] = dot_nt(mixed_ref[...], wb_ref[:, width:]).astype(BF16)

    full = (seq_len, model)
    def by_rows(cols):
        return pl.BlockSpec((chunk, cols), lambda i: (i, 0))

    heads_of = pl.BlockSpec((heads, chunk, seq_len), lambda i: (0, i, 0))
    kept = [
        (full, F32, by_rows(model)),
        (full, BF16, by_rows(model)),
        ((seq_len, 3 * width), BF16, by_rows(3 * width)),
        ((heads, seq_len, seq_len), BF16, heads_of),
        ((seq_len, width), BF16, by_rows(width)),
    ]
    return pl.pallas_call(
        body,
        out_shape=[pltpu.HBM(shape, dtype) for shape, dtype, _ in kept]
        + [jax.ShapeDtypeStruct(full, BF16)],
        grid=(seq_len // chunk,),
        in_specs=[whole(full)]
        + [whole(full)] * count
        + [whole((1, model)), whole(weights[0].shape), whole(weights[1].shape)]
        + [heads_of],
        out_specs=[spec for _, _, spec in kept] + [by_rows(model)],
        scratch_shapes=[
            pltpu.VMEM(full, F32),
            pltpu.VMEM(full, BF16),
            pltpu.VMEM((seq_len, 3 * width), BF16),
        ],
        compiler_params=PARAMS,
        cost_estimate=COST,
    )(base, *partials, gain[None], *weights, bias)


def attention_backward(grad, weights, joint, prob):
    seq_len, model = grad.shape
    heads = prob.shape[0]
    width = weights[0].shape[1] // 2
    head_width = width // heads
    chunk = 128
    steps = seq_len // chunk
    scale = head_width**-0.5

    def body(grad_ref, wa_ref, wb_ref, joint_ref, prob_ref, dj_ref, ds_ref, partial_ref, dk_acc, dv_acc):
        step = pl.program_id(0)

        @pl.when(step == 0)
        def _():
            dk_acc[...] = jnp.zeros_like(dk_acc)
            dv_acc[...] = jnp.zeros_like(dv_acc)

        masks = lane_masks(head_width)
        rows = pl.ds(pl.multiple_of(step * chunk, chunk), chunk)
        grad_mixed = dot_nn(grad_ref[...], wb_ref[:, width:]).astype(BF16)
        for pair in range(heads // 2):
            cols = slice(pair * 2 * head_width, (pair + 1) * 2 * head_width)
            query = joint_ref[rows, cols]
            key = joint_ref[:, slice(width + cols.start, width + cols.stop)]
            value = joint_ref[:, slice(2 * width + cols.start, 2 * width + cols.stop)]
            go = grad_mixed[:, cols]
            dq = None
            dk = None
            dv = None
            for side in range(2):
                head = 2 * pair + side
                low = prob_ref[head]
                wide = low.astype(F32)
                grad_prob = dot_nt(go, masked(value, masks[side]))
                inner = jnp.sum(wide * grad_prob, axis=-1, keepdims=True)
                ds = (wide * (grad_prob - inner)).astype(BF16)
                ds_ref[head] = ds
                one_q = dot_nn(ds, masked(key, masks[side]))
                one_k = dot_tn(ds, masked(query, masks[side]))
                one_v = dot_tn(low, masked(go, masks[side]))
                dq = one_q if dq is None else dq + one_q
                dk = one_k if dk is None else dk + one_k
                dv = one_v if dv is None else dv + one_v
            dj_ref[rows, cols] = (dq * scale).astype(BF16)
            dk_acc[:, cols] += dk
            dv_acc[:, cols] += dv

        @pl.when(step == steps - 1)
        def _():
            dj_ref[:, width : 2 * width] = dk_acc[...].astype(BF16)
            dj_ref[:, 2 * width :] = dv_acc[...].astype(BF16)
            partial_ref[...] = (
                dot_nt(dj_ref[:, : 2 * width], wa_ref[...])
                + dot_nt(dj_ref[:, 2 * width :], wb_ref[:, :width])
            ).astype(BF16)

    full = (seq_len, model)
    rows_of = pl.BlockSpec((heads, chunk, seq_len), lambda i: (0, i, 0))
    return pl.pallas_call(
        body,
        out_shape=[
            jax.ShapeDtypeStruct((seq_len, 3 * width), BF16),
            pltpu.HBM(prob.shape, BF16),
            jax.ShapeDtypeStruct(full, BF16),
        ],
        grid=(steps,),
        in_specs=[
            pl.BlockSpec((chunk, model), lambda i: (i, 0)),
            whole(weights[0].shape),
            whole(weights[1].shape),
            whole(joint.shape),
            rows_of,
        ],
        out_specs=[whole((seq_len, 3 * width)), rows_of, whole(full)],
        scratch_shapes=[pltpu.VMEM((seq_len, width), F32)] * 2,
        compiler_params=PARAMS,
        cost_estimate=COST,
    )(grad, *weights, joint, prob)


def split_first(where, a, b, send_a, send_b, keep_a, keep_b, blocks):
    rows = send_a.shape[2]
    x, y = where[1] & 1, where[1] >> 1
    for k in range(blocks):
        for j in range(2):
            for i in range(2):
                at = (k * 4 + j * 2 + i) * rows
                piece_a, piece_b = a[at : at + rows], b[at : at + rows]

                @pl.when(x == i)
                def _():
                    keep_a[k, j] = piece_a

                @pl.when(x != i)
                def _():
                    send_a[k, j] = piece_a

                @pl.when(y == j)
                def _():
                    keep_b[k, i] = piece_b

                @pl.when(y != j)
                def _():
                    send_b[k, i] = piece_b


def weight_grads(blocks, lefts, rights):
    model = lefts[0][0].shape[1]
    cols = sum(stop - start for _, _, start, stop in lefts)
    rows = model // blocks // 4
    half = ((blocks, 2, rows, cols), BF16)
    flat = [t for pair in lefts + rights for t in pair[:2]]

    def body(where, *refs):
        inputs, outs = refs[: len(flat)], refs[len(flat) :]

        def side(number, pairs):
            return jnp.concatenate(
                [
                    dot_tn(
                        inputs[number + 2 * i][...], inputs[number + 2 * i + 1][:, start:stop]
                    ).astype(BF16)
                    for i, (_, _, start, stop) in enumerate(pairs)
                ],
                axis=1,
            )

        split_first(where, side(0, lefts), side(2 * len(lefts), rights), *outs, blocks)

    return kernel_call(body, [half] * 4, place_scalars(), flat)


def table_grad(ds, buckets, bucket_count):
    heads, seq_len, _ = ds.shape
    group = 8

    def body(ds_ref, bucket_ref, out_ref, acc):
        acc[...] = jnp.zeros_like(acc)

        def one(number, carry):
            rows = pl.ds(pl.multiple_of(number * group, group), group)
            index = bucket_ref[rows, :]
            hot = jnp.concatenate(
                [jnp.where(index == level, 1.0, 0.0) for level in range(bucket_count)], axis=0
            ).astype(BF16)
            right = jnp.concatenate(
                [ds_ref[head, rows, :].astype(F32) for head in range(heads)], axis=0
            ).astype(BF16)
            acc[...] += dot_nt(hot, right)
            return carry

        lax.fori_loop(0, seq_len // group, one, 0, unroll=4)
        shape = acc.shape
        same = (
            lax.broadcasted_iota(jnp.int32, shape, 0) % group
            == lax.broadcasted_iota(jnp.int32, shape, 1) % group
        )
        kept = jnp.where(same, acc[...], 0.0)
        spread = (
            lax.broadcasted_iota(jnp.int32, (bucket_count, shape[0]), 1) // group
            == lax.broadcasted_iota(jnp.int32, (bucket_count, shape[0]), 0)
        ).astype(F32)
        gather = (
            lax.broadcasted_iota(jnp.int32, (heads, shape[1]), 1) // group
            == lax.broadcasted_iota(jnp.int32, (heads, shape[1]), 0)
        ).astype(F32)
        exact = dict(preferred_element_type=F32, precision=lax.Precision.HIGHEST)
        by_level = jnp.dot(spread, kept, **exact)
        out_ref[...] = lax.dot_general(gather, by_level, (((1,), (1,)), ((), ())), **exact)

    vmem = pl.BlockSpec(memory_space=pltpu.VMEM)
    return pl.pallas_call(
        body,
        out_shape=jax.ShapeDtypeStruct((heads, bucket_count), F32),
        in_specs=[vmem, vmem],
        out_specs=vmem,
        scratch_shapes=[pltpu.VMEM((bucket_count * group, heads * group), F32)],
        compiler_params=PARAMS,
        cost_estimate=COST,
    )(ds, buckets)


def dense_forward(base, partials, gain, w_in, w_out):
    seq_len, model = base.shape
    hidden_width = w_in.shape[1]
    chunk = 512
    steps = hidden_width // chunk

    def body(base_ref, own_ref, got_ref, gain_ref, in_ref, out_ref, stream_ref, normed_ref, hidden_ref, slope_ref, partial_ref, acc):
        step = pl.program_id(0)

        @pl.when(step == 0)
        def _():
            rows = stream_sum(base_ref, (own_ref, got_ref))
            stream_ref[...] = rows
            normed_ref[...] = normalize(rows, gain_ref[...]).astype(BF16)
            acc[...] = jnp.zeros_like(acc)

        pre = dot_nn(normed_ref[...], in_ref[...])
        act, slope = smooth_both(pre)
        hidden = act.astype(BF16)
        hidden_ref[...] = hidden
        slope_ref[...] = slope.astype(BF16)
        acc[...] += dot_nt(hidden, out_ref[...])

        @pl.when(step == steps - 1)
        def _():
            partial_ref[...] = acc[...].astype(BF16)

    full = (seq_len, model)
    col = pl.BlockSpec((model, chunk), lambda i: (0, i))
    act = pl.BlockSpec((seq_len, chunk), lambda i: (0, i))
    return pl.pallas_call(
        body,
        out_shape=[
            jax.ShapeDtypeStruct(full, F32),
            jax.ShapeDtypeStruct(full, BF16),
            pltpu.HBM((seq_len, hidden_width), BF16),
            pltpu.HBM((seq_len, hidden_width), BF16),
            jax.ShapeDtypeStruct(full, BF16),
        ],
        grid=(steps,),
        in_specs=[whole(full)] * 3 + [whole((1, model)), col, col],
        out_specs=[whole(full), whole(full), act, act, whole(full)],
        scratch_shapes=[pltpu.VMEM(full, F32)],
        compiler_params=PARAMS,
        cost_estimate=COST,
    )(base, *partials, gain[None], w_in, w_out)


def norm_step(grad_ref, rows_ref, gain_ref, own_ref, got_ref):
    upstream = both(own_ref, got_ref)
    rows = rows_ref[...].astype(F32)
    scale = row_scale(rows)
    scaled = upstream * gain_ref[...]
    inner = jnp.mean(scaled * rows, axis=-1, keepdims=True)
    grad_rows = scale * scaled - rows * (scale * scale * scale * inner)
    grad_gain = jnp.sum(upstream * rows * scale, axis=0, keepdims=True)
    return grad_ref[...].astype(F32) + grad_rows, grad_gain


def norm_kernel(grad, rows, gain, partials):
    full = rows.shape

    def body(_, grad_ref, rows_ref, gain_ref, own_ref, got_ref, out_ref, low_ref, gain_out):
        total, gain_out[...] = norm_step(grad_ref, rows_ref, gain_ref, own_ref, got_ref)
        out_ref[...] = total
        low_ref[...] = total.astype(BF16)

    return kernel_call(
        body,
        [(full, F32), (full, BF16), ((1, full[1]), F32)],
        place_scalars(),
        (grad, rows, gain[None], *partials),
    )


def dense_backward(grad, rows, gain, partials, w_in, w_out, slope):
    seq_len, model = rows.shape
    hidden_width = w_in.shape[1]
    chunk = 512
    steps = hidden_width // chunk

    def body(grad_ref, rows_ref, gain_ref, own_ref, got_ref, in_ref, out_ref, slope_ref, total_ref, low_ref, dpre_ref, partial_ref, gain_out, acc):
        step = pl.program_id(0)

        @pl.when(step == 0)
        def _():
            total, gain_out[...] = norm_step(grad_ref, rows_ref, gain_ref, own_ref, got_ref)
            total_ref[...] = total
            low_ref[...] = total.astype(BF16)
            acc[...] = jnp.zeros_like(acc)

        dpre = (dot_nn(low_ref[...], out_ref[...]) * slope_ref[...].astype(F32)).astype(BF16)
        dpre_ref[...] = dpre
        acc[...] += dot_nt(dpre, in_ref[...])

        @pl.when(step == steps - 1)
        def _():
            partial_ref[...] = acc[...].astype(BF16)

    full = (seq_len, model)
    col = pl.BlockSpec((model, chunk), lambda i: (0, i))
    act = pl.BlockSpec((seq_len, chunk), lambda i: (0, i))
    return pl.pallas_call(
        body,
        out_shape=[
            jax.ShapeDtypeStruct(full, F32),
            jax.ShapeDtypeStruct(full, BF16),
            jax.ShapeDtypeStruct((seq_len, hidden_width), BF16),
            jax.ShapeDtypeStruct(full, BF16),
            jax.ShapeDtypeStruct((1, model), F32),
        ],
        grid=(steps,),
        in_specs=[whole(full)] * 2 + [whole((1, model))] + [whole(full)] * 2 + [col, col, act],
        out_specs=[whole(full), whole(full), act, whole(full), whole((1, model))],
        scratch_shapes=[pltpu.VMEM(full, F32)],
        compiler_params=PARAMS,
        cost_estimate=COST,
    )(grad, rows, gain[None], *partials, w_in, w_out, slope)


def send_slots(base, partials, gain, spots, blocks):
    seq_len, model = base.shape
    slots = spots[1] // blocks
    full = (seq_len, model)

    def body(_, base_ref, own_ref, got_ref, gain_ref, spot_ref, stream_ref, normed_ref, *outs):
        rows = stream_sum(base_ref, (own_ref, got_ref))
        stream_ref[...] = rows
        normed = normalize(rows, gain_ref[...]).astype(BF16)
        normed_ref[...] = normed
        for block in range(blocks):
            slot = lax.broadcasted_iota(jnp.int32, (slots, seq_len), 0) + block * slots
            hot = jnp.where(slot == spot_ref[...], 1.0, 0.0).astype(BF16)
            outs[block][...] = dot_nn(hot, normed).astype(BF16)

    return kernel_call(
        body,
        [(full, F32), (full, BF16)] + [((slots, model), BF16)] * blocks,
        place_scalars(),
        (base, *partials, gain[None], spots[0]),
    )


def stacked(blocks):
    rows, cols = blocks[0].shape

    def body(_, *refs):
        for number, ref in enumerate(refs[:-1]):
            refs[-1][number * rows : (number + 1) * rows, :] = ref[...]

    return kernel_call(body, [((len(blocks) * rows, cols), blocks[0].dtype)], place_scalars(), blocks)[0]


def route_softmax(rows, router):
    logits = dot_nt(rows, router)
    exp_part = jnp.exp(logits - jnp.max(logits, axis=-1, keepdims=True))
    return exp_part / jnp.sum(exp_part, axis=-1, keepdims=True)


def expert_step(rows, grads, router, w_in, w_out):
    half, model = rows[0].shape
    hidden_width = w_in.shape[1]
    chunk = 512
    steps = hidden_width // chunk
    total = 2 * half

    def body(where, own_ref, other_ref, own_grad, other_grad, router_ref, in_ref, out_ref, hidden_ref, dpre_ref, grad_ref, res_own, res_other, back_own, back_other, res_acc, back_acc, rows_ref):
        step = pl.program_id(0)

        @pl.when(step == 0)
        def _():
            rows_ref[:half, :] = own_ref[...]
            rows_ref[half:, :] = other_ref[...]
            here = lax.broadcasted_iota(jnp.int32, (1, router_ref.shape[0]), 1) == where[0]
            for side, grad in enumerate((own_grad, other_grad)):
                part = slice(side * half, (side + 1) * half)
                prob = route_softmax(rows_ref[part, :], router_ref[...])
                gate = jnp.sum(jnp.where(here, prob, 0.0), axis=-1, keepdims=True)
                grad_ref[part, :] = (gate * grad[...].astype(F32)).astype(BF16)
            res_acc[...] = jnp.zeros_like(res_acc)
            back_acc[...] = jnp.zeros_like(back_acc)

        pre = dot_nn(rows_ref[...], in_ref[...])
        act, slope = smooth_both(pre)
        hidden = act.astype(BF16)
        hidden_ref[...] = hidden
        dpre = (dot_nt(grad_ref[...], out_ref[...]) * slope).astype(BF16)
        dpre_ref[...] = dpre
        res_acc[...] += dot_nn(hidden, out_ref[...])
        back_acc[...] += dot_nt(dpre, in_ref[...])

        @pl.when(step == steps - 1)
        def _():
            res_own[...] = res_acc[:half, :]
            res_other[...] = res_acc[half:, :].astype(BF16)
            back_own[...] = back_acc[:half, :]
            back_other[...] = back_acc[half:, :].astype(BF16)

    part = (half, model)
    act = pl.BlockSpec((total, chunk), lambda i: (0, i))
    return pl.pallas_call(
        body,
        out_shape=[
            pltpu.HBM((total, hidden_width), BF16),
            pltpu.HBM((total, hidden_width), BF16),
            jax.ShapeDtypeStruct((total, model), BF16),
            jax.ShapeDtypeStruct(part, F32),
            jax.ShapeDtypeStruct(part, BF16),
            jax.ShapeDtypeStruct(part, F32),
            jax.ShapeDtypeStruct(part, BF16),
        ],
        grid=(steps,),
        in_specs=[pl.BlockSpec(memory_space=pltpu.SMEM)]
        + [whole(part)] * 4
        + [
            whole(router.shape),
            pl.BlockSpec((model, chunk), lambda i: (0, i)),
            pl.BlockSpec((chunk, model), lambda i: (i, 0)),
        ],
        out_specs=[act, act, whole((total, model))] + [whole(part)] * 4,
        scratch_shapes=[pltpu.VMEM((total, model), F32)] * 2 + [pltpu.VMEM((total, model), BF16)],
        compiler_params=LARGE,
        cost_estimate=COST,
    )(place_scalars(), *rows, *grads, router, w_in, w_out)


def expert_finish(result, back, rows, grads, router, blocks):
    half, model = rows.shape
    slots = half // blocks

    def body(where, res_own, res_got, back_own, back_got, rows_ref, grad_ref, router_ref, *outs):
        here = lax.broadcasted_iota(jnp.int32, (1, router_ref.shape[0]), 1) == where[0]
        prob = route_softmax(rows_ref[...], router_ref[...])
        gate = jnp.sum(jnp.where(here, prob, 0.0), axis=-1, keepdims=True)
        result = res_own[...] + res_got[...].astype(F32)
        grad_gate = jnp.sum(grad_ref[...].astype(F32) * result, axis=-1, keepdims=True)
        dz = (prob * (jnp.where(here, grad_gate, 0.0) - grad_gate * gate)).astype(BF16)
        total = back_own[...] + back_got[...].astype(F32) + dot_nn(dz, router_ref[...])
        for block in range(blocks):
            part = slice(block * slots, (block + 1) * slots)
            outs[block][...] = total[part, :].astype(BF16)
            outs[blocks + block][...] = result[part, :].astype(BF16)
        outs[-1][...] = dot_tn(dz, rows_ref[...])

    return kernel_call(
        body,
        [((slots, model), BF16)] * (2 * blocks) + [(router.shape, F32)],
        place_scalars(),
        (*result, *back, rows, grads, router),
    )


def expert_grads(rows, hidden, dpre, grads):
    half, model = rows[0].shape
    hidden_width = hidden.shape[1]
    quarter = hidden_width // 4

    def body(where, own_ref, other_ref, hidden_ref, dpre_ref, grad_ref, send_a, send_b, keep_a, keep_b, rows_ref):
        @pl.when(pl.program_id(0) == 0)
        def _():
            rows_ref[:half, :] = own_ref[...]
            rows_ref[half:, :] = other_ref[...]

        step = pl.program_id(0)
        x, y = where[1] & 1, where[1] >> 1
        for first, value, keep, send in (
            ((step & 1) == x, dot_tn(rows_ref[...], dpre_ref[...]), keep_a, send_a),
            ((step >> 1) == y, dot_tn(hidden_ref[...], grad_ref[...]), keep_b, send_b),
        ):
            low = value.astype(BF16)

            @pl.when(first)
            def _():
                keep[0] = low

            @pl.when(jnp.logical_not(first))
            def _():
                send[0] = low

    def early(step):
        return jnp.minimum(step, 1)

    def late(step):
        return jnp.maximum(step - 2, 0)

    def spot_keep(step, where):
        y = where[1] >> 1
        return (1 - y) * early(step) + y * late(step), 0, 0

    def spot_send(step, where):
        y = where[1] >> 1
        return y * early(step) + (1 - y) * late(step), 0, 0

    act = pl.BlockSpec((2 * half, quarter), lambda i, w: (0, i))
    shape_a, shape_b = (model, quarter), (quarter, model)
    col = pl.BlockSpec((1,) + shape_a, lambda i, w: (i >> 1, 0, 0))
    return pl.pallas_call(
        body,
        out_shape=[jax.ShapeDtypeStruct((2,) + shape, BF16) for shape in (shape_a, shape_b)] * 2,
        grid_spec=pltpu.PrefetchScalarGridSpec(
            num_scalar_prefetch=1,
            grid=(4,),
            in_specs=[whole(None), whole(None), act, act, whole(None)],
            out_specs=[
                col,
                pl.BlockSpec((1,) + shape_b, spot_send),
                col,
                pl.BlockSpec((1,) + shape_b, spot_keep),
            ],
            scratch_shapes=[pltpu.VMEM((2 * half, model), BF16)],
        ),
        compiler_params=MIDDLE,
        cost_estimate=COST,
    )(
        place_scalars(),
        *rows,
        pltpu.with_memory_space_constraint(hidden, pltpu.HBM),
        pltpu.with_memory_space_constraint(dpre, pltpu.HBM),
        grads,
    )


def receive_slots(grad, rows, gain, spots, halves):
    full = rows.shape
    half = halves[0].shape[0]

    def body(_, grad_ref, rows_ref, gain_ref, spot_ref, own_ref, got_ref, out_ref, low_ref, gain_out):
        slot = lax.broadcasted_iota(jnp.int32, (full[0], half), 1)
        first = jnp.where(slot == spot_ref[...], 1.0, 0.0).astype(BF16)
        second = jnp.where(slot + half == spot_ref[...], 1.0, 0.0).astype(BF16)
        upstream = dot_nn(first, own_ref[...]) + dot_nn(second, got_ref[...])
        value = rows_ref[...]
        scale = row_scale(value)
        scaled = upstream * gain_ref[...]
        inner = jnp.mean(scaled * value, axis=-1, keepdims=True)
        total = grad_ref[...].astype(F32) + (
            scale * scaled - value * (scale * scale * scale * inner)
        )
        gain_out[...] = jnp.sum(upstream * value * scale, axis=0, keepdims=True)
        out_ref[...] = total
        low_ref[...] = total.astype(BF16)

    return kernel_call(
        body,
        [(full, F32), (full, BF16), ((1, full[1]), F32)],
        place_scalars(),
        (grad, rows, gain[None], spots) + tuple(halves),
    )


def on_device(
    tokens,
    cotangent,
    routes,
    buckets,
    norm_first,
    query_first,
    key_first,
    value_first,
    output_first,
    table_first,
    dense_gain,
    dense_in,
    dense_out,
    norm_second,
    query_second,
    key_second,
    value_second,
    output_second,
    table_second,
    expert_gain,
    router,
    expert_in,
    expert_out,
):
    mp_index = lax.axis_index("mp")
    z_index = lax.axis_index("expert")
    z_count = lax.axis_size("expert")
    tok_local, model_width = tokens.shape
    seq_len = buckets.shape[0]
    expert_count = router.shape[1]
    capacity = seq_len // 2
    slots = capacity // lax.axis_size("mp")
    bucket_count = table_first.shape[0]
    head_local = table_first.shape[1] // lax.axis_size("mp")

    width = query_first.shape[1]
    ff_width = dense_in.shape[1]
    shards = (
        (
            jnp.concatenate([query_first, key_first], axis=1),
            jnp.concatenate([value_first, output_first.T], axis=1),
        ),
        (dense_in, dense_out.T),
        (
            jnp.concatenate([query_second, key_second], axis=1),
            jnp.concatenate([value_second, output_second.T], axis=1),
        ),
    )
    far_one = z_spread(quarter_of(*shards[0]))

    def local_bias(table, token):
        return build_bias(
            buckets, lax.dynamic_slice_in_dim(table, mp_index * head_local, head_local, 1).T, token
        )

    chosen = routes[:, 0]
    experts = jnp.arange(expert_count, dtype=jnp.int32)
    picked = chosen[:, None] == experts[None, :]
    order = jnp.arange(seq_len, dtype=jnp.int32)
    earlier = (order[None, :] < order[:, None]).astype(BF16)
    rank = jnp.sum(
        jnp.where(picked, dot_nn(earlier, picked.astype(BF16)), 0.0), axis=1
    ).astype(jnp.int32)
    distance = (chosen - z_index + z_count) % z_count
    spot = distance * slots + rank % slots
    half = z_count * slots
    in_own_half = rank // slots == mp_index
    send_spots = jnp.where(in_own_half, spot, -1)[None, :]
    back_spots = jnp.where(in_own_half, spot, spot + half)[:, None]

    def sent_on(blocks):
        return [blocks[0]] + [shift(blocks[step], "expert", step) for step in range(1, z_count)]

    def with_other(own):
        return own, flip(own, "mp", 0)

    def sent_back(blocks):
        return [blocks[0]] + [
            shift(blocks[step], "expert", z_count - step) for step in range(1, z_count)
        ]

    def swapped(partial):
        return partial, flip(partial, "mp", 0)

    def gathered(partial):
        rows = partial.shape[0] // 2
        return tuple(
            lax.all_gather(part, "mp", axis=0) for part in (partial[:rows], partial[rows:])
        )

    piece_ff, far_one = meet(quarter_of(*shards[1]), far_one)
    near_one = plane_first(far_one)
    got_ff = z_parts(piece_ff)
    bias_one = local_bias(table_first, far_one[0, 0, :8, :128])
    tokens, cotangent, near_one, bias_one = meet(tokens, cotangent, near_one, bias_one)
    diag_one = plane_second(*near_one)
    stream_zero = lax.all_gather(tokens, "mp", axis=0, tiled=True)
    grad_four = lax.all_gather(cotangent, "mp", axis=0, tiled=True)
    bias_two = local_bias(table_second, near_one[0][0, 0, :8, :128])
    diag_one, got_ff, bias_two, stream_zero, grad_four, send_spots, back_spots = meet(
        diag_one, got_ff, bias_two, stream_zero, grad_four, send_spots, back_spots
    )
    piece_two, far_ff = meet(quarter_of(*shards[2]), jnp.stack(got_ff, axis=1))
    near_ff = plane_first(far_ff)
    got_two = z_parts(piece_two)
    weights_one = assemble(*shards[0], (far_one, *near_one, *diag_one))
    _, normed_one, joint_one, prob_one, mixed_one, partial = attention_forward(
        tie(stream_zero, far_ff), (), norm_first, weights_one, bias_one
    )
    partial, near_ff, got_two = meet(partial, near_ff, got_two)
    diag_ff = plane_second(*near_ff)
    far_two = jnp.stack(got_two, axis=1)
    diag_ff, pair, far_two = meet(diag_ff, swapped(partial), far_two)
    near_two = plane_first(far_two)
    to_slots = (jnp.arange(half, dtype=jnp.int32)[:, None] == send_spots).astype(BF16)
    grad_sent = dot_nn(to_slots, tie(grad_four, pair)).astype(BF16)
    grad_got = sent_on([grad_sent[i * slots : (i + 1) * slots] for i in range(z_count)])
    w_in_full, w_out_full = assemble(*shards[1], (far_ff, *near_ff, *diag_ff))
    stream_one, normed_ff, hidden, slope, partial = dense_forward(
        stream_zero, pair, dense_gain, w_in_full, tie(w_out_full, grad_sent)
    )
    near_two, partial = meet(near_two, partial)
    diag_two = plane_second(*near_two)
    diag_two, pair = meet(diag_two, swapped(partial))
    weights_two = assemble(*shards[2], (far_two, *near_two, *diag_two))
    stream_two, normed_two, joint_two, prob_two, mixed_two, partial = attention_forward(
        stream_one, pair, norm_second, weights_two, bias_two
    )

    partial, grad_got = meet(partial, grad_got)

    grad_slots, pair = meet(with_other(stacked(grad_got)), swapped(partial))
    stream_three, moe_rows, *sent = send_slots(
        stream_two, pair, expert_gain, (send_spots, half), z_count
    )
    moe_slots = with_other(stacked(sent_on(sent)))
    router_rows = router.T
    expert_hidden, expert_dpre, expert_rows, res_own, res_other, back_own, back_other = expert_step(
        moe_slots, grad_slots, router_rows, expert_in[0], expert_out[0]
    )
    halves_e = expert_grads(moe_slots, expert_hidden, expert_dpre, expert_rows)
    res_got, back_got, halves_e = meet(
        flip(res_other, "mp", 0), flip(back_other, "mp", 0), halves_e
    )
    got_e = first_trip(*halves_e[:2])
    keep_e = [part[None] for part in halves_e[2:]]
    *returns, grad_router = expert_finish(
        (res_own, res_got),
        (back_own, back_got),
        moe_slots[0],
        grad_slots[0],
        router_rows,
        z_count,
    )
    back_slots = with_other(stacked(sent_back(returns[:z_count])))
    grad_three, grad_low, grad_expert_gain = receive_slots(
        grad_four, stream_three, expert_gain, back_spots, back_slots
    )
    grad_low, got_e = meet(grad_low, got_e)
    send_ea, send_eb, *keep_e = reduce_second(*keep_e, got_e[0][None], got_e[1][None])
    send_ea, send_eb, grad_low = meet(send_ea, send_eb, grad_low)
    got_e = second_trip(send_ea, send_eb)

    def attention_grads(kernel, normed, dj, low, mixed):
        return kernel(
            z_count,
            [(normed, dj, 0, 2 * width)],
            [(normed, dj, 2 * width, 3 * width), (low, mixed, 0, width)],
        )

    dj_two, ds_two, partial = attention_backward(grad_low, weights_two, joint_two, prob_two)
    partial, dj_two, got_e = meet(partial, dj_two, got_e)
    held_e = expert_held(*keep_e, *got_e)
    held_e, dj_two, partial = meet(held_e, dj_two, partial)
    from_e = (flip(held_e[0], "dp", 1), flip(held_e[1], "dp", 0))
    halves_two = attention_grads(weight_grads, normed_two, dj_two, grad_low, mixed_two)
    halves_two, partial = meet(halves_two, partial)
    got_two = first_trip(*halves_two[:2])
    grad_two, grad_low, dpre, partial, grad_norm_second = dense_backward(
        grad_three, stream_two, norm_second, gathered(partial), w_in_full, w_out_full, slope
    )
    halves_ff = weight_grads(
        z_count, [(normed_ff, dpre, 0, ff_width)], [(grad_low, hidden, 0, ff_width)]
    )
    from_e, halves_ff, partial, got_two, *result_blocks = meet(
        from_e, halves_ff, partial, got_two, *returns[z_count:]
    )
    got_ff = first_trip(*halves_ff[:2])
    result_got = sent_back(result_blocks)
    *send_two, keep_a, keep_b = reduce_second(*halves_two[2:], *got_two)
    keep_two = (keep_a, keep_b)
    grad_one, grad_low, grad_dense_gain = norm_kernel(
        grad_two, stream_one, dense_gain, gathered(tie(partial, send_two))
    )
    dj_one, ds_one, partial = attention_backward(grad_low, weights_one, joint_one, prob_one)
    dj_one, partial, result_got, send_two = meet(dj_one, partial, result_got, send_two)
    got_two = second_trip(*send_two)
    result_own = stacked(result_got)
    halves_one = attention_grads(weight_grads, normed_one, dj_one, grad_low, mixed_one)
    halves_one, partial = meet(halves_one, partial)
    grad_zero, _, grad_norm_first = norm_kernel(
        grad_one, stream_zero, norm_first, gathered(partial)
    )
    grad_norm_first, halves_one, got_two = meet(grad_norm_first, halves_one, got_two)
    own_two, send_two = reduce_third(*keep_two, *got_two)
    send_two, got_ff, halves_one = meet(send_two, got_ff, halves_one)
    got_two = z_trip(send_two)
    *send_ff, keep_a, keep_b = reduce_second(*halves_ff[2:], *got_ff)
    keep_ff = (keep_a, keep_b)
    send_ff, ds_two = meet(send_ff, ds_two)
    got_ff = second_trip(*send_ff)
    table_two_grad = table_grad(ds_two, buckets, bucket_count)
    table_two_grad, got_ff, got_two, halves_one = meet(table_two_grad, got_ff, got_two, halves_one)
    send_ff, keep_ff = reduce_halves(*keep_ff, *got_ff)
    send_ff, halves_one, ds_one, held_e, from_e = meet(send_ff, halves_one, ds_one, held_e, from_e)
    got_ff = flip(send_ff, "expert", 1)
    got_one = first_trip(*halves_one[:2])
    far_e = last_trip_e(held_e, from_e)
    table_one_grad = table_grad(ds_one, buckets, bucket_count)
    table_one_grad, got_one, got_two = meet(table_one_grad, got_one, got_two)
    *send_one, keep_a, keep_b = reduce_second(*halves_one[2:], *got_one)
    got_one = second_trip(*send_one)
    held_two = reduce_fourth(own_two, got_two)
    small = pack_small(
        (grad_norm_first, grad_dense_gain, grad_norm_second, grad_expert_gain),
        grad_router,
        (table_one_grad, table_two_grad),
    )
    held_two, got_ff, small = meet(held_two, got_ff, small)
    send_ff, keep_ff = reduce_last_half(keep_ff, got_ff)
    got_ff = flip(send_ff, "expert", 0)
    send_ff, got_one = meet(send_ff, got_one)
    send_one, keep_one = reduce_halves(keep_a, keep_b, *got_one)
    send_one, got_ff, held_two, small, far_e = meet(send_one, got_ff, held_two, small, far_e)
    held = jnp.concatenate([add_low(keep_ff, got_ff), held_two], axis=-1)
    near = plane_first(held)
    got_one = flip(send_one, "expert", 1)
    got_small = flip(small, "mp", 0)
    expert_in_sum, expert_out_sum = expert_last(held_e, from_e, far_e)
    small, got_small, near, got_one, expert_in_sum = meet(
        small, got_small, near, got_one, expert_in_sum
    )
    small = small + got_small
    diagonal = plane_second(*near)
    send_one, keep_one = reduce_last_half(keep_one, got_one)
    got_one = flip(send_one, "expert", 0)
    got_small = flip(small, "expert", 1)
    diagonal, got_one, small, got_small = meet(diagonal, got_one, small, got_small)
    small = small + got_small
    held_one = add_low(keep_one, got_one)
    near_one = plane_first(held_one)
    got_small = flip(small, "expert", 0)
    (ff_in, ff_out), two = reduce_last(held, near, diagonal, (ff_width, 2 * width))
    near_one, ff_in, small, got_small, result_own = meet(
        near_one, ff_in, small, got_small, result_own
    )
    small = small + got_small
    diag_one = plane_second(*near_one)
    for bit in range(lax.axis_size("dp").bit_length() - 1):
        small = small + flip(small, "dp", bit)
    (one,) = reduce_last(held_one, near_one, diag_one, (2 * width,))
    first_row = mp_index * tok_local
    grad_zero = lax.dynamic_slice_in_dim(grad_zero, first_row, tok_local, 0)

    result_got = flip(result_own, "mp", 0)
    spots_here = lax.dynamic_slice_in_dim(back_spots, first_row, tok_local, 0)
    lanes = jnp.arange(half, dtype=jnp.int32)[None, :]
    result_rows = dot_nn((lanes == spots_here).astype(BF16), result_own) + dot_nn(
        (lanes + half == spots_here).astype(BF16), result_got
    )
    own_rows = lax.dynamic_slice_in_dim(moe_rows, first_row, tok_local, 0)
    own_picked = lax.dynamic_slice_in_dim(picked, first_row, tok_local, 0)
    own_gate = jnp.sum(
        jnp.where(own_picked, route_softmax(own_rows, router_rows), 0.0), axis=-1, keepdims=True
    )
    final_rows = (
        lax.dynamic_slice_in_dim(stream_three, first_row, tok_local, 0) + own_gate * result_rows
    )

    router_sum = small[4 : 4 + expert_count].T
    base = 4 + expert_count
    table_one_sum, table_two_sum = (
        jnp.concatenate(
            [
                small[base : base + head_local, at * 128 : at * 128 + bucket_count]
                for at in (layer * 2, layer * 2 + 1)
            ],
            axis=0,
        ).T
        for layer in range(2)
    )

    return (
        final_rows,
        grad_zero,
        small[0],
        one[0][:, :width],
        one[0][:, width:],
        one[1][:, :width],
        one[1][:, width:].T,
        table_one_sum,
        small[1],
        ff_in,
        ff_out.T,
        small[2],
        two[0][:, :width],
        two[0][:, width:],
        two[1][:, :width],
        two[1][:, width:].T,
        table_two_sum,
        small[3],
        router_sum,
        expert_in_sum[None],
        expert_out_sum[None],
    )


def solution(mesh):
    rows = P(("dp", "expert", "mp"), None)
    cols_in, cols_out = P("expert", "mp"), P("mp", "expert")
    attention_in = (P(), cols_in, cols_in, cols_in, cols_out, P())
    dense = (P(), cols_in, cols_out)
    return jax.shard_map(
        on_device,
        mesh=mesh,
        in_specs=(rows, rows, P(("dp", "expert"), None), P())
        + attention_in
        + dense
        + attention_in
        + (P(), P(), P("expert", None, "mp"), P("expert", "mp", None)),
        out_specs=(rows, rows)
        + attention_in
        + dense
        + attention_in
        + (P(), P(), P("expert", None, "mp"), P("expert", "mp", None)),
        check_vma=False,
    )
```

```python
import functools

import jax
import jax.numpy as jnp
from jax import lax
from jax.experimental import pallas as pl
from jax.experimental.pallas import tpu as pltpu
from jax.sharding import PartitionSpec as P

EPSILON = 1e-06
BF16 = jnp.bfloat16
F32 = jnp.float32


def smooth_both(values):
    square = values * values
    tangent = jnp.tanh(0.7978845608 * values * (1.0 + 0.044715 * square))
    rest = 0.5 * (1.0 + tangent)
    slope = rest + (0.5 * 0.7978845608) * values * (1.0 - tangent * tangent) * (
        1.0 + 0.134145 * square
    )
    return values * rest, slope


def row_scale(rows):
    return lax.rsqrt(jnp.mean(rows * rows, axis=-1, keepdims=True) + EPSILON)


def normalize(rows, gain):
    return rows * row_scale(rows) * gain


def dot_nn(a, b):
    return jnp.dot(a, b, preferred_element_type=F32)


def dot_tn(a, b):
    return lax.dot_general(a, b, (((0,), (0,)), ((), ())), preferred_element_type=F32)


def dot_nt(a, b):
    return lax.dot_general(a, b, (((1,), (1,)), ((), ())), preferred_element_type=F32)


def flip(x, axis, bit):
    count = lax.axis_size(axis)
    return lax.ppermute(x, axis, [(i, i ^ (1 << bit)) for i in range(count)])


def meet(*values):
    leaves, tree = jax.tree.flatten(values)
    return jax.tree.unflatten(tree, lax.optimization_barrier(leaves))


def tie(value, *others):
    return meet(value, *others)[0]


def shift(x, axis, step):
    count = lax.axis_size(axis)
    return lax.ppermute(x, axis, [(i, (i + step) % count) for i in range(count)])


COST = pl.CostEstimate(flops=1, transcendentals=0, bytes_accessed=1)


def kernel_call(body, outs, scalars, arrays, limit=16):
    vmem = pl.BlockSpec(memory_space=pltpu.VMEM)
    return pl.pallas_call(
        body,
        out_shape=[jax.ShapeDtypeStruct(shape, dtype) for shape, dtype in outs],
        in_specs=[pl.BlockSpec(memory_space=pltpu.SMEM)] + [vmem] * len(arrays),
        out_specs=[vmem] * len(outs),
        compiler_params=pltpu.CompilerParams(vmem_limit_bytes=limit << 20),
        cost_estimate=COST,
    )(scalars, *arrays)


def place_scalars():
    return jnp.stack([lax.axis_index("expert"), lax.axis_index("dp") & 3]).astype(jnp.int32)


def plane_first(held):
    return flip(held, "dp", 0), flip(held, "dp", 1)


def plane_second(from_x, from_y):
    return flip(from_x[0], "dp", 1), flip(from_y[1], "dp", 0)


def quarter_of(left, right):
    rows = left.shape[0] // 4
    place = (lax.axis_index("dp") & 3) * rows
    return jnp.stack([lax.dynamic_slice_in_dim(t, place, rows, 0) for t in (left, right)])


def z_parts(piece):
    return [shift(piece, "expert", step) for step in range(1, lax.axis_size("expert"))]


def z_spread(piece):
    return jnp.stack(z_parts(piece), axis=1)


def assemble(left, right, pieces):
    count = lax.axis_size("expert")
    rows, cols = left.shape
    quarter = rows // 4

    def body(where, left_ref, right_ref, own, from_x, from_y, diag_left, diag_right, *outs):
        z, place = where[0], where[1]
        for side, (shard, diag) in enumerate(((left_ref, diag_left), (right_ref, diag_right))):
            outs[side][pl.ds(pl.multiple_of(z * rows, 16), rows), :] = shard[...]
            for step in range(1, count):
                base = lax.rem(z + count - step, count) * rows
                for key, ref in ((0, own), (1, from_x), (2, from_y), (3, diag)):
                    row = pl.multiple_of(base + (place ^ key) * quarter, 16)
                    outs[side][pl.ds(row, quarter), :] = (
                        ref[step - 1] if key == 3 else ref[side, step - 1]
                    )

    full = ((count * rows, cols), left.dtype)
    return kernel_call(body, [full, full], place_scalars(), (left, right) + tuple(pieces))


def add_low(a, b):
    return (a.astype(F32) + b.astype(F32)).astype(BF16)


def first_trip(send_a, send_b):
    return flip(send_a, "dp", 0), flip(send_b, "dp", 1)


def second_trip(send_a, send_b):
    return flip(send_a, "dp", 1), flip(send_b, "dp", 0)


def reduce_second(keep_a, keep_b, got_a, got_b):
    blocks = keep_a.shape[0]

    def body(where, keep_a, keep_b, got_a, got_b, send_a, send_b, next_a, next_b):
        x, y = where[1] & 1, where[1] >> 1
        for k in range(blocks):
            send_a[k] = add_low(keep_a[k, 1 - y], got_a[k, 1 - y])
            next_a[k] = add_low(keep_a[k, y], got_a[k, y])
            send_b[k] = add_low(keep_b[k, 1 - x], got_b[k, 1 - x])
            next_b[k] = add_low(keep_b[k, x], got_b[k, x])

    parts = [((blocks,) + keep.shape[2:], BF16) for keep in (keep_a, keep_b)]
    return kernel_call(body, parts * 2, place_scalars(), (keep_a, keep_b, got_a, got_b))


def far_sum(keep_a, keep_b, got_a, got_b):
    for bit in range(2, lax.axis_size("dp").bit_length() - 1):
        keep_a, keep_b = add_low(keep_a, got_a), add_low(keep_b, got_b)
        got_a, got_b = flip(keep_a, "dp", bit), flip(keep_b, "dp", bit)
    return keep_a, keep_b, got_a, got_b


def expert_held(*parts):
    def body(where, keep_a, keep_b, got_a, got_b, held_a, held_b):
        held_a[...] = add_low(keep_a[...], got_a[...])
        held_b[...] = add_low(keep_b[...], got_b[...])

    shapes = [(part.shape, BF16) for part in parts[:2]]
    return kernel_call(body, shapes, place_scalars(), far_sum(*parts))


def last_trip_e(held, got):
    both_a, both_b = (jnp.concatenate(pair, axis=0) for pair in zip(held, got))
    return flip(both_a, "dp", 0), flip(both_b, "dp", 1)


def expert_last(held, got, far):
    def body(where, *refs):
        place = where[1]
        for side in range(2):
            own, near, both = (refs[side + 2 * number] for number in range(3))
            rows, cols = own.shape[1:]
            first = 2 if side == 0 else 1
            for key, value in (
                (0, own[0]),
                (first, near[0]),
                (3 - first, both[0]),
                (3, both[1]),
            ):
                if side == 0:
                    at = pl.multiple_of((place ^ key) * cols, 128)
                    refs[6][:, pl.ds(at, cols)] = value.astype(F32)
                else:
                    at = pl.multiple_of((place ^ key) * rows, 16)
                    refs[7][pl.ds(at, rows), :] = value.astype(F32)

    (_, model, quarter), _ = (part.shape for part in held)
    shapes = [((model, 4 * quarter), F32), ((4 * quarter, model), F32)]
    return kernel_call(body, shapes, place_scalars(), (*held, *got, *far))


def reduce_third(*parts):
    blocks, rows, cols = parts[0].shape

    def body(where, keep_a, keep_b, got_a, got_b, *outs):
        for step, out in enumerate(outs):
            block = lax.rem(where[0] + step, blocks)
            out[0] = add_low(keep_a[block], got_a[block])
            out[1] = add_low(keep_b[block], got_b[block])

    own, *sends = kernel_call(
        body, [((2, rows, cols), BF16)] * blocks, place_scalars(), far_sum(*parts)
    )
    return own, sends


def reduce_halves(*parts):
    blocks, rows, cols = parts[0].shape
    half = blocks // 2

    def body(where, keep_a, keep_b, got_a, got_b, send, keep):
        upper = where[0] // half
        for k in range(half):
            for out, base in ((send, (1 - upper) * half), (keep, upper * half)):
                out[k, 0] = add_low(keep_a[base + k], got_a[base + k])
                out[k, 1] = add_low(keep_b[base + k], got_b[base + k])

    return kernel_call(
        body, [((half, 2, rows, cols), BF16)] * 2, place_scalars(), far_sum(*parts)
    )


def reduce_last_half(keep, got):
    half = keep.shape[0]

    def body(where, keep, got, send, own):
        odd = lax.rem(where[0], half)
        send[...] = add_low(keep[1 - odd], got[1 - odd])
        own[...] = add_low(keep[odd], got[odd])

    return kernel_call(
        body, [(keep.shape[1:], BF16)] * 2, place_scalars(), (keep, got)
    )


def z_trip(sends):
    return [shift(send, "expert", step + 1) for step, send in enumerate(sends)]


def reduce_fourth(own, got):
    total = own.astype(F32)
    for part in got:
        total = total + part.astype(F32)
    return total.astype(BF16)


def reduce_last(held, near, diagonal, widths):
    _, rows, _ = held.shape

    def body(where, own, from_x, from_y, diag_a, diag_b, *outs):
        place = where[1]
        start = 0
        for number, width in enumerate(widths):
            cols = slice(start, start + width)
            for side, diag in enumerate((diag_a, diag_b)):
                out = outs[2 * number + side]
                for key, ref in ((0, own), (1, from_x), (2, from_y), (3, diag)):
                    row = pl.multiple_of((place ^ key) * rows, 8)
                    value = ref[:, cols] if key == 3 else ref[side, :, cols]
                    out[pl.ds(row, rows), :] = value.astype(F32)
            start += width

    shapes = [((4 * rows, width), F32) for width in widths for _ in range(2)]
    outs = kernel_call(body, shapes, place_scalars(), (held, *near, *diagonal))
    return [outs[2 * i : 2 * i + 2] for i in range(len(widths))]


def pack_small(gains, router, tables):
    model = gains[0].shape[1]
    heads, levels = tables[0].shape
    top = len(gains) + router.shape[0]
    share = 1.0 / lax.axis_size("mp")

    def body(core, *refs):
        out = refs[-1]
        out[...] = jnp.zeros_like(out)
        for number in range(len(gains)):
            out[number : number + 1, :] = refs[number][...] * share
        out[len(gains) : top, :] = refs[len(gains)][...]
        for layer in range(2):
            for side in range(2):

                @pl.when(core[0] == side)
                def _():
                    at = (layer * 2 + side) * 128
                    out[top : top + heads, at : at + levels] = refs[len(gains) + 1 + layer][...]

    return kernel_call(
        body,
        [((16, model), F32)],
        jnp.stack([lax.axis_index("mp")]).astype(jnp.int32),
        (*gains, router, *tables),
    )[0]


def whole(shape):
    return pl.BlockSpec(memory_space=pltpu.VMEM)


PARAMS = pltpu.CompilerParams(vmem_limit_bytes=24 << 20)
MIDDLE = pltpu.CompilerParams(vmem_limit_bytes=20 << 20)
LARGE = pltpu.CompilerParams(vmem_limit_bytes=30 << 20)


def build_bias(buckets, tables, token):
    heads = tables.shape[0]
    seq_len = buckets.shape[0]
    padded = jnp.pad(tables, ((0, 0), (0, 128 - tables.shape[1])))

    def body(bucket_ref, table_ref, _, out_ref):
        head = pl.program_id(0)
        row = jnp.broadcast_to(table_ref[pl.ds(head, 1), :], (seq_len, 128))
        for part in range(seq_len // 128):
            index = bucket_ref[:, part * 128 : (part + 1) * 128]
            out_ref[0, :, part * 128 : (part + 1) * 128] = jnp.take_along_axis(row, index, axis=1)

    return pl.pallas_call(
        body,
        out_shape=jax.ShapeDtypeStruct((heads, seq_len, seq_len), F32),
        grid=(heads,),
        in_specs=[whole((seq_len, seq_len)), whole((heads, 128)), whole(token.shape)],
        out_specs=pl.BlockSpec((1, seq_len, seq_len), lambda h: (h, 0, 0)),
        compiler_params=PARAMS,
        cost_estimate=COST,
    )(buckets, padded, token)


def lane_masks(head_width):
    lane = lax.broadcasted_iota(jnp.int32, (1, 2 * head_width), 1)
    return [lane < head_width, lane >= head_width]


def masked(value, mask):
    return jnp.where(mask, value, jnp.zeros_like(value))


def both(first, second):
    if len(first.shape) == 2:
        return first[...].astype(F32) + second[...].astype(F32)
    return jnp.concatenate(
        [part[0].astype(F32) + part[1].astype(F32) for part in (first, second)], axis=0
    )


def stream_sum(base, partials):
    total = base[...].astype(F32)
    if partials:
        total = total + both(*partials)
    return total


def attention_forward(base, partials, gain, weights, bias):
    seq_len, model = base.shape
    heads = bias.shape[0]
    width = weights[0].shape[1] // 2
    head_width = width // heads
    chunk = 256
    scale = head_width**-0.5
    count = len(partials)

    def body(*refs):
        base_ref, part_refs = refs[0], refs[1 : 1 + count]
        gain_ref, wa_ref, wb_ref, bias_ref = refs[1 + count : 5 + count]
        stream_out, normed_out, joint_out, prob_ref, mixed_ref, partial_ref = refs[5 + count : -3]
        stream_ref, normed_ref, joint_ref = refs[-3:]
        step = pl.program_id(0)

        @pl.when(step == 0)
        def _():
            rows = stream_sum(base_ref, part_refs)
            stream_ref[...] = rows
            normed = normalize(rows, gain_ref[...]).astype(BF16)
            normed_ref[...] = normed
            left = dot_nn(normed, wa_ref[...]).astype(BF16)
            joint_ref[:, :width] = left[:, :width] * jnp.asarray(scale, BF16)
            joint_ref[:, width : 2 * width] = left[:, width:]
            joint_ref[:, 2 * width :] = dot_nn(normed, wb_ref[:, :width]).astype(BF16)

        masks = lane_masks(head_width)
        rows = pl.ds(pl.multiple_of(step * chunk, chunk), chunk)
        stream_out[...] = stream_ref[rows, :]
        normed_out[...] = normed_ref[rows, :]
        joint_out[...] = joint_ref[rows, :]
        for pair in range(heads // 2):
            cols = slice(pair * 2 * head_width, (pair + 1) * 2 * head_width)
            query = joint_ref[rows, cols]
            key = joint_ref[:, slice(width + cols.start, width + cols.stop)]
            value = joint_ref[:, slice(2 * width + cols.start, 2 * width + cols.stop)]
            mixed = None
            for side in range(2):
                head = 2 * pair + side
                scores = dot_nt(query, masked(key, masks[side])) + bias_ref[head]
                exp_part = jnp.exp(scores - jnp.max(scores, axis=-1, keepdims=True))
                share = 1.0 / jnp.sum(exp_part, axis=-1, keepdims=True)
                prob = (exp_part * share).astype(BF16)
                prob_ref[head] = prob
                out = dot_nn(prob, masked(value, masks[side]))
                mixed = out if mixed is None else mixed + out
            mixed_ref[:, cols] = mixed.astype(BF16)
        partial_ref[...] = dot_nt(mixed_ref[...], wb_ref[:, width:]).astype(BF16)

    full = (seq_len, model)
    def by_rows(cols):
        return pl.BlockSpec((chunk, cols), lambda i: (i, 0))

    heads_of = pl.BlockSpec((heads, chunk, seq_len), lambda i: (0, i, 0))
    kept = [
        (full, F32, by_rows(model)),
        (full, BF16, by_rows(model)),
        ((seq_len, 3 * width), BF16, by_rows(3 * width)),
        ((heads, seq_len, seq_len), BF16, heads_of),
        ((seq_len, width), BF16, by_rows(width)),
    ]
    return pl.pallas_call(
        body,
        out_shape=[pltpu.HBM(shape, dtype) for shape, dtype, _ in kept]
        + [jax.ShapeDtypeStruct(full, BF16)],
        grid=(seq_len // chunk,),
        in_specs=[whole(full)]
        + [whole(full)] * count
        + [whole((1, model)), whole(weights[0].shape), whole(weights[1].shape)]
        + [heads_of],
        out_specs=[spec for _, _, spec in kept] + [by_rows(model)],
        scratch_shapes=[
            pltpu.VMEM(full, F32),
            pltpu.VMEM(full, BF16),
            pltpu.VMEM((seq_len, 3 * width), BF16),
        ],
        compiler_params=PARAMS,
        cost_estimate=COST,
    )(base, *partials, gain[None], *weights, bias)


def attention_backward(grad, weights, joint, prob):
    seq_len, model = grad.shape
    heads = prob.shape[0]
    width = weights[0].shape[1] // 2
    head_width = width // heads
    chunk = 256
    steps = seq_len // chunk
    scale = head_width**-0.5

    def body(grad_ref, wa_ref, wb_ref, joint_ref, prob_ref, dj_ref, ds_ref, partial_ref, dk_acc, dv_acc):
        step = pl.program_id(0)

        @pl.when(step == 0)
        def _():
            dk_acc[...] = jnp.zeros_like(dk_acc)
            dv_acc[...] = jnp.zeros_like(dv_acc)

        masks = lane_masks(head_width)
        rows = pl.ds(pl.multiple_of(step * chunk, chunk), chunk)
        grad_mixed = dot_nn(grad_ref[...], wb_ref[:, width:]).astype(BF16)
        for pair in range(heads // 2):
            cols = slice(pair * 2 * head_width, (pair + 1) * 2 * head_width)
            query = joint_ref[rows, cols]
            key = joint_ref[:, slice(width + cols.start, width + cols.stop)]
            value = joint_ref[:, slice(2 * width + cols.start, 2 * width + cols.stop)]
            go = grad_mixed[:, cols]
            dq = None
            dk = None
            dv = None
            for side in range(2):
                head = 2 * pair + side
                low = prob_ref[head]
                wide = low.astype(F32)
                grad_prob = dot_nt(go, masked(value, masks[side]))
                inner = jnp.sum(wide * grad_prob, axis=-1, keepdims=True)
                ds = (wide * (grad_prob - inner)).astype(BF16)
                ds_ref[head] = ds
                one_q = dot_nn(ds, masked(key, masks[side]))
                one_k = dot_tn(ds, masked(query, masks[side]))
                one_v = dot_tn(low, masked(go, masks[side]))
                dq = one_q if dq is None else dq + one_q
                dk = one_k if dk is None else dk + one_k
                dv = one_v if dv is None else dv + one_v
            dj_ref[rows, cols] = (dq * scale).astype(BF16)
            dk_acc[:, cols] += dk
            dv_acc[:, cols] += dv

        @pl.when(step == steps - 1)
        def _():
            dj_ref[:, width : 2 * width] = dk_acc[...].astype(BF16)
            dj_ref[:, 2 * width :] = dv_acc[...].astype(BF16)
            partial_ref[...] = (
                dot_nt(dj_ref[:, : 2 * width], wa_ref[...])
                + dot_nt(dj_ref[:, 2 * width :], wb_ref[:, :width])
            ).astype(BF16)

    full = (seq_len, model)
    rows_of = pl.BlockSpec((heads, chunk, seq_len), lambda i: (0, i, 0))
    return pl.pallas_call(
        body,
        out_shape=[
            jax.ShapeDtypeStruct((seq_len, 3 * width), BF16),
            pltpu.HBM(prob.shape, BF16),
            jax.ShapeDtypeStruct(full, BF16),
        ],
        grid=(steps,),
        in_specs=[
            pl.BlockSpec((chunk, model), lambda i: (i, 0)),
            whole(weights[0].shape),
            whole(weights[1].shape),
            whole(joint.shape),
            rows_of,
        ],
        out_specs=[whole((seq_len, 3 * width)), rows_of, whole(full)],
        scratch_shapes=[pltpu.VMEM((seq_len, width), F32)] * 2,
        compiler_params=PARAMS,
        cost_estimate=COST,
    )(grad, *weights, joint, prob)


def split_first(where, a, b, send_a, send_b, keep_a, keep_b, blocks):
    rows = send_a.shape[2]
    x, y = where[1] & 1, where[1] >> 1
    for k in range(blocks):
        for j in range(2):
            for i in range(2):
                at = (k * 4 + j * 2 + i) * rows
                piece_a, piece_b = a[at : at + rows], b[at : at + rows]

                @pl.when(x == i)
                def _():
                    keep_a[k, j] = piece_a

                @pl.when(x != i)
                def _():
                    send_a[k, j] = piece_a

                @pl.when(y == j)
                def _():
                    keep_b[k, i] = piece_b

                @pl.when(y != j)
                def _():
                    send_b[k, i] = piece_b


def weight_grads(blocks, lefts, rights):
    model = lefts[0][0].shape[1]
    cols = sum(stop - start for _, _, start, stop in lefts)
    rows = model // blocks // 4
    half = ((blocks, 2, rows, cols), BF16)
    flat = [t for pair in lefts + rights for t in pair[:2]]

    def body(where, *refs):
        inputs, outs = refs[: len(flat)], refs[len(flat) :]

        def side(number, pairs):
            return jnp.concatenate(
                [
                    dot_tn(
                        inputs[number + 2 * i][...], inputs[number + 2 * i + 1][:, start:stop]
                    ).astype(BF16)
                    for i, (_, _, start, stop) in enumerate(pairs)
                ],
                axis=1,
            )

        split_first(where, side(0, lefts), side(2 * len(lefts), rights), *outs, blocks)

    return kernel_call(body, [half] * 4, place_scalars(), flat)


def table_grad(ds, buckets, bucket_count):
    heads, seq_len, _ = ds.shape
    group = 8

    def body(ds_ref, bucket_ref, out_ref, acc):
        acc[...] = jnp.zeros_like(acc)

        def one(number, carry):
            rows = pl.ds(pl.multiple_of(number * group, group), group)
            index = bucket_ref[rows, :]
            hot = jnp.concatenate(
                [jnp.where(index == level, 1.0, 0.0) for level in range(bucket_count)], axis=0
            ).astype(BF16)
            right = jnp.concatenate(
                [ds_ref[head, rows, :].astype(F32) for head in range(heads)], axis=0
            ).astype(BF16)
            acc[...] += dot_nt(hot, right)
            return carry

        lax.fori_loop(0, seq_len // group, one, 0, unroll=4)
        shape = acc.shape
        same = (
            lax.broadcasted_iota(jnp.int32, shape, 0) % group
            == lax.broadcasted_iota(jnp.int32, shape, 1) % group
        )
        kept = jnp.where(same, acc[...], 0.0)
        spread = (
            lax.broadcasted_iota(jnp.int32, (bucket_count, shape[0]), 1) // group
            == lax.broadcasted_iota(jnp.int32, (bucket_count, shape[0]), 0)
        ).astype(F32)
        gather = (
            lax.broadcasted_iota(jnp.int32, (heads, shape[1]), 1) // group
            == lax.broadcasted_iota(jnp.int32, (heads, shape[1]), 0)
        ).astype(F32)
        exact = dict(preferred_element_type=F32, precision=lax.Precision.HIGHEST)
        by_level = jnp.dot(spread, kept, **exact)
        out_ref[...] = lax.dot_general(gather, by_level, (((1,), (1,)), ((), ())), **exact)

    vmem = pl.BlockSpec(memory_space=pltpu.VMEM)
    return pl.pallas_call(
        body,
        out_shape=jax.ShapeDtypeStruct((heads, bucket_count), F32),
        in_specs=[vmem, vmem],
        out_specs=vmem,
        scratch_shapes=[pltpu.VMEM((bucket_count * group, heads * group), F32)],
        compiler_params=PARAMS,
        cost_estimate=COST,
    )(ds, buckets)


def dense_forward(base, partials, gain, w_in, w_out):
    seq_len, model = base.shape
    hidden_width = w_in.shape[1]
    chunk = 512
    steps = hidden_width // chunk

    def body(base_ref, own_ref, got_ref, gain_ref, in_ref, out_ref, stream_ref, normed_ref, hidden_ref, slope_ref, partial_ref, acc):
        step = pl.program_id(0)

        @pl.when(step == 0)
        def _():
            rows = stream_sum(base_ref, (own_ref, got_ref))
            stream_ref[...] = rows
            normed_ref[...] = normalize(rows, gain_ref[...]).astype(BF16)
            acc[...] = jnp.zeros_like(acc)

        pre = dot_nn(normed_ref[...], in_ref[...])
        act, slope = smooth_both(pre)
        hidden = act.astype(BF16)
        hidden_ref[...] = hidden
        slope_ref[...] = slope.astype(BF16)
        acc[...] += dot_nt(hidden, out_ref[...])

        @pl.when(step == steps - 1)
        def _():
            partial_ref[...] = acc[...].astype(BF16)

    full = (seq_len, model)
    col = pl.BlockSpec((model, chunk), lambda i: (0, i))
    act = pl.BlockSpec((seq_len, chunk), lambda i: (0, i))
    return pl.pallas_call(
        body,
        out_shape=[
            jax.ShapeDtypeStruct(full, F32),
            jax.ShapeDtypeStruct(full, BF16),
            pltpu.HBM((seq_len, hidden_width), BF16),
            pltpu.HBM((seq_len, hidden_width), BF16),
            jax.ShapeDtypeStruct(full, BF16),
        ],
        grid=(steps,),
        in_specs=[whole(full)] * 3 + [whole((1, model)), col, col],
        out_specs=[whole(full), whole(full), act, act, whole(full)],
        scratch_shapes=[pltpu.VMEM(full, F32)],
        compiler_params=PARAMS,
        cost_estimate=COST,
    )(base, *partials, gain[None], w_in, w_out)


def norm_step(grad_ref, rows_ref, gain_ref, own_ref, got_ref):
    upstream = both(own_ref, got_ref)
    rows = rows_ref[...].astype(F32)
    scale = row_scale(rows)
    scaled = upstream * gain_ref[...]
    inner = jnp.mean(scaled * rows, axis=-1, keepdims=True)
    grad_rows = scale * scaled - rows * (scale * scale * scale * inner)
    grad_gain = jnp.sum(upstream * rows * scale, axis=0, keepdims=True)
    return grad_ref[...].astype(F32) + grad_rows, grad_gain


def norm_kernel(grad, rows, gain, partials):
    full = rows.shape

    def body(_, grad_ref, rows_ref, gain_ref, own_ref, got_ref, out_ref, low_ref, gain_out):
        total, gain_out[...] = norm_step(grad_ref, rows_ref, gain_ref, own_ref, got_ref)
        out_ref[...] = total
        low_ref[...] = total.astype(BF16)

    return kernel_call(
        body,
        [(full, F32), (full, BF16), ((1, full[1]), F32)],
        place_scalars(),
        (grad, rows, gain[None], *partials),
    )


def dense_backward(grad, rows, gain, partials, w_in, w_out, slope):
    seq_len, model = rows.shape
    hidden_width = w_in.shape[1]
    chunk = 512
    steps = hidden_width // chunk

    def body(grad_ref, rows_ref, gain_ref, own_ref, got_ref, in_ref, out_ref, slope_ref, total_ref, low_ref, dpre_ref, partial_ref, gain_out, acc):
        step = pl.program_id(0)

        @pl.when(step == 0)
        def _():
            total, gain_out[...] = norm_step(grad_ref, rows_ref, gain_ref, own_ref, got_ref)
            total_ref[...] = total
            low_ref[...] = total.astype(BF16)
            acc[...] = jnp.zeros_like(acc)

        dpre = (dot_nn(low_ref[...], out_ref[...]) * slope_ref[...].astype(F32)).astype(BF16)
        dpre_ref[...] = dpre
        acc[...] += dot_nt(dpre, in_ref[...])

        @pl.when(step == steps - 1)
        def _():
            partial_ref[...] = acc[...].astype(BF16)

    full = (seq_len, model)
    col = pl.BlockSpec((model, chunk), lambda i: (0, i))
    act = pl.BlockSpec((seq_len, chunk), lambda i: (0, i))
    return pl.pallas_call(
        body,
        out_shape=[
            jax.ShapeDtypeStruct(full, F32),
            jax.ShapeDtypeStruct(full, BF16),
            jax.ShapeDtypeStruct((seq_len, hidden_width), BF16),
            jax.ShapeDtypeStruct(full, BF16),
            jax.ShapeDtypeStruct((1, model), F32),
        ],
        grid=(steps,),
        in_specs=[whole(full)] * 2 + [whole((1, model))] + [whole(full)] * 2 + [col, col, act],
        out_specs=[whole(full), whole(full), act, whole(full), whole((1, model))],
        scratch_shapes=[pltpu.VMEM(full, F32)],
        compiler_params=PARAMS,
        cost_estimate=COST,
    )(grad, rows, gain[None], *partials, w_in, w_out, slope)


def send_slots(base, partials, gain, spots, blocks):
    seq_len, model = base.shape
    slots = spots[1] // blocks
    full = (seq_len, model)

    def body(_, base_ref, own_ref, got_ref, gain_ref, spot_ref, stream_ref, normed_ref, *outs):
        rows = stream_sum(base_ref, (own_ref, got_ref))
        stream_ref[...] = rows
        normed = normalize(rows, gain_ref[...]).astype(BF16)
        normed_ref[...] = normed
        for block in range(blocks):
            slot = lax.broadcasted_iota(jnp.int32, (slots, seq_len), 0) + block * slots
            hot = jnp.where(slot == spot_ref[...], 1.0, 0.0).astype(BF16)
            outs[block][...] = dot_nn(hot, normed).astype(BF16)

    return kernel_call(
        body,
        [(full, F32), (full, BF16)] + [((slots, model), BF16)] * blocks,
        place_scalars(),
        (base, *partials, gain[None], spots[0]),
    )


def stacked(blocks):
    rows, cols = blocks[0].shape

    def body(_, *refs):
        for number, ref in enumerate(refs[:-1]):
            refs[-1][number * rows : (number + 1) * rows, :] = ref[...]

    return kernel_call(body, [((len(blocks) * rows, cols), blocks[0].dtype)], place_scalars(), blocks)[0]


def route_softmax(rows, router):
    logits = dot_nt(rows, router)
    exp_part = jnp.exp(logits - jnp.max(logits, axis=-1, keepdims=True))
    return exp_part / jnp.sum(exp_part, axis=-1, keepdims=True)


def expert_step(rows, grads, router, w_in, w_out):
    half, model = rows[0].shape
    hidden_width = w_in.shape[1]
    chunk = 512
    steps = hidden_width // chunk
    total = 2 * half

    def body(where, own_ref, other_ref, own_grad, other_grad, router_ref, in_ref, out_ref, hidden_ref, dpre_ref, grad_ref, res_own, res_other, back_own, back_other, res_acc, back_acc, rows_ref):
        step = pl.program_id(0)

        @pl.when(step == 0)
        def _():
            rows_ref[:half, :] = own_ref[...]
            rows_ref[half:, :] = other_ref[...]
            here = lax.broadcasted_iota(jnp.int32, (1, router_ref.shape[0]), 1) == where[0]
            for side, grad in enumerate((own_grad, other_grad)):
                part = slice(side * half, (side + 1) * half)
                prob = route_softmax(rows_ref[part, :], router_ref[...])
                gate = jnp.sum(jnp.where(here, prob, 0.0), axis=-1, keepdims=True)
                grad_ref[part, :] = (gate * grad[...].astype(F32)).astype(BF16)
            res_acc[...] = jnp.zeros_like(res_acc)
            back_acc[...] = jnp.zeros_like(back_acc)

        pre = dot_nn(rows_ref[...], in_ref[...])
        act, slope = smooth_both(pre)
        hidden = act.astype(BF16)
        hidden_ref[...] = hidden
        dpre = (dot_nt(grad_ref[...], out_ref[...]) * slope).astype(BF16)
        dpre_ref[...] = dpre
        res_acc[...] += dot_nn(hidden, out_ref[...])
        back_acc[...] += dot_nt(dpre, in_ref[...])

        @pl.when(step == steps - 1)
        def _():
            res_own[...] = res_acc[:half, :]
            res_other[...] = res_acc[half:, :].astype(BF16)
            back_own[...] = back_acc[:half, :]
            back_other[...] = back_acc[half:, :].astype(BF16)

    part = (half, model)
    act = pl.BlockSpec((total, chunk), lambda i: (0, i))
    return pl.pallas_call(
        body,
        out_shape=[
            pltpu.HBM((total, hidden_width), BF16),
            pltpu.HBM((total, hidden_width), BF16),
            jax.ShapeDtypeStruct((total, model), BF16),
            jax.ShapeDtypeStruct(part, F32),
            jax.ShapeDtypeStruct(part, BF16),
            jax.ShapeDtypeStruct(part, F32),
            jax.ShapeDtypeStruct(part, BF16),
        ],
        grid=(steps,),
        in_specs=[pl.BlockSpec(memory_space=pltpu.SMEM)]
        + [whole(part)] * 4
        + [
            whole(router.shape),
            pl.BlockSpec((model, chunk), lambda i: (0, i)),
            pl.BlockSpec((chunk, model), lambda i: (i, 0)),
        ],
        out_specs=[act, act, whole((total, model))] + [whole(part)] * 4,
        scratch_shapes=[pltpu.VMEM((total, model), F32)] * 2 + [pltpu.VMEM((total, model), BF16)],
        compiler_params=LARGE,
        cost_estimate=COST,
    )(place_scalars(), *rows, *grads, router, w_in, w_out)


def expert_finish(result, back, rows, grads, router, blocks):
    half, model = rows.shape
    slots = half // blocks

    def body(where, res_own, res_got, back_own, back_got, rows_ref, grad_ref, router_ref, *outs):
        here = lax.broadcasted_iota(jnp.int32, (1, router_ref.shape[0]), 1) == where[0]
        prob = route_softmax(rows_ref[...], router_ref[...])
        gate = jnp.sum(jnp.where(here, prob, 0.0), axis=-1, keepdims=True)
        result = res_own[...] + res_got[...].astype(F32)
        grad_gate = jnp.sum(grad_ref[...].astype(F32) * result, axis=-1, keepdims=True)
        dz = (prob * (jnp.where(here, grad_gate, 0.0) - grad_gate * gate)).astype(BF16)
        total = back_own[...] + back_got[...].astype(F32) + dot_nn(dz, router_ref[...])
        for block in range(blocks):
            part = slice(block * slots, (block + 1) * slots)
            outs[block][...] = total[part, :].astype(BF16)
            outs[blocks + block][...] = result[part, :].astype(BF16)
        outs[-1][...] = dot_tn(dz, rows_ref[...])

    return kernel_call(
        body,
        [((slots, model), BF16)] * (2 * blocks) + [(router.shape, F32)],
        place_scalars(),
        (*result, *back, rows, grads, router),
    )


def expert_grads(kept, rows, hidden, dpre, grads):
    half, model = rows[0].shape
    hidden_width = hidden.shape[1]
    quarter = hidden_width // 4

    def spot_a(step, where):
        x = where[1] & 1
        return step * 2 + (x if kept else 1 - x)

    def spot_b(step, where):
        y = where[1] >> 1
        return (y if kept else 1 - y) * 2 + step

    def body(where, own_ref, other_ref, hidden_ref, dpre_ref, grad_ref, out_a, out_b, rows_ref):
        @pl.when(pl.program_id(0) == 0)
        def _():
            rows_ref[:half, :] = own_ref[...]
            rows_ref[half:, :] = other_ref[...]

        out_a[0] = dot_tn(rows_ref[...], dpre_ref[...]).astype(BF16)
        out_b[0] = dot_tn(hidden_ref[...], grad_ref[...]).astype(BF16)

    shape_a, shape_b = (model, quarter), (quarter, model)
    return pl.pallas_call(
        body,
        out_shape=[jax.ShapeDtypeStruct((2,) + shape, BF16) for shape in (shape_a, shape_b)],
        grid_spec=pltpu.PrefetchScalarGridSpec(
            num_scalar_prefetch=1,
            grid=(2,),
            in_specs=[
                whole(None),
                whole(None),
                pl.BlockSpec((2 * half, quarter), lambda i, w: (0, spot_b(i, w))),
                pl.BlockSpec((2 * half, quarter), lambda i, w: (0, spot_a(i, w))),
                whole(None),
            ],
            out_specs=[
                pl.BlockSpec((1,) + shape_a, lambda i, w: (i, 0, 0)),
                pl.BlockSpec((1,) + shape_b, lambda i, w: (i, 0, 0)),
            ],
            scratch_shapes=[pltpu.VMEM((2 * half, model), BF16)],
        ),
        compiler_params=MIDDLE,
        cost_estimate=COST,
    )(
        place_scalars(),
        *rows,
        pltpu.with_memory_space_constraint(hidden, pltpu.HBM),
        pltpu.with_memory_space_constraint(dpre, pltpu.HBM),
        grads,
    )


def receive_slots(grad, rows, gain, spots, halves):
    full = rows.shape
    half = halves[0].shape[0]

    def body(_, grad_ref, rows_ref, gain_ref, spot_ref, own_ref, got_ref, out_ref, low_ref, gain_out):
        slot = lax.broadcasted_iota(jnp.int32, (full[0], half), 1)
        first = jnp.where(slot == spot_ref[...], 1.0, 0.0).astype(BF16)
        second = jnp.where(slot + half == spot_ref[...], 1.0, 0.0).astype(BF16)
        upstream = dot_nn(first, own_ref[...]) + dot_nn(second, got_ref[...])
        value = rows_ref[...]
        scale = row_scale(value)
        scaled = upstream * gain_ref[...]
        inner = jnp.mean(scaled * value, axis=-1, keepdims=True)
        total = grad_ref[...].astype(F32) + (
            scale * scaled - value * (scale * scale * scale * inner)
        )
        gain_out[...] = jnp.sum(upstream * value * scale, axis=0, keepdims=True)
        out_ref[...] = total
        low_ref[...] = total.astype(BF16)

    return kernel_call(
        body,
        [(full, F32), (full, BF16), ((1, full[1]), F32)],
        place_scalars(),
        (grad, rows, gain[None], spots) + tuple(halves),
    )


def on_device(
    tokens,
    cotangent,
    routes,
    buckets,
    norm_first,
    query_first,
    key_first,
    value_first,
    output_first,
    table_first,
    dense_gain,
    dense_in,
    dense_out,
    norm_second,
    query_second,
    key_second,
    value_second,
    output_second,
    table_second,
    expert_gain,
    router,
    expert_in,
    expert_out,
):
    mp_index = lax.axis_index("mp")
    z_index = lax.axis_index("expert")
    z_count = lax.axis_size("expert")
    tok_local, model_width = tokens.shape
    seq_len = buckets.shape[0]
    expert_count = router.shape[1]
    capacity = seq_len // 2
    slots = capacity // lax.axis_size("mp")
    bucket_count = table_first.shape[0]
    head_local = table_first.shape[1] // lax.axis_size("mp")

    width = query_first.shape[1]
    ff_width = dense_in.shape[1]
    shards = (
        (
            jnp.concatenate([query_first, key_first], axis=1),
            jnp.concatenate([value_first, output_first.T], axis=1),
        ),
        (dense_in, dense_out.T),
        (
            jnp.concatenate([query_second, key_second], axis=1),
            jnp.concatenate([value_second, output_second.T], axis=1),
        ),
    )
    far_one = z_spread(quarter_of(*shards[0]))

    def local_bias(table, token):
        return build_bias(
            buckets, lax.dynamic_slice_in_dim(table, mp_index * head_local, head_local, 1).T, token
        )

    chosen = routes[:, 0]
    experts = jnp.arange(expert_count, dtype=jnp.int32)
    picked = chosen[:, None] == experts[None, :]
    order = jnp.arange(seq_len, dtype=jnp.int32)
    earlier = (order[None, :] < order[:, None]).astype(BF16)
    rank = jnp.sum(
        jnp.where(picked, dot_nn(earlier, picked.astype(BF16)), 0.0), axis=1
    ).astype(jnp.int32)
    distance = (chosen - z_index + z_count) % z_count
    spot = distance * slots + rank % slots
    half = z_count * slots
    in_own_half = rank // slots == mp_index
    send_spots = jnp.where(in_own_half, spot, -1)[None, :]
    back_spots = jnp.where(in_own_half, spot, spot + half)[:, None]

    def sent_on(blocks):
        return [blocks[0]] + [shift(blocks[step], "expert", step) for step in range(1, z_count)]

    def with_other(own):
        return own, flip(own, "mp", 0)

    def sent_back(blocks):
        return [blocks[0]] + [
            shift(blocks[step], "expert", z_count - step) for step in range(1, z_count)
        ]

    def swapped(partial):
        return partial, flip(partial, "mp", 0)

    def gathered(partial):
        rows = partial.shape[0] // 2
        return tuple(
            lax.all_gather(part, "mp", axis=0) for part in (partial[:rows], partial[rows:])
        )

    piece_ff, far_one = meet(quarter_of(*shards[1]), far_one)
    near_one = plane_first(far_one)
    got_ff = z_parts(piece_ff)
    bias_one = local_bias(table_first, far_one[0, 0, :8, :128])
    tokens, cotangent, near_one, bias_one = meet(tokens, cotangent, near_one, bias_one)
    diag_one = plane_second(*near_one)
    stream_zero = lax.all_gather(tokens, "mp", axis=0, tiled=True)
    grad_four = lax.all_gather(cotangent, "mp", axis=0, tiled=True)
    bias_two = local_bias(table_second, near_one[0][0, 0, :8, :128])
    diag_one, got_ff, bias_two, stream_zero, grad_four, send_spots, back_spots = meet(
        diag_one, got_ff, bias_two, stream_zero, grad_four, send_spots, back_spots
    )
    piece_two, far_ff = meet(quarter_of(*shards[2]), jnp.stack(got_ff, axis=1))
    near_ff = plane_first(far_ff)
    got_two = z_parts(piece_two)
    weights_one = assemble(*shards[0], (far_one, *near_one, *diag_one))
    _, normed_one, joint_one, prob_one, mixed_one, partial = attention_forward(
        tie(stream_zero, far_ff), (), norm_first, weights_one, bias_one
    )
    partial, near_ff, got_two = meet(partial, near_ff, got_two)
    diag_ff = plane_second(*near_ff)
    far_two = jnp.stack(got_two, axis=1)
    diag_ff, pair, far_two = meet(diag_ff, swapped(partial), far_two)
    near_two = plane_first(far_two)
    to_slots = (jnp.arange(half, dtype=jnp.int32)[:, None] == send_spots).astype(BF16)
    grad_sent = dot_nn(to_slots, tie(grad_four, pair)).astype(BF16)
    grad_got = sent_on([grad_sent[i * slots : (i + 1) * slots] for i in range(z_count)])
    w_in_full, w_out_full = assemble(*shards[1], (far_ff, *near_ff, *diag_ff))
    stream_one, normed_ff, hidden, slope, partial = dense_forward(
        stream_zero, pair, dense_gain, w_in_full, tie(w_out_full, grad_sent)
    )
    near_two, partial = meet(near_two, partial)
    diag_two = plane_second(*near_two)
    diag_two, pair = meet(diag_two, swapped(partial))
    weights_two = assemble(*shards[2], (far_two, *near_two, *diag_two))
    stream_two, normed_two, joint_two, prob_two, mixed_two, partial = attention_forward(
        stream_one, pair, norm_second, weights_two, bias_two
    )

    partial, grad_got = meet(partial, grad_got)

    grad_slots, pair = meet(with_other(stacked(grad_got)), swapped(partial))
    stream_three, moe_rows, *sent = send_slots(
        stream_two, pair, expert_gain, (send_spots, half), z_count
    )
    moe_slots = with_other(stacked(sent_on(sent)))
    router_rows = router.T
    expert_hidden, expert_dpre, expert_rows, res_own, res_other, back_own, back_other = expert_step(
        moe_slots, grad_slots, router_rows, expert_in[0], expert_out[0]
    )
    inputs_e = (moe_slots, expert_hidden, expert_dpre, expert_rows)
    send_e = expert_grads(False, *inputs_e)
    send_e, inputs_e, res_got, back_got = meet(
        send_e, inputs_e, flip(res_other, "mp", 0), flip(back_other, "mp", 0)
    )
    got_e = first_trip(*send_e)
    keep_e = expert_grads(True, *inputs_e)
    res_got, back_got, keep_e = meet(res_got, back_got, keep_e)
    keep_e = [part[None] for part in keep_e]
    *returns, grad_router = expert_finish(
        (res_own, res_got),
        (back_own, back_got),
        moe_slots[0],
        grad_slots[0],
        router_rows,
        z_count,
    )
    back_got, got_e = meet(sent_back(returns[:z_count]), got_e)
    send_ea, send_eb, *keep_e = reduce_second(*keep_e, got_e[0][None], got_e[1][None])
    send_ea, send_eb, back_got = meet(send_ea, send_eb, back_got)
    got_e = second_trip(send_ea, send_eb)
    grad_three, grad_low, grad_expert_gain = receive_slots(
        grad_four, stream_three, expert_gain, back_spots, with_other(stacked(back_got))
    )

    def attention_grads(kernel, normed, dj, low, mixed):
        return kernel(
            z_count,
            [(normed, dj, 0, 2 * width)],
            [(normed, dj, 2 * width, 3 * width), (low, mixed, 0, width)],
        )

    dj_two, ds_two, partial = attention_backward(grad_low, weights_two, joint_two, prob_two)
    partial, dj_two, got_e = meet(partial, dj_two, got_e)
    held_e = expert_held(*keep_e, *got_e)
    held_e, dj_two, partial = meet(held_e, dj_two, partial)
    from_e = (flip(held_e[0], "dp", 1), flip(held_e[1], "dp", 0))
    halves_two = attention_grads(weight_grads, normed_two, dj_two, grad_low, mixed_two)
    halves_two, partial = meet(halves_two, partial)
    got_two = first_trip(*halves_two[:2])
    grad_two, grad_low, dpre, partial, grad_norm_second = dense_backward(
        grad_three, stream_two, norm_second, gathered(partial), w_in_full, w_out_full, slope
    )
    halves_ff = weight_grads(
        z_count, [(normed_ff, dpre, 0, ff_width)], [(grad_low, hidden, 0, ff_width)]
    )
    from_e, halves_ff, partial, got_two, *result_blocks = meet(
        from_e, halves_ff, partial, got_two, *returns[z_count:]
    )
    got_ff = first_trip(*halves_ff[:2])
    result_got = sent_back(result_blocks)
    *send_two, keep_a, keep_b = reduce_second(*halves_two[2:], *got_two)
    keep_two = (keep_a, keep_b)
    grad_one, grad_low, grad_dense_gain = norm_kernel(
        grad_two, stream_one, dense_gain, gathered(tie(partial, send_two))
    )
    dj_one, ds_one, partial = attention_backward(grad_low, weights_one, joint_one, prob_one)
    dj_one, partial, result_got, send_two = meet(dj_one, partial, result_got, send_two)
    got_two = second_trip(*send_two)
    result_own = stacked(result_got)
    halves_one = attention_grads(weight_grads, normed_one, dj_one, grad_low, mixed_one)
    halves_one, partial = meet(halves_one, partial)
    grad_zero, _, grad_norm_first = norm_kernel(
        grad_one, stream_zero, norm_first, gathered(partial)
    )
    grad_norm_first, halves_one, got_two = meet(grad_norm_first, halves_one, got_two)
    own_two, send_two = reduce_third(*keep_two, *got_two)
    send_two, got_ff, halves_one = meet(send_two, got_ff, halves_one)
    got_two = z_trip(send_two)
    *send_ff, keep_a, keep_b = reduce_second(*halves_ff[2:], *got_ff)
    keep_ff = (keep_a, keep_b)
    send_ff, ds_two = meet(send_ff, ds_two)
    got_ff = second_trip(*send_ff)
    table_two_grad = table_grad(ds_two, buckets, bucket_count)
    table_two_grad, got_ff, got_two, halves_one = meet(table_two_grad, got_ff, got_two, halves_one)
    send_ff, keep_ff = reduce_halves(*keep_ff, *got_ff)
    send_ff, halves_one, ds_one, held_e, from_e = meet(send_ff, halves_one, ds_one, held_e, from_e)
    got_ff = flip(send_ff, "expert", 1)
    got_one = first_trip(*halves_one[:2])
    far_e = last_trip_e(held_e, from_e)
    table_one_grad = table_grad(ds_one, buckets, bucket_count)
    table_one_grad, got_one, got_two = meet(table_one_grad, got_one, got_two)
    *send_one, keep_a, keep_b = reduce_second(*halves_one[2:], *got_one)
    got_one = second_trip(*send_one)
    held_two = reduce_fourth(own_two, got_two)
    small = pack_small(
        (grad_norm_first, grad_dense_gain, grad_norm_second, grad_expert_gain),
        grad_router,
        (table_one_grad, table_two_grad),
    )
    held_two, got_ff, small = meet(held_two, got_ff, small)
    send_ff, keep_ff = reduce_last_half(keep_ff, got_ff)
    got_ff = flip(send_ff, "expert", 0)
    send_ff, got_one = meet(send_ff, got_one)
    send_one, keep_one = reduce_halves(keep_a, keep_b, *got_one)
    send_one, got_ff, held_two, small, far_e = meet(send_one, got_ff, held_two, small, far_e)
    held = jnp.concatenate([add_low(keep_ff, got_ff), held_two], axis=-1)
    near = plane_first(held)
    got_one = flip(send_one, "expert", 1)
    got_small = flip(small, "mp", 0)
    expert_in_sum, expert_out_sum = expert_last(held_e, from_e, far_e)
    small, got_small, near, got_one, expert_in_sum = meet(
        small, got_small, near, got_one, expert_in_sum
    )
    small = small + got_small
    diagonal = plane_second(*near)
    send_one, keep_one = reduce_last_half(keep_one, got_one)
    got_one = flip(send_one, "expert", 0)
    got_small = flip(small, "expert", 1)
    diagonal, got_one, small, got_small = meet(diagonal, got_one, small, got_small)
    small = small + got_small
    held_one = add_low(keep_one, got_one)
    near_one = plane_first(held_one)
    got_small = flip(small, "expert", 0)
    (ff_in, ff_out), two = reduce_last(held, near, diagonal, (ff_width, 2 * width))
    near_one, ff_in, small, got_small, result_own = meet(
        near_one, ff_in, small, got_small, result_own
    )
    small = small + got_small
    diag_one = plane_second(*near_one)
    for bit in range(lax.axis_size("dp").bit_length() - 1):
        small = small + flip(small, "dp", bit)
    (one,) = reduce_last(held_one, near_one, diag_one, (2 * width,))
    first_row = mp_index * tok_local
    grad_zero = lax.dynamic_slice_in_dim(grad_zero, first_row, tok_local, 0)

    result_got = flip(result_own, "mp", 0)
    spots_here = lax.dynamic_slice_in_dim(back_spots, first_row, tok_local, 0)
    lanes = jnp.arange(half, dtype=jnp.int32)[None, :]
    result_rows = dot_nn((lanes == spots_here).astype(BF16), result_own) + dot_nn(
        (lanes + half == spots_here).astype(BF16), result_got
    )
    own_rows = lax.dynamic_slice_in_dim(moe_rows, first_row, tok_local, 0)
    own_picked = lax.dynamic_slice_in_dim(picked, first_row, tok_local, 0)
    own_gate = jnp.sum(
        jnp.where(own_picked, route_softmax(own_rows, router_rows), 0.0), axis=-1, keepdims=True
    )
    final_rows = (
        lax.dynamic_slice_in_dim(stream_three, first_row, tok_local, 0) + own_gate * result_rows
    )

    router_sum = small[4 : 4 + expert_count].T
    base = 4 + expert_count
    table_one_sum, table_two_sum = (
        jnp.concatenate(
            [
                small[base : base + head_local, at * 128 : at * 128 + bucket_count]
                for at in (layer * 2, layer * 2 + 1)
            ],
            axis=0,
        ).T
        for layer in range(2)
    )

    return (
        final_rows,
        grad_zero,
        small[0],
        one[0][:, :width],
        one[0][:, width:],
        one[1][:, :width],
        one[1][:, width:].T,
        table_one_sum,
        small[1],
        ff_in,
        ff_out.T,
        small[2],
        two[0][:, :width],
        two[0][:, width:],
        two[1][:, :width],
        two[1][:, width:].T,
        table_two_sum,
        small[3],
        router_sum,
        expert_in_sum[None],
        expert_out_sum[None],
    )


def solution(mesh):
    rows = P(("dp", "expert", "mp"), None)
    cols_in, cols_out = P("expert", "mp"), P("mp", "expert")
    attention_in = (P(), cols_in, cols_in, cols_in, cols_out, P())
    dense = (P(), cols_in, cols_out)
    return jax.shard_map(
        on_device,
        mesh=mesh,
        in_specs=(rows, rows, P(("dp", "expert"), None), P())
        + attention_in
        + dense
        + attention_in
        + (P(), P(), P("expert", None, "mp"), P("expert", "mp", None)),
        out_specs=(rows, rows)
        + attention_in
        + dense
        + attention_in
        + (P(), P(), P("expert", None, "mp"), P("expert", "mp", None)),
        check_vma=False,
    )
```

```python
import functools

import jax
import jax.numpy as jnp
from jax import lax
from jax.experimental import pallas as pl
from jax.experimental.pallas import tpu as pltpu
from jax.sharding import PartitionSpec as P

EPSILON = 1e-06
BF16 = jnp.bfloat16
F32 = jnp.float32


def smooth_both(values):
    square = values * values
    tangent = jnp.tanh(0.7978845608 * values * (1.0 + 0.044715 * square))
    rest = 0.5 * (1.0 + tangent)
    slope = rest + (0.5 * 0.7978845608) * values * (1.0 - tangent * tangent) * (
        1.0 + 0.134145 * square
    )
    return values * rest, slope


def row_scale(rows):
    return lax.rsqrt(jnp.mean(rows * rows, axis=-1, keepdims=True) + EPSILON)


def normalize(rows, gain):
    return rows * row_scale(rows) * gain


def dot_nn(a, b):
    return jnp.dot(a, b, preferred_element_type=F32)


def dot_tn(a, b):
    return lax.dot_general(a, b, (((0,), (0,)), ((), ())), preferred_element_type=F32)


def dot_nt(a, b):
    return lax.dot_general(a, b, (((1,), (1,)), ((), ())), preferred_element_type=F32)


def flip(x, axis, bit):
    count = lax.axis_size(axis)
    return lax.ppermute(x, axis, [(i, i ^ (1 << bit)) for i in range(count)])


def meet(*values):
    leaves, tree = jax.tree.flatten(values)
    return jax.tree.unflatten(tree, lax.optimization_barrier(leaves))


def tie(value, *others):
    return meet(value, *others)[0]


def shift(x, axis, step):
    count = lax.axis_size(axis)
    return lax.ppermute(x, axis, [(i, (i + step) % count) for i in range(count)])


COST = pl.CostEstimate(flops=1, transcendentals=0, bytes_accessed=1)


def kernel_call(body, outs, scalars, arrays, limit=16):
    vmem = pl.BlockSpec(memory_space=pltpu.VMEM)
    return pl.pallas_call(
        body,
        out_shape=[jax.ShapeDtypeStruct(shape, dtype) for shape, dtype in outs],
        in_specs=[pl.BlockSpec(memory_space=pltpu.SMEM)] + [vmem] * len(arrays),
        out_specs=[vmem] * len(outs),
        compiler_params=pltpu.CompilerParams(vmem_limit_bytes=limit << 20),
        cost_estimate=COST,
    )(scalars, *arrays)


def place_scalars():
    return jnp.stack([lax.axis_index("expert"), lax.axis_index("dp") & 3]).astype(jnp.int32)


def plane_first(held):
    return flip(held, "dp", 0), flip(held, "dp", 1)


def plane_second(from_x, from_y):
    return flip(from_x[0], "dp", 1), flip(from_y[1], "dp", 0)


def quarter_of(left, right):
    rows = left.shape[0] // 4
    place = (lax.axis_index("dp") & 3) * rows
    return jnp.stack([lax.dynamic_slice_in_dim(t, place, rows, 0) for t in (left, right)])


def z_parts(piece):
    return [shift(piece, "expert", step) for step in range(1, lax.axis_size("expert"))]


def z_spread(piece):
    return jnp.stack(z_parts(piece), axis=1)


def assemble(left, right, pieces):
    count = lax.axis_size("expert")
    rows, cols = left.shape
    quarter = rows // 4

    def body(where, left_ref, right_ref, own, from_x, from_y, diag_left, diag_right, *outs):
        z, place = where[0], where[1]
        for side, (shard, diag) in enumerate(((left_ref, diag_left), (right_ref, diag_right))):
            outs[side][pl.ds(pl.multiple_of(z * rows, 16), rows), :] = shard[...]
            for step in range(1, count):
                base = lax.rem(z + count - step, count) * rows
                for key, ref in ((0, own), (1, from_x), (2, from_y), (3, diag)):
                    row = pl.multiple_of(base + (place ^ key) * quarter, 16)
                    outs[side][pl.ds(row, quarter), :] = (
                        ref[step - 1] if key == 3 else ref[side, step - 1]
                    )

    full = ((count * rows, cols), left.dtype)
    return kernel_call(body, [full, full], place_scalars(), (left, right) + tuple(pieces))


def add_low(a, b):
    return (a.astype(F32) + b.astype(F32)).astype(BF16)


def first_trip(send_a, send_b):
    return flip(send_a, "dp", 0), flip(send_b, "dp", 1)


def second_trip(send_a, send_b):
    return flip(send_a, "dp", 1), flip(send_b, "dp", 0)


def reduce_second(keep_a, keep_b, got_a, got_b):
    blocks = keep_a.shape[0]

    def body(where, keep_a, keep_b, got_a, got_b, send_a, send_b, next_a, next_b):
        x, y = where[1] & 1, where[1] >> 1
        for k in range(blocks):
            send_a[k] = add_low(keep_a[k, 1 - y], got_a[k, 1 - y])
            next_a[k] = add_low(keep_a[k, y], got_a[k, y])
            send_b[k] = add_low(keep_b[k, 1 - x], got_b[k, 1 - x])
            next_b[k] = add_low(keep_b[k, x], got_b[k, x])

    parts = [((blocks,) + keep.shape[2:], BF16) for keep in (keep_a, keep_b)]
    return kernel_call(body, parts * 2, place_scalars(), (keep_a, keep_b, got_a, got_b))


def far_sum(keep_a, keep_b, got_a, got_b):
    for bit in range(2, lax.axis_size("dp").bit_length() - 1):
        keep_a, keep_b = add_low(keep_a, got_a), add_low(keep_b, got_b)
        got_a, got_b = flip(keep_a, "dp", bit), flip(keep_b, "dp", bit)
    return keep_a, keep_b, got_a, got_b


def expert_held(*parts):
    def body(where, keep_a, keep_b, got_a, got_b, held_a, held_b):
        held_a[...] = add_low(keep_a[...], got_a[...])
        held_b[...] = add_low(keep_b[...], got_b[...])

    shapes = [(part.shape, BF16) for part in parts[:2]]
    return kernel_call(body, shapes, place_scalars(), far_sum(*parts))


def last_trip_e(held, got):
    both_a, both_b = (jnp.concatenate(pair, axis=0) for pair in zip(held, got))
    return flip(both_a, "dp", 0), flip(both_b, "dp", 1)


def expert_last(held, got, far):
    def body(where, *refs):
        place = where[1]
        for side in range(2):
            own, near, both = (refs[side + 2 * number] for number in range(3))
            rows, cols = own.shape[1:]
            first = 2 if side == 0 else 1
            for key, value in (
                (0, own[0]),
                (first, near[0]),
                (3 - first, both[0]),
                (3, both[1]),
            ):
                if side == 0:
                    at = pl.multiple_of((place ^ key) * cols, 128)
                    refs[6][:, pl.ds(at, cols)] = value.astype(F32)
                else:
                    at = pl.multiple_of((place ^ key) * rows, 16)
                    refs[7][pl.ds(at, rows), :] = value.astype(F32)

    (_, model, quarter), _ = (part.shape for part in held)
    shapes = [((model, 4 * quarter), F32), ((4 * quarter, model), F32)]
    return kernel_call(body, shapes, place_scalars(), (*held, *got, *far))


def reduce_third(*parts):
    blocks, rows, cols = parts[0].shape

    def body(where, keep_a, keep_b, got_a, got_b, *outs):
        for step, out in enumerate(outs):
            block = lax.rem(where[0] + step, blocks)
            out[0] = add_low(keep_a[block], got_a[block])
            out[1] = add_low(keep_b[block], got_b[block])

    own, *sends = kernel_call(
        body, [((2, rows, cols), BF16)] * blocks, place_scalars(), far_sum(*parts)
    )
    return own, sends


def reduce_halves(*parts):
    blocks, rows, cols = parts[0].shape
    half = blocks // 2

    def body(where, keep_a, keep_b, got_a, got_b, send, keep):
        upper = where[0] // half
        for k in range(half):
            for out, base in ((send, (1 - upper) * half), (keep, upper * half)):
                out[k, 0] = add_low(keep_a[base + k], got_a[base + k])
                out[k, 1] = add_low(keep_b[base + k], got_b[base + k])

    return kernel_call(
        body, [((half, 2, rows, cols), BF16)] * 2, place_scalars(), far_sum(*parts)
    )


def reduce_last_half(keep, got):
    half = keep.shape[0]

    def body(where, keep, got, send, own):
        odd = lax.rem(where[0], half)
        send[...] = add_low(keep[1 - odd], got[1 - odd])
        own[...] = add_low(keep[odd], got[odd])

    return kernel_call(
        body, [(keep.shape[1:], BF16)] * 2, place_scalars(), (keep, got)
    )


def z_trip(sends):
    return [shift(send, "expert", step + 1) for step, send in enumerate(sends)]


def reduce_fourth(own, got):
    total = own.astype(F32)
    for part in got:
        total = total + part.astype(F32)
    return total.astype(BF16)


def reduce_last(held, near, diagonal, widths):
    _, rows, _ = held.shape

    def body(where, own, from_x, from_y, diag_a, diag_b, *outs):
        place = where[1]
        start = 0
        for number, width in enumerate(widths):
            cols = slice(start, start + width)
            for side, diag in enumerate((diag_a, diag_b)):
                out = outs[2 * number + side]
                for key, ref in ((0, own), (1, from_x), (2, from_y), (3, diag)):
                    row = pl.multiple_of((place ^ key) * rows, 8)
                    value = ref[:, cols] if key == 3 else ref[side, :, cols]
                    out[pl.ds(row, rows), :] = value.astype(F32)
            start += width

    shapes = [((4 * rows, width), F32) for width in widths for _ in range(2)]
    outs = kernel_call(body, shapes, place_scalars(), (held, *near, *diagonal))
    return [outs[2 * i : 2 * i + 2] for i in range(len(widths))]


def pack_small(gains, router, tables):
    model = gains[0].shape[1]
    heads, levels = tables[0].shape
    top = len(gains) + router.shape[0]
    share = 1.0 / lax.axis_size("mp")

    def body(core, *refs):
        out = refs[-1]
        out[...] = jnp.zeros_like(out)
        for number in range(len(gains)):
            out[number : number + 1, :] = refs[number][...] * share
        out[len(gains) : top, :] = refs[len(gains)][...]
        for layer in range(2):
            for side in range(2):

                @pl.when(core[0] == side)
                def _():
                    at = (layer * 2 + side) * 128
                    out[top : top + heads, at : at + levels] = refs[len(gains) + 1 + layer][...]

    return kernel_call(
        body,
        [((16, model), F32)],
        jnp.stack([lax.axis_index("mp")]).astype(jnp.int32),
        (*gains, router, *tables),
    )[0]


def whole(shape):
    return pl.BlockSpec(memory_space=pltpu.VMEM)


PARAMS = pltpu.CompilerParams(vmem_limit_bytes=24 << 20)
MIDDLE = pltpu.CompilerParams(vmem_limit_bytes=20 << 20)
LARGE = pltpu.CompilerParams(vmem_limit_bytes=30 << 20)


def build_bias(buckets, tables, token):
    heads = tables.shape[0]
    seq_len = buckets.shape[0]
    padded = jnp.pad(tables, ((0, 0), (0, 128 - tables.shape[1])))

    def body(bucket_ref, table_ref, _, out_ref):
        head = pl.program_id(0)
        row = jnp.broadcast_to(table_ref[pl.ds(head, 1), :], (seq_len, 128))
        for part in range(seq_len // 128):
            index = bucket_ref[:, part * 128 : (part + 1) * 128]
            out_ref[0, :, part * 128 : (part + 1) * 128] = jnp.take_along_axis(row, index, axis=1)

    return pl.pallas_call(
        body,
        out_shape=jax.ShapeDtypeStruct((heads, seq_len, seq_len), F32),
        grid=(heads,),
        in_specs=[whole((seq_len, seq_len)), whole((heads, 128)), whole(token.shape)],
        out_specs=pl.BlockSpec((1, seq_len, seq_len), lambda h: (h, 0, 0)),
        compiler_params=PARAMS,
        cost_estimate=COST,
    )(buckets, padded, token)


def lane_masks(head_width):
    lane = lax.broadcasted_iota(jnp.int32, (1, 2 * head_width), 1)
    return [lane < head_width, lane >= head_width]


def masked(value, mask):
    return jnp.where(mask, value, jnp.zeros_like(value))


def both(first, second):
    if len(first.shape) == 2:
        return first[...].astype(F32) + second[...].astype(F32)
    return jnp.concatenate(
        [part[0].astype(F32) + part[1].astype(F32) for part in (first, second)], axis=0
    )


def stream_sum(base, partials):
    total = base[...].astype(F32)
    if partials:
        total = total + both(*partials)
    return total


def attention_forward(base, partials, gain, weights, bias):
    seq_len, model = base.shape
    heads = bias.shape[0]
    width = weights[0].shape[1] // 2
    head_width = width // heads
    chunk = 256
    scale = head_width**-0.5
    count = len(partials)

    def body(*refs):
        base_ref, part_refs = refs[0], refs[1 : 1 + count]
        gain_ref, wa_ref, wb_ref, bias_ref = refs[1 + count : 5 + count]
        stream_out, normed_out, joint_out, prob_ref, mixed_ref, partial_ref = refs[5 + count : -3]
        stream_ref, normed_ref, joint_ref = refs[-3:]
        step = pl.program_id(0)

        @pl.when(step == 0)
        def _():
            rows = stream_sum(base_ref, part_refs)
            stream_ref[...] = rows
            normed = normalize(rows, gain_ref[...]).astype(BF16)
            normed_ref[...] = normed
            left = dot_nn(normed, wa_ref[...]).astype(BF16)
            joint_ref[:, :width] = left[:, :width] * jnp.asarray(scale, BF16)
            joint_ref[:, width : 2 * width] = left[:, width:]
            joint_ref[:, 2 * width :] = dot_nn(normed, wb_ref[:, :width]).astype(BF16)

        masks = lane_masks(head_width)
        rows = pl.ds(pl.multiple_of(step * chunk, chunk), chunk)
        stream_out[...] = stream_ref[rows, :]
        normed_out[...] = normed_ref[rows, :]
        joint_out[...] = joint_ref[rows, :]
        for pair in range(heads // 2):
            cols = slice(pair * 2 * head_width, (pair + 1) * 2 * head_width)
            query = joint_ref[rows, cols]
            key = joint_ref[:, slice(width + cols.start, width + cols.stop)]
            value = joint_ref[:, slice(2 * width + cols.start, 2 * width + cols.stop)]
            mixed = None
            for side in range(2):
                head = 2 * pair + side
                scores = dot_nt(query, masked(key, masks[side])) + bias_ref[head]
                exp_part = jnp.exp(scores - jnp.max(scores, axis=-1, keepdims=True))
                share = 1.0 / jnp.sum(exp_part, axis=-1, keepdims=True)
                prob = (exp_part * share).astype(BF16)
                prob_ref[head] = prob
                out = dot_nn(prob, masked(value, masks[side]))
                mixed = out if mixed is None else mixed + out
            mixed_ref[:, cols] = mixed.astype(BF16)
        partial_ref[...] = dot_nt(mixed_ref[...], wb_ref[:, width:]).astype(BF16)

    full = (seq_len, model)
    def by_rows(cols):
        return pl.BlockSpec((chunk, cols), lambda i: (i, 0))

    heads_of = pl.BlockSpec((heads, chunk, seq_len), lambda i: (0, i, 0))
    kept = [
        (full, F32, by_rows(model)),
        (full, BF16, by_rows(model)),
        ((seq_len, 3 * width), BF16, by_rows(3 * width)),
        ((heads, seq_len, seq_len), BF16, heads_of),
        ((seq_len, width), BF16, by_rows(width)),
    ]
    return pl.pallas_call(
        body,
        out_shape=[pltpu.HBM(shape, dtype) for shape, dtype, _ in kept]
        + [jax.ShapeDtypeStruct(full, BF16)],
        grid=(seq_len // chunk,),
        in_specs=[whole(full)]
        + [whole(full)] * count
        + [whole((1, model)), whole(weights[0].shape), whole(weights[1].shape)]
        + [heads_of],
        out_specs=[spec for _, _, spec in kept] + [by_rows(model)],
        scratch_shapes=[
            pltpu.VMEM(full, F32),
            pltpu.VMEM(full, BF16),
            pltpu.VMEM((seq_len, 3 * width), BF16),
        ],
        compiler_params=PARAMS,
        cost_estimate=COST,
    )(base, *partials, gain[None], *weights, bias)


def attention_backward(grad, weights, joint, prob):
    seq_len, model = grad.shape
    heads = prob.shape[0]
    width = weights[0].shape[1] // 2
    head_width = width // heads
    chunk = 256
    steps = seq_len // chunk
    scale = head_width**-0.5

    def body(grad_ref, wa_ref, wb_ref, joint_ref, prob_ref, dj_ref, ds_ref, partial_ref, dk_acc, dv_acc):
        step = pl.program_id(0)

        @pl.when(step == 0)
        def _():
            dk_acc[...] = jnp.zeros_like(dk_acc)
            dv_acc[...] = jnp.zeros_like(dv_acc)

        masks = lane_masks(head_width)
        rows = pl.ds(pl.multiple_of(step * chunk, chunk), chunk)
        grad_mixed = dot_nn(grad_ref[...], wb_ref[:, width:]).astype(BF16)
        for pair in range(heads // 2):
            cols = slice(pair * 2 * head_width, (pair + 1) * 2 * head_width)
            query = joint_ref[rows, cols]
            key = joint_ref[:, slice(width + cols.start, width + cols.stop)]
            value = joint_ref[:, slice(2 * width + cols.start, 2 * width + cols.stop)]
            go = grad_mixed[:, cols]
            dq = None
            dk = None
            dv = None
            for side in range(2):
                head = 2 * pair + side
                low = prob_ref[head]
                wide = low.astype(F32)
                grad_prob = dot_nt(go, masked(value, masks[side]))
                inner = jnp.sum(wide * grad_prob, axis=-1, keepdims=True)
                ds = (wide * (grad_prob - inner)).astype(BF16)
                ds_ref[head] = ds
                one_q = dot_nn(ds, masked(key, masks[side]))
                one_k = dot_tn(ds, masked(query, masks[side]))
                one_v = dot_tn(low, masked(go, masks[side]))
                dq = one_q if dq is None else dq + one_q
                dk = one_k if dk is None else dk + one_k
                dv = one_v if dv is None else dv + one_v
            dj_ref[rows, cols] = (dq * scale).astype(BF16)
            dk_acc[:, cols] += dk
            dv_acc[:, cols] += dv

        @pl.when(step == steps - 1)
        def _():
            dj_ref[:, width : 2 * width] = dk_acc[...].astype(BF16)
            dj_ref[:, 2 * width :] = dv_acc[...].astype(BF16)
            partial_ref[...] = (
                dot_nt(dj_ref[:, : 2 * width], wa_ref[...])
                + dot_nt(dj_ref[:, 2 * width :], wb_ref[:, :width])
            ).astype(BF16)

    full = (seq_len, model)
    rows_of = pl.BlockSpec((heads, chunk, seq_len), lambda i: (0, i, 0))
    return pl.pallas_call(
        body,
        out_shape=[
            jax.ShapeDtypeStruct((seq_len, 3 * width), BF16),
            pltpu.HBM(prob.shape, BF16),
            jax.ShapeDtypeStruct(full, BF16),
        ],
        grid=(steps,),
        in_specs=[
            pl.BlockSpec((chunk, model), lambda i: (i, 0)),
            whole(weights[0].shape),
            whole(weights[1].shape),
            whole(joint.shape),
            rows_of,
        ],
        out_specs=[whole((seq_len, 3 * width)), rows_of, whole(full)],
        scratch_shapes=[pltpu.VMEM((seq_len, width), F32)] * 2,
        compiler_params=PARAMS,
        cost_estimate=COST,
    )(grad, *weights, joint, prob)


def split_first(where, a, b, send_a, send_b, keep_a, keep_b, blocks):
    rows = send_a.shape[2]
    x, y = where[1] & 1, where[1] >> 1
    for k in range(blocks):
        for j in range(2):
            for i in range(2):
                at = (k * 4 + j * 2 + i) * rows
                piece_a, piece_b = a[at : at + rows], b[at : at + rows]

                @pl.when(x == i)
                def _():
                    keep_a[k, j] = piece_a

                @pl.when(x != i)
                def _():
                    send_a[k, j] = piece_a

                @pl.when(y == j)
                def _():
                    keep_b[k, i] = piece_b

                @pl.when(y != j)
                def _():
                    send_b[k, i] = piece_b


def weight_grads(blocks, lefts, rights):
    model = lefts[0][0].shape[1]
    cols = sum(stop - start for _, _, start, stop in lefts)
    rows = model // blocks // 4
    half = ((blocks, 2, rows, cols), BF16)
    flat = [t for pair in lefts + rights for t in pair[:2]]

    def body(where, *refs):
        inputs, outs = refs[: len(flat)], refs[len(flat) :]

        def side(number, pairs):
            return jnp.concatenate(
                [
                    dot_tn(
                        inputs[number + 2 * i][...], inputs[number + 2 * i + 1][:, start:stop]
                    ).astype(BF16)
                    for i, (_, _, start, stop) in enumerate(pairs)
                ],
                axis=1,
            )

        split_first(where, side(0, lefts), side(2 * len(lefts), rights), *outs, blocks)

    return kernel_call(body, [half] * 4, place_scalars(), flat)


def table_grad(ds, buckets, bucket_count):
    heads, seq_len, _ = ds.shape
    group = 8

    def body(ds_ref, bucket_ref, out_ref, acc):
        acc[...] = jnp.zeros_like(acc)

        def one(number, carry):
            rows = pl.ds(pl.multiple_of(number * group, group), group)
            index = bucket_ref[rows, :]
            hot = jnp.concatenate(
                [jnp.where(index == level, 1.0, 0.0) for level in range(bucket_count)], axis=0
            ).astype(BF16)
            right = jnp.concatenate(
                [ds_ref[head, rows, :].astype(F32) for head in range(heads)], axis=0
            ).astype(BF16)
            acc[...] += dot_nt(hot, right)
            return carry

        lax.fori_loop(0, seq_len // group, one, 0, unroll=4)
        shape = acc.shape
        same = (
            lax.broadcasted_iota(jnp.int32, shape, 0) % group
            == lax.broadcasted_iota(jnp.int32, shape, 1) % group
        )
        kept = jnp.where(same, acc[...], 0.0)
        spread = (
            lax.broadcasted_iota(jnp.int32, (bucket_count, shape[0]), 1) // group
            == lax.broadcasted_iota(jnp.int32, (bucket_count, shape[0]), 0)
        ).astype(F32)
        gather = (
            lax.broadcasted_iota(jnp.int32, (heads, shape[1]), 1) // group
            == lax.broadcasted_iota(jnp.int32, (heads, shape[1]), 0)
        ).astype(F32)
        exact = dict(preferred_element_type=F32, precision=lax.Precision.HIGHEST)
        by_level = jnp.dot(spread, kept, **exact)
        out_ref[...] = lax.dot_general(gather, by_level, (((1,), (1,)), ((), ())), **exact)

    vmem = pl.BlockSpec(memory_space=pltpu.VMEM)
    return pl.pallas_call(
        body,
        out_shape=jax.ShapeDtypeStruct((heads, bucket_count), F32),
        in_specs=[vmem, vmem],
        out_specs=vmem,
        scratch_shapes=[pltpu.VMEM((bucket_count * group, heads * group), F32)],
        compiler_params=PARAMS,
        cost_estimate=COST,
    )(ds, buckets)


def dense_forward(base, partials, gain, w_in, w_out):
    seq_len, model = base.shape
    hidden_width = w_in.shape[1]
    chunk = 512
    steps = hidden_width // chunk

    def body(base_ref, own_ref, got_ref, gain_ref, in_ref, out_ref, stream_ref, normed_ref, hidden_ref, slope_ref, partial_ref, acc):
        step = pl.program_id(0)

        @pl.when(step == 0)
        def _():
            rows = stream_sum(base_ref, (own_ref, got_ref))
            stream_ref[...] = rows
            normed_ref[...] = normalize(rows, gain_ref[...]).astype(BF16)
            acc[...] = jnp.zeros_like(acc)

        pre = dot_nn(normed_ref[...], in_ref[...])
        act, slope = smooth_both(pre)
        hidden = act.astype(BF16)
        hidden_ref[...] = hidden
        slope_ref[...] = slope.astype(BF16)
        acc[...] += dot_nt(hidden, out_ref[...])

        @pl.when(step == steps - 1)
        def _():
            partial_ref[...] = acc[...].astype(BF16)

    full = (seq_len, model)
    col = pl.BlockSpec((model, chunk), lambda i: (0, i))
    act = pl.BlockSpec((seq_len, chunk), lambda i: (0, i))
    return pl.pallas_call(
        body,
        out_shape=[
            jax.ShapeDtypeStruct(full, F32),
            jax.ShapeDtypeStruct(full, BF16),
            pltpu.HBM((seq_len, hidden_width), BF16),
            pltpu.HBM((seq_len, hidden_width), BF16),
            jax.ShapeDtypeStruct(full, BF16),
        ],
        grid=(steps,),
        in_specs=[whole(full)] * 3 + [whole((1, model)), col, col],
        out_specs=[whole(full), whole(full), act, act, whole(full)],
        scratch_shapes=[pltpu.VMEM(full, F32)],
        compiler_params=PARAMS,
        cost_estimate=COST,
    )(base, *partials, gain[None], w_in, w_out)


def norm_step(grad_ref, rows_ref, gain_ref, own_ref, got_ref):
    upstream = both(own_ref, got_ref)
    rows = rows_ref[...].astype(F32)
    scale = row_scale(rows)
    scaled = upstream * gain_ref[...]
    inner = jnp.mean(scaled * rows, axis=-1, keepdims=True)
    grad_rows = scale * scaled - rows * (scale * scale * scale * inner)
    grad_gain = jnp.sum(upstream * rows * scale, axis=0, keepdims=True)
    return grad_ref[...].astype(F32) + grad_rows, grad_gain


def norm_kernel(grad, rows, gain, partials):
    full = rows.shape

    def body(_, grad_ref, rows_ref, gain_ref, own_ref, got_ref, out_ref, low_ref, gain_out):
        total, gain_out[...] = norm_step(grad_ref, rows_ref, gain_ref, own_ref, got_ref)
        out_ref[...] = total
        low_ref[...] = total.astype(BF16)

    return kernel_call(
        body,
        [(full, F32), (full, BF16), ((1, full[1]), F32)],
        place_scalars(),
        (grad, rows, gain[None], *partials),
    )


def dense_backward(grad, rows, gain, partials, w_in, w_out, slope):
    seq_len, model = rows.shape
    hidden_width = w_in.shape[1]
    chunk = 512
    steps = hidden_width // chunk

    def body(grad_ref, rows_ref, gain_ref, own_ref, got_ref, in_ref, out_ref, slope_ref, total_ref, low_ref, dpre_ref, partial_ref, gain_out, acc):
        step = pl.program_id(0)

        @pl.when(step == 0)
        def _():
            total, gain_out[...] = norm_step(grad_ref, rows_ref, gain_ref, own_ref, got_ref)
            total_ref[...] = total
            low_ref[...] = total.astype(BF16)
            acc[...] = jnp.zeros_like(acc)

        dpre = (dot_nn(low_ref[...], out_ref[...]) * slope_ref[...].astype(F32)).astype(BF16)
        dpre_ref[...] = dpre
        acc[...] += dot_nt(dpre, in_ref[...])

        @pl.when(step == steps - 1)
        def _():
            partial_ref[...] = acc[...].astype(BF16)

    full = (seq_len, model)
    col = pl.BlockSpec((model, chunk), lambda i: (0, i))
    act = pl.BlockSpec((seq_len, chunk), lambda i: (0, i))
    return pl.pallas_call(
        body,
        out_shape=[
            jax.ShapeDtypeStruct(full, F32),
            jax.ShapeDtypeStruct(full, BF16),
            jax.ShapeDtypeStruct((seq_len, hidden_width), BF16),
            jax.ShapeDtypeStruct(full, BF16),
            jax.ShapeDtypeStruct((1, model), F32),
        ],
        grid=(steps,),
        in_specs=[whole(full)] * 2 + [whole((1, model))] + [whole(full)] * 2 + [col, col, act],
        out_specs=[whole(full), whole(full), act, whole(full), whole((1, model))],
        scratch_shapes=[pltpu.VMEM(full, F32)],
        compiler_params=PARAMS,
        cost_estimate=COST,
    )(grad, rows, gain[None], *partials, w_in, w_out, slope)


def send_slots(base, partials, gain, spots, blocks):
    seq_len, model = base.shape
    slots = spots[1] // blocks
    full = (seq_len, model)

    def body(_, base_ref, own_ref, got_ref, gain_ref, spot_ref, stream_ref, normed_ref, *outs):
        rows = stream_sum(base_ref, (own_ref, got_ref))
        stream_ref[...] = rows
        normed = normalize(rows, gain_ref[...]).astype(BF16)
        normed_ref[...] = normed
        for block in range(blocks):
            slot = lax.broadcasted_iota(jnp.int32, (slots, seq_len), 0) + block * slots
            hot = jnp.where(slot == spot_ref[...], 1.0, 0.0).astype(BF16)
            outs[block][...] = dot_nn(hot, normed).astype(BF16)

    return kernel_call(
        body,
        [(full, F32), (full, BF16)] + [((slots, model), BF16)] * blocks,
        place_scalars(),
        (base, *partials, gain[None], spots[0]),
    )


def stacked(blocks):
    rows, cols = blocks[0].shape

    def body(_, *refs):
        for number, ref in enumerate(refs[:-1]):
            refs[-1][number * rows : (number + 1) * rows, :] = ref[...]

    return kernel_call(body, [((len(blocks) * rows, cols), blocks[0].dtype)], place_scalars(), blocks)[0]


def route_softmax(rows, router):
    logits = dot_nt(rows, router)
    exp_part = jnp.exp(logits - jnp.max(logits, axis=-1, keepdims=True))
    return exp_part / jnp.sum(exp_part, axis=-1, keepdims=True)


def expert_step(rows, grads, router, w_in, w_out):
    half, model = rows[0].shape
    hidden_width = w_in.shape[1]
    chunk = 512
    steps = hidden_width // chunk
    total = 2 * half

    def body(where, own_ref, other_ref, own_grad, other_grad, router_ref, in_ref, out_ref, hidden_ref, dpre_ref, grad_ref, res_own, res_other, back_own, back_other, res_acc, back_acc, rows_ref):
        step = pl.program_id(0)

        @pl.when(step == 0)
        def _():
            rows_ref[:half, :] = own_ref[...]
            rows_ref[half:, :] = other_ref[...]
            here = lax.broadcasted_iota(jnp.int32, (1, router_ref.shape[0]), 1) == where[0]
            for side, grad in enumerate((own_grad, other_grad)):
                part = slice(side * half, (side + 1) * half)
                prob = route_softmax(rows_ref[part, :], router_ref[...])
                gate = jnp.sum(jnp.where(here, prob, 0.0), axis=-1, keepdims=True)
                grad_ref[part, :] = (gate * grad[...].astype(F32)).astype(BF16)
            res_acc[...] = jnp.zeros_like(res_acc)
            back_acc[...] = jnp.zeros_like(back_acc)

        pre = dot_nn(rows_ref[...], in_ref[...])
        act, slope = smooth_both(pre)
        hidden = act.astype(BF16)
        hidden_ref[...] = hidden
        dpre = (dot_nt(grad_ref[...], out_ref[...]) * slope).astype(BF16)
        dpre_ref[...] = dpre
        res_acc[...] += dot_nn(hidden, out_ref[...])
        back_acc[...] += dot_nt(dpre, in_ref[...])

        @pl.when(step == steps - 1)
        def _():
            res_own[...] = res_acc[:half, :]
            res_other[...] = res_acc[half:, :].astype(BF16)
            back_own[...] = back_acc[:half, :]
            back_other[...] = back_acc[half:, :].astype(BF16)

    part = (half, model)
    act = pl.BlockSpec((total, chunk), lambda i: (0, i))
    return pl.pallas_call(
        body,
        out_shape=[
            pltpu.HBM((total, hidden_width), BF16),
            pltpu.HBM((total, hidden_width), BF16),
            jax.ShapeDtypeStruct((total, model), BF16),
            jax.ShapeDtypeStruct(part, F32),
            jax.ShapeDtypeStruct(part, BF16),
            jax.ShapeDtypeStruct(part, F32),
            jax.ShapeDtypeStruct(part, BF16),
        ],
        grid=(steps,),
        in_specs=[pl.BlockSpec(memory_space=pltpu.SMEM)]
        + [whole(part)] * 4
        + [
            whole(router.shape),
            pl.BlockSpec((model, chunk), lambda i: (0, i)),
            pl.BlockSpec((chunk, model), lambda i: (i, 0)),
        ],
        out_specs=[act, act, whole((total, model))] + [whole(part)] * 4,
        scratch_shapes=[pltpu.VMEM((total, model), F32)] * 2 + [pltpu.VMEM((total, model), BF16)],
        compiler_params=LARGE,
        cost_estimate=COST,
    )(place_scalars(), *rows, *grads, router, w_in, w_out)


def expert_finish(result, back, rows, grads, router, blocks):
    half, model = rows.shape
    slots = half // blocks

    def body(where, res_own, res_got, back_own, back_got, rows_ref, grad_ref, router_ref, *outs):
        here = lax.broadcasted_iota(jnp.int32, (1, router_ref.shape[0]), 1) == where[0]
        prob = route_softmax(rows_ref[...], router_ref[...])
        gate = jnp.sum(jnp.where(here, prob, 0.0), axis=-1, keepdims=True)
        result = res_own[...] + res_got[...].astype(F32)
        grad_gate = jnp.sum(grad_ref[...].astype(F32) * result, axis=-1, keepdims=True)
        dz = (prob * (jnp.where(here, grad_gate, 0.0) - grad_gate * gate)).astype(BF16)
        total = back_own[...] + back_got[...].astype(F32) + dot_nn(dz, router_ref[...])
        for block in range(blocks):
            part = slice(block * slots, (block + 1) * slots)
            outs[block][...] = total[part, :].astype(BF16)
            outs[blocks + block][...] = result[part, :].astype(BF16)
        outs[-1][...] = dot_tn(dz, rows_ref[...])

    return kernel_call(
        body,
        [((slots, model), BF16)] * (2 * blocks) + [(router.shape, F32)],
        place_scalars(),
        (*result, *back, rows, grads, router),
    )


def expert_grads(kept, rows, hidden, dpre, grads):
    half, model = rows[0].shape
    hidden_width = hidden.shape[1]
    quarter = hidden_width // 4

    def spot_a(step, where):
        x = where[1] & 1
        return step * 2 + (x if kept else 1 - x)

    def spot_b(step, where):
        y = where[1] >> 1
        return (y if kept else 1 - y) * 2 + step

    def body(where, own_ref, other_ref, hidden_ref, dpre_ref, grad_ref, out_a, out_b, rows_ref):
        @pl.when(pl.program_id(0) == 0)
        def _():
            rows_ref[:half, :] = own_ref[...]
            rows_ref[half:, :] = other_ref[...]

        out_a[0] = dot_tn(rows_ref[...], dpre_ref[...]).astype(BF16)
        out_b[0] = dot_tn(hidden_ref[...], grad_ref[...]).astype(BF16)

    shape_a, shape_b = (model, quarter), (quarter, model)
    return pl.pallas_call(
        body,
        out_shape=[jax.ShapeDtypeStruct((2,) + shape, BF16) for shape in (shape_a, shape_b)],
        grid_spec=pltpu.PrefetchScalarGridSpec(
            num_scalar_prefetch=1,
            grid=(2,),
            in_specs=[
                whole(None),
                whole(None),
                pl.BlockSpec((2 * half, quarter), lambda i, w: (0, spot_b(i, w))),
                pl.BlockSpec((2 * half, quarter), lambda i, w: (0, spot_a(i, w))),
                whole(None),
            ],
            out_specs=[
                pl.BlockSpec((1,) + shape_a, lambda i, w: (i, 0, 0)),
                pl.BlockSpec((1,) + shape_b, lambda i, w: (i, 0, 0)),
            ],
            scratch_shapes=[pltpu.VMEM((2 * half, model), BF16)],
        ),
        compiler_params=MIDDLE,
        cost_estimate=COST,
    )(
        place_scalars(),
        *rows,
        pltpu.with_memory_space_constraint(hidden, pltpu.HBM),
        pltpu.with_memory_space_constraint(dpre, pltpu.HBM),
        grads,
    )


def receive_slots(grad, rows, gain, spots, halves):
    full = rows.shape
    half = halves[0].shape[0]

    def body(_, grad_ref, rows_ref, gain_ref, spot_ref, own_ref, got_ref, out_ref, low_ref, gain_out):
        slot = lax.broadcasted_iota(jnp.int32, (full[0], half), 1)
        first = jnp.where(slot == spot_ref[...], 1.0, 0.0).astype(BF16)
        second = jnp.where(slot + half == spot_ref[...], 1.0, 0.0).astype(BF16)
        upstream = dot_nn(first, own_ref[...]) + dot_nn(second, got_ref[...])
        value = rows_ref[...]
        scale = row_scale(value)
        scaled = upstream * gain_ref[...]
        inner = jnp.mean(scaled * value, axis=-1, keepdims=True)
        total = grad_ref[...].astype(F32) + (
            scale * scaled - value * (scale * scale * scale * inner)
        )
        gain_out[...] = jnp.sum(upstream * value * scale, axis=0, keepdims=True)
        out_ref[...] = total
        low_ref[...] = total.astype(BF16)

    return kernel_call(
        body,
        [(full, F32), (full, BF16), ((1, full[1]), F32)],
        place_scalars(),
        (grad, rows, gain[None], spots) + tuple(halves),
    )


def on_device(
    tokens,
    cotangent,
    routes,
    buckets,
    norm_first,
    query_first,
    key_first,
    value_first,
    output_first,
    table_first,
    dense_gain,
    dense_in,
    dense_out,
    norm_second,
    query_second,
    key_second,
    value_second,
    output_second,
    table_second,
    expert_gain,
    router,
    expert_in,
    expert_out,
):
    mp_index = lax.axis_index("mp")
    z_index = lax.axis_index("expert")
    z_count = lax.axis_size("expert")
    tok_local, model_width = tokens.shape
    seq_len = buckets.shape[0]
    expert_count = router.shape[1]
    capacity = seq_len // 2
    slots = capacity // lax.axis_size("mp")
    bucket_count = table_first.shape[0]
    head_local = table_first.shape[1] // lax.axis_size("mp")

    width = query_first.shape[1]
    ff_width = dense_in.shape[1]
    shards = (
        (
            jnp.concatenate([query_first, key_first], axis=1),
            jnp.concatenate([value_first, output_first.T], axis=1),
        ),
        (dense_in, dense_out.T),
        (
            jnp.concatenate([query_second, key_second], axis=1),
            jnp.concatenate([value_second, output_second.T], axis=1),
        ),
    )
    far_one = z_spread(quarter_of(*shards[0]))

    def local_bias(table, token):
        return build_bias(
            buckets, lax.dynamic_slice_in_dim(table, mp_index * head_local, head_local, 1).T, token
        )

    chosen = routes[:, 0]
    experts = jnp.arange(expert_count, dtype=jnp.int32)
    picked = chosen[:, None] == experts[None, :]
    order = jnp.arange(seq_len, dtype=jnp.int32)
    earlier = (order[None, :] < order[:, None]).astype(BF16)
    rank = jnp.sum(
        jnp.where(picked, dot_nn(earlier, picked.astype(BF16)), 0.0), axis=1
    ).astype(jnp.int32)
    distance = (chosen - z_index + z_count) % z_count
    spot = distance * slots + rank % slots
    half = z_count * slots
    in_own_half = rank // slots == mp_index
    send_spots = jnp.where(in_own_half, spot, -1)[None, :]
    back_spots = jnp.where(in_own_half, spot, spot + half)[:, None]

    def sent_on(blocks):
        return [blocks[0]] + [shift(blocks[step], "expert", step) for step in range(1, z_count)]

    def with_other(own):
        return own, flip(own, "mp", 0)

    def sent_back(blocks):
        return [blocks[0]] + [
            shift(blocks[step], "expert", z_count - step) for step in range(1, z_count)
        ]

    def swapped(partial):
        return partial, flip(partial, "mp", 0)

    def gathered(partial):
        rows = partial.shape[0] // 2
        return tuple(
            lax.all_gather(part, "mp", axis=0) for part in (partial[:rows], partial[rows:])
        )

    piece_ff, far_one = meet(quarter_of(*shards[1]), far_one)
    near_one = plane_first(far_one)
    got_ff = z_parts(piece_ff)
    bias_one = local_bias(table_first, far_one[0, 0, :8, :128])
    tokens, cotangent, near_one, bias_one = meet(tokens, cotangent, near_one, bias_one)
    diag_one = plane_second(*near_one)
    stream_zero = lax.all_gather(tokens, "mp", axis=0, tiled=True)
    grad_four = lax.all_gather(cotangent, "mp", axis=0, tiled=True)
    bias_two = local_bias(table_second, near_one[0][0, 0, :8, :128])
    diag_one, got_ff, bias_two, stream_zero, grad_four, send_spots, back_spots = meet(
        diag_one, got_ff, bias_two, stream_zero, grad_four, send_spots, back_spots
    )
    piece_two, far_ff = meet(quarter_of(*shards[2]), jnp.stack(got_ff, axis=1))
    near_ff = plane_first(far_ff)
    got_two = z_parts(piece_two)
    weights_one = assemble(*shards[0], (far_one, *near_one, *diag_one))
    _, normed_one, joint_one, prob_one, mixed_one, partial = attention_forward(
        tie(stream_zero, far_ff), (), norm_first, weights_one, bias_one
    )
    partial, near_ff, got_two = meet(partial, near_ff, got_two)
    diag_ff = plane_second(*near_ff)
    far_two = jnp.stack(got_two, axis=1)
    diag_ff, pair, far_two = meet(diag_ff, swapped(partial), far_two)
    near_two = plane_first(far_two)
    to_slots = (jnp.arange(half, dtype=jnp.int32)[:, None] == send_spots).astype(BF16)
    grad_sent = dot_nn(to_slots, tie(grad_four, pair)).astype(BF16)
    grad_got = sent_on([grad_sent[i * slots : (i + 1) * slots] for i in range(z_count)])
    w_in_full, w_out_full = assemble(*shards[1], (far_ff, *near_ff, *diag_ff))
    stream_one, normed_ff, hidden, slope, partial = dense_forward(
        stream_zero, pair, dense_gain, w_in_full, tie(w_out_full, grad_sent)
    )
    near_two, partial = meet(near_two, partial)
    diag_two = plane_second(*near_two)
    diag_two, pair = meet(diag_two, swapped(partial))
    weights_two = assemble(*shards[2], (far_two, *near_two, *diag_two))
    stream_two, normed_two, joint_two, prob_two, mixed_two, partial = attention_forward(
        stream_one, pair, norm_second, weights_two, bias_two
    )

    partial, grad_got = meet(partial, grad_got)

    grad_slots, pair = meet(with_other(stacked(grad_got)), swapped(partial))
    stream_three, moe_rows, *sent = send_slots(
        stream_two, pair, expert_gain, (send_spots, half), z_count
    )
    moe_slots = with_other(stacked(sent_on(sent)))
    router_rows = router.T
    expert_hidden, expert_dpre, expert_rows, res_own, res_other, back_own, back_other = expert_step(
        moe_slots, grad_slots, router_rows, expert_in[0], expert_out[0]
    )
    inputs_e = (moe_slots, expert_hidden, expert_dpre, expert_rows)
    send_e = expert_grads(False, *inputs_e)
    send_e, inputs_e, res_got, back_got = meet(
        send_e, inputs_e, flip(res_other, "mp", 0), flip(back_other, "mp", 0)
    )
    got_e = first_trip(*send_e)
    keep_e = expert_grads(True, *inputs_e)
    res_got, back_got, keep_e = meet(res_got, back_got, keep_e)
    keep_e = [part[None] for part in keep_e]
    *returns, grad_router = expert_finish(
        (res_own, res_got),
        (back_own, back_got),
        moe_slots[0],
        grad_slots[0],
        router_rows,
        z_count,
    )
    back_got, got_e = meet(sent_back(returns[:z_count]), got_e)
    send_ea, send_eb, *keep_e = reduce_second(*keep_e, got_e[0][None], got_e[1][None])
    send_ea, send_eb, back_got = meet(send_ea, send_eb, back_got)
    got_e = second_trip(send_ea, send_eb)
    grad_three, grad_low, grad_expert_gain = receive_slots(
        grad_four, stream_three, expert_gain, back_spots, with_other(stacked(back_got))
    )

    def attention_grads(kernel, normed, dj, low, mixed):
        return kernel(
            z_count,
            [(normed, dj, 0, 2 * width)],
            [(normed, dj, 2 * width, 3 * width), (low, mixed, 0, width)],
        )

    dj_two, ds_two, partial = attention_backward(grad_low, weights_two, joint_two, prob_two)
    partial, dj_two, got_e = meet(partial, dj_two, got_e)
    held_e = expert_held(*keep_e, *got_e)
    held_e, dj_two, partial = meet(held_e, dj_two, partial)
    from_e = (flip(held_e[0], "dp", 1), flip(held_e[1], "dp", 0))
    halves_two = attention_grads(weight_grads, normed_two, dj_two, grad_low, mixed_two)
    halves_two, partial = meet(halves_two, partial)
    got_two = first_trip(*halves_two[:2])
    grad_two, grad_low, dpre, partial, grad_norm_second = dense_backward(
        grad_three, stream_two, norm_second, gathered(partial), w_in_full, w_out_full, slope
    )
    halves_ff = weight_grads(
        z_count, [(normed_ff, dpre, 0, ff_width)], [(grad_low, hidden, 0, ff_width)]
    )
    from_e, halves_ff, partial, got_two, *result_blocks = meet(
        from_e, halves_ff, partial, got_two, *returns[z_count:]
    )
    got_ff = first_trip(*halves_ff[:2])
    result_got = sent_back(result_blocks)
    *send_two, keep_a, keep_b = reduce_second(*halves_two[2:], *got_two)
    keep_two = (keep_a, keep_b)
    grad_one, grad_low, grad_dense_gain = norm_kernel(
        grad_two, stream_one, dense_gain, gathered(tie(partial, send_two))
    )
    dj_one, ds_one, partial = attention_backward(grad_low, weights_one, joint_one, prob_one)
    dj_one, partial, result_got, send_two, got_ff = meet(
        dj_one, partial, result_got, send_two, got_ff
    )
    *send_ff, keep_ff_a, keep_ff_b = reduce_second(*halves_ff[2:], *got_ff)
    keep_ff = (keep_ff_a, keep_ff_b)
    send_ff, dj_one = meet(send_ff, dj_one)
    got_ff = second_trip(*send_ff)
    got_two = second_trip(*send_two)
    result_own = stacked(result_got)
    halves_one = attention_grads(weight_grads, normed_one, dj_one, grad_low, mixed_one)
    halves_one, partial = meet(halves_one, partial)
    grad_zero, _, grad_norm_first = norm_kernel(
        grad_one, stream_zero, norm_first, gathered(partial)
    )
    grad_norm_first, halves_one, got_two, got_ff = meet(
        grad_norm_first, halves_one, got_two, got_ff
    )
    send_ff, keep_ff = reduce_halves(*keep_ff, *got_ff)
    send_ff, halves_one, ds_two, ds_one, held_e, from_e = meet(
        send_ff, halves_one, ds_two, ds_one, held_e, from_e
    )
    got_ff = flip(send_ff, "expert", 1)
    got_one = first_trip(*halves_one[:2])
    far_e = last_trip_e(held_e, from_e)
    send_two, keep_two = reduce_halves(*keep_two, *got_two)
    table_two_grad = table_grad(ds_two, buckets, bucket_count)
    ds_one, table_two_grad = meet(ds_one, table_two_grad)
    table_one_grad = table_grad(ds_one, buckets, bucket_count)
    table_one_grad, got_one, send_two = meet(table_one_grad, got_one, send_two)
    *send_one, keep_a, keep_b = reduce_second(*halves_one[2:], *got_one)
    got_one = second_trip(*send_one)
    small = pack_small(
        (grad_norm_first, grad_dense_gain, grad_norm_second, grad_expert_gain),
        grad_router,
        (table_one_grad, table_two_grad),
    )
    got_ff, small, send_two = meet(got_ff, small, send_two)
    send_ff, keep_ff = reduce_last_half(keep_ff, got_ff)
    got_ff = flip(send_ff, "expert", 0)
    got_two = flip(send_two, "expert", 1)
    send_ff, got_one = meet(send_ff, got_one)
    send_one, keep_one = reduce_halves(keep_a, keep_b, *got_one)
    send_one, got_ff, far_e, small = meet(send_one, got_ff, far_e, small)
    held_ff = add_low(keep_ff, got_ff)
    near_ff = plane_first(held_ff)
    got_one = flip(send_one, "expert", 1)
    got_small = flip(small, "mp", 0)
    expert_in_sum, expert_out_sum = expert_last(held_e, from_e, far_e)
    small, got_small, near_ff, got_two, expert_in_sum = meet(
        small, got_small, near_ff, got_two, expert_in_sum
    )
    small = small + got_small
    diag_ff = plane_second(*near_ff)
    send_two, keep_two = reduce_last_half(keep_two, got_two)
    got_two = flip(send_two, "expert", 0)
    send_two, got_one = meet(send_two, got_one)
    send_one, keep_one = reduce_last_half(keep_one, got_one)
    got_one = flip(send_one, "expert", 0)
    got_small = flip(small, "dp", 0)
    diag_ff, got_one, got_two, small, got_small = meet(
        diag_ff, got_one, got_two, small, got_small
    )
    small = small + got_small
    held = jnp.concatenate([add_low(keep_one, got_one), add_low(keep_two, got_two)], axis=-1)
    near = plane_first(held)
    got_small = flip(small, "expert", 0)
    ((ff_in, ff_out),) = reduce_last(held_ff, near_ff, diag_ff, (ff_width,))
    near, ff_in, small, got_small, result_own = meet(near, ff_in, small, got_small, result_own)
    small = small + got_small
    diagonal = plane_second(*near)
    small = small + flip(small, "expert", 1)
    for bit in range(1, lax.axis_size("dp").bit_length() - 1):
        small = small + flip(small, "dp", bit)
    one, two = reduce_last(held, near, diagonal, (2 * width, 2 * width))
    first_row = mp_index * tok_local
    grad_zero = lax.dynamic_slice_in_dim(grad_zero, first_row, tok_local, 0)

    result_got = flip(result_own, "mp", 0)
    spots_here = lax.dynamic_slice_in_dim(back_spots, first_row, tok_local, 0)
    lanes = jnp.arange(half, dtype=jnp.int32)[None, :]
    result_rows = dot_nn((lanes == spots_here).astype(BF16), result_own) + dot_nn(
        (lanes + half == spots_here).astype(BF16), result_got
    )
    own_rows = lax.dynamic_slice_in_dim(moe_rows, first_row, tok_local, 0)
    own_picked = lax.dynamic_slice_in_dim(picked, first_row, tok_local, 0)
    own_gate = jnp.sum(
        jnp.where(own_picked, route_softmax(own_rows, router_rows), 0.0), axis=-1, keepdims=True
    )
    final_rows = (
        lax.dynamic_slice_in_dim(stream_three, first_row, tok_local, 0) + own_gate * result_rows
    )

    router_sum = small[4 : 4 + expert_count].T
    base = 4 + expert_count
    table_one_sum, table_two_sum = (
        jnp.concatenate(
            [
                small[base : base + head_local, at * 128 : at * 128 + bucket_count]
                for at in (layer * 2, layer * 2 + 1)
            ],
            axis=0,
        ).T
        for layer in range(2)
    )

    return (
        final_rows,
        grad_zero,
        small[0],
        one[0][:, :width],
        one[0][:, width:],
        one[1][:, :width],
        one[1][:, width:].T,
        table_one_sum,
        small[1],
        ff_in,
        ff_out.T,
        small[2],
        two[0][:, :width],
        two[0][:, width:],
        two[1][:, :width],
        two[1][:, width:].T,
        table_two_sum,
        small[3],
        router_sum,
        expert_in_sum[None],
        expert_out_sum[None],
    )


def solution(mesh):
    rows = P(("dp", "expert", "mp"), None)
    cols_in, cols_out = P("expert", "mp"), P("mp", "expert")
    attention_in = (P(), cols_in, cols_in, cols_in, cols_out, P())
    dense = (P(), cols_in, cols_out)
    return jax.shard_map(
        on_device,
        mesh=mesh,
        in_specs=(rows, rows, P(("dp", "expert"), None), P())
        + attention_in
        + dense
        + attention_in
        + (P(), P(), P("expert", None, "mp"), P("expert", "mp", None)),
        out_specs=(rows, rows)
        + attention_in
        + dense
        + attention_in
        + (P(), P(), P("expert", None, "mp"), P("expert", "mp", None)),
        check_vma=False,
    )
```
